32 devices in a mesh: rows: 8 (over z, core), cols: 4 (over y, x).
Axes of the slice: x: 2, y: 2, z: 4, core: 2. Of those that a mesh axis runs over, the one named last changes fastest.
Arguments:
- wave_coarse: float32 [192, 192, 192], P('rows', 'cols'), may hold values from -6 to 6
- potential_coarse: float32 [192, 192, 192], P('rows', 'cols'), may hold values from 0 to 5
- potential_fine: float32 [384, 384, 384], P('cols', 'rows'), may hold values from 0 to 5
Outputs:
- fine_wave: float32 [384, 384, 384], P('cols', 'rows')
The draws below stay inside these ranges and needn't reach their ends.
All inputs are finite; a program needn't handle non-finite values.
Results may differ from the reference program's by a relative error of at most 0.0003.
Values sent between devices are 32-bit elements; how exact they have to be, the bound alone decides.
A program may use at most 128 MiB of HBM per device.

```python
import math
import jax
import jax.numpy as jnp
from jax import lax

NC = 192
NF = 384
COARSE_STEPS = 1
FINE_STEPS = 1


def incline_potential(key, length, steepness, rough_low, rough_high):
    positions = jnp.arange(length, dtype=jnp.float32) / length
    incline = steepness * (positions[:, None, None] + positions[None, :, None] + positions[None, None, :])
    roughness = jax.random.uniform(key, (length, length, length), jnp.float32, rough_low, rough_high)
    return incline + roughness


def draw_potential_coarse(key, part):
    return incline_potential(jax.random.fold_in(key, 11), NC, 1.1, 0.0, 1.5)


def draw_potential_fine(key, part):
    return incline_potential(jax.random.fold_in(key, 23), NF, 1.1, 0.0, 1.5)


def steps_of(rng, extent, shards, least, top_value):
    loudness = 1.0
    for position, blocks in shards:
        draws = jax.random.uniform(jax.random.fold_in(jax.random.fold_in(rng, 6), position), (blocks,), jnp.float32, least / len(shards), top_value / len(shards))
        loudness = loudness * jnp.repeat(jnp.exp(draws), extent[position] // blocks).reshape((-1,) + (1,) * (len(extent) - 1 - position))
    return loudness


def scatter_about(key, dims, scale, reach, shards=(), kind=jnp.bfloat16):
    gain = steps_of(key, dims, shards, -0.22, 0.18) if shards else 1.0
    drawn = jax.random.normal(key, dims, jnp.float32) * scale * gain
    return jnp.minimum(jnp.maximum(drawn, -reach), reach).astype(kind)


def setup_inputs(seed: int = 0) -> dict:
    seeds = jax.random.split(jax.random.key(seed), 4)
    return {
        "wave_coarse": scatter_about(seeds[0], (NC, NC, NC), 1.0, 6.0, ((0, 8), (1, 4)), jnp.float32),
        "potential_coarse": draw_potential_coarse(jax.random.fold_in(seeds[3], 71), 0),
        "potential_fine": draw_potential_fine(jax.random.fold_in(seeds[3], 71), 0),
    }


TIME_STEP = 0.5
CONTACT = 0.4
DIPOLE_STRENGTH = 0.3
EPSILON = 1e-06

def hartley(values, dimension):
    spectrum = jnp.fft.fft(values, axis=dimension)
    return (spectrum.real - spectrum.imag).astype(values.dtype)

def hartley_cube(values):
    for dimension in range(3):
        values = hartley(values, dimension)
    return values

def wavenumbers(length, spacing):
    positions = jnp.arange(length, dtype=jnp.int32)
    signed = jnp.where(positions < length // 2, positions, positions - length)
    return 2.0 * math.pi / (length * spacing) * signed.astype(jnp.float32)

def multipliers(along_x, along_y, along_z, length):
    squares = along_x + along_y + along_z
    volume = float(length) ** 3
    kinetic = jnp.exp(-0.5 * TIME_STEP * squares) / volume
    nonzero = jnp.where(squares > 0, squares, 1.0)
    dipolar = jnp.where(squares > 0, DIPOLE_STRENGTH * (3.0 * along_z - squares) / nonzero, 0.0) / volume
    return (kinetic, dipolar)

def advance(amplitude, potential, kinetic, dipolar, length):
    evolved = hartley_cube(kinetic * hartley_cube(amplitude))
    density = evolved * evolved
    field_dd = hartley_cube(dipolar * hartley_cube(density))
    damped = jnp.exp(-TIME_STEP * (potential + CONTACT * density + field_dd)) * evolved
    squares = jnp.sum(damped * damped)
    return damped * lax.rsqrt(squares / float(length) ** 3 + EPSILON)

def refine(values, dimension):
    spectrum = hartley(values, dimension)
    lower_half, upper_half = jnp.split(spectrum, 2, axis=dimension)
    empty_band = jnp.zeros_like(lower_half)
    padded = jnp.concatenate([lower_half, empty_band, empty_band, upper_half], axis=dimension)
    return hartley(padded, dimension) / NC

def grid_kernels(length, spacing):
    waves = wavenumbers(length, spacing)
    squared = waves * waves
    return multipliers(squared[:, None, None], squared[None, :, None], squared[None, None, :], length)

def reference(wave_coarse, potential_coarse, potential_fine):
    kinetic, dipolar = grid_kernels(NC, 2.0)
    amplitude = wave_coarse
    for repeat in range(COARSE_STEPS):
        amplitude = advance(amplitude, potential_coarse, kinetic, dipolar, NC)
    for dimension in range(3):
        amplitude = refine(amplitude, dimension)
    potential = jnp.transpose(potential_fine, (2, 1, 0))
    kinetic, dipolar = grid_kernels(NF, 1.0)
    for repeat in range(FINE_STEPS):
        amplitude = advance(amplitude, potential, kinetic, dipolar, NF)
    return jnp.transpose(amplitude, (2, 1, 0))
```

```python
import functools
import math

import jax
import jax.numpy as jnp
from jax import lax
from jax.experimental import pallas as pl
from jax.experimental.pallas import tpu as pltpu
from jax.sharding import PartitionSpec as P

TIME_STEP = 0.5
CONTACT = 0.4
DIPOLE_STRENGTH = 0.3
EPSILON = 1e-06
HIGH = lax.Precision.HIGH
HIGHEST = lax.Precision.HIGHEST
MESH = pl.DeviceIdType.MESH


def cas_values(product, length):
    phases = 2.0 * math.pi / length * (product % length).astype(jnp.float32)
    return jnp.cos(phases) + jnp.sin(phases)


def cas_matrix(length):
    positions = jnp.arange(length, dtype=jnp.int32)
    return cas_values(positions[:, None] * positions[None, :], length)


def lift_matrix(length):
    positions = jnp.arange(length, dtype=jnp.int32)
    lifted = jnp.where(positions < length // 2, positions, positions + length)
    fine_points = jnp.arange(2 * length, dtype=jnp.int32)
    return cas_values(lifted[:, None] * fine_points[None, :], 2 * length)


def wavenumbers(length, block_count, offset, spacing):
    positions = offset + jnp.arange(block_count, dtype=jnp.int32)
    signed = jnp.where(positions < length // 2, positions, positions - length)
    return 2.0 * math.pi / (length * spacing) * signed.astype(jnp.float32)


def dipolar_weights(along_x, along_y, along_z, length):
    squares = along_x + along_y + along_z
    nonzero = jnp.where(squares > 0, squares, 1.0)
    weights = jnp.where(squares > 0, DIPOLE_STRENGTH * (3.0 * along_z - squares) / nonzero, 0.0)
    return weights / float(length) ** 3


def exchange_kernel(axes, sizes, *refs):
    count = len(axes)
    sources, targets = refs[:count], refs[count : 2 * count]
    send_sems, recv_sems, local_sems = refs[2 * count :]
    row, col = lax.axis_index("rows"), lax.axis_index("cols")

    def place(axis, index):
        return (index, col) if axis == "rows" else (row, index)

    barrier = pltpu.get_barrier_semaphore()
    waits = 0
    for axis in sorted(set(axes)):
        size = sizes[axis]
        me = lax.axis_index(axis)
        for step in range(1, size):
            peer = lax.rem(me + step, size)
            pl.semaphore_signal(barrier, inc=1, device_id=place(axis, peer), device_id_type=MESH)
        waits += size - 1
    pl.semaphore_wait(barrier, waits)
    most = max(sizes[axis] for axis in axes)
    order = sorted(range(1, most), key=lambda step: abs(2 * step - most))
    copies = []
    for step in order:
        for index, axis in enumerate(axes):
            size = sizes[axis]
            if step >= size:
                continue
            me = lax.axis_index(axis)
            peer = lax.rem(me + step, size)
            copy = pltpu.make_async_remote_copy(
                src_ref=sources[index].at[peer],
                dst_ref=targets[index].at[me],
                send_sem=send_sems.at[index, step],
                recv_sem=recv_sems.at[index, step],
                device_id=place(axis, peer),
                device_id_type=MESH,
            )
            copy.start()
            copies.append(copy)
    for index, axis in enumerate(axes):
        me = lax.axis_index(axis)
        copy = pltpu.make_async_copy(
            sources[index].at[me], targets[index].at[me], local_sems.at[index]
        )
        copy.start()
        copies.append(copy)
    for copy in copies:
        copy.wait()


class Exchanger:
    def __init__(self, sizes):
        self.sizes = sizes
        self.calls = 0

    def __call__(self, *pairs):
        arrays = [array for array, _ in pairs]
        axes = tuple(axis for _, axis in pairs)
        most = max(self.sizes.values())
        count = len(arrays)
        self.calls += 1
        return pl.pallas_call(
            functools.partial(exchange_kernel, axes, self.sizes),
            out_shape=[jax.ShapeDtypeStruct(a.shape, a.dtype) for a in arrays],
            in_specs=[pl.BlockSpec(memory_space=pl.ANY)] * count,
            out_specs=[pl.BlockSpec(memory_space=pl.ANY)] * count,
            scratch_shapes=[
                pltpu.SemaphoreType.DMA((count, most)),
                pltpu.SemaphoreType.DMA((count, most)),
                pltpu.SemaphoreType.DMA((count,)),
            ],
            compiler_params=pltpu.CompilerParams(
                collective_id=self.calls - 1, has_side_effects=True
            ),
            name=f"exchange_{self.calls - 1}",
        )(*arrays)


def give(values, matrix, parts, precision=HIGH):
    if matrix is None:
        turned = jnp.transpose(values, (2, 0, 1))
    else:
        turned = jnp.einsum("abl,lk->kab", values, matrix, precision=precision)
    length, rows_extent, cols_extent = turned.shape
    return turned.reshape(parts, length // parts, rows_extent * cols_extent)


def take(received, axis, rows_extent):
    parts, block, area = received.shape
    cols_extent = area // rows_extent
    received = received.reshape(parts, block, rows_extent, cols_extent)
    if axis == "cols":
        return received.transpose(2, 1, 0, 3).reshape(rows_extent, block, parts * cols_extent)
    return received.transpose(1, 3, 0, 2).reshape(block, cols_extent, parts * rows_extent)


def apply(values, matrix, precision=HIGH):
    return jnp.einsum("abl,lk->abk", values, matrix, precision=precision)


def split_product(values, matrix):
    high = matrix.astype(jnp.bfloat16)
    low = (matrix - high.astype(jnp.float32)).astype(jnp.bfloat16)
    top = values.astype(jnp.bfloat16)
    rest = (values - top.astype(jnp.float32)).astype(jnp.bfloat16)
    product = functools.partial(jnp.dot, preferred_element_type=jnp.float32)
    return product(top, high) + (product(top, low) + product(rest, high))


def gather_pieces(received, held):
    parts, chunk = received.shape[0], held.shape[0]
    width = received.shape[2] // chunk
    for s in range(chunk):
        for p in range(parts):
            held[s, :, p * width : (p + 1) * width] = received[p, :, s * width : (s + 1) * width]


def scatter_pieces(held, sent):
    parts, chunk = sent.shape[0], held.shape[0]
    width = sent.shape[2] // chunk
    for s in range(chunk):
        for p in range(parts):
            sent[p, :, s * width : (s + 1) * width] = held[s, :, p * width : (p + 1) * width]


def assemble_kernel(received, matrix, out, held):
    gather_pieces(received, held)
    chunk, k, length = held.shape
    product = split_product(held[...].reshape(chunk * k, length), matrix[...])
    out[...] = product.reshape(out.shape)


def chunk_of(spectators, width, k):
    for chunk in range(1, spectators):
        if spectators % chunk == 0 and chunk * width % 128 == 0 and chunk * k >= 256:
            return chunk
    return spectators


def assemble(received, spectators, matrix):
    parts, k, area = received.shape
    chunk = chunk_of(spectators, area // spectators, k)
    length, points = matrix.shape
    if k % 8:
        held = received.reshape(parts, k, spectators, -1).transpose(2, 1, 0, 3)
        return apply(held.reshape(spectators, k, length), matrix)
    return pl.pallas_call(
        assemble_kernel,
        grid=(spectators // chunk,),
        in_specs=[
            pl.BlockSpec((parts, k, area // spectators * chunk), lambda i: (0, 0, i)),
            pl.BlockSpec((length, points), lambda i: (0, 0)),
        ],
        out_specs=pl.BlockSpec((chunk, k, points), lambda i: (i, 0, 0)),
        out_shape=jax.ShapeDtypeStruct((spectators, k, points), jnp.float32),
        scratch_shapes=[pltpu.VMEM((chunk, k, length), jnp.float32)],
    )(received, matrix)


def halves(values):
    high = values.astype(jnp.bfloat16)
    return high, (values - high.astype(jnp.float32)).astype(jnp.bfloat16)


def product_of(left, right):
    product = functools.partial(jnp.dot, preferred_element_type=jnp.float32)
    return product(left[0], right[0]) + (product(left[0], right[1]) + product(left[1], right[0]))


def planes_kernel(flows, sizes, chunks, volume, *refs):
    row, col = lax.axis_index("rows"), lax.axis_index("cols")

    def place(axis, index):
        return (index, col) if axis == "rows" else (row, index)

    matrix = refs[0]
    inputs = [refs[1 + 4 * i : 5 + 4 * i] for i in range(len(flows))]
    at = 1 + 4 * len(flows)
    outs = refs[at : at + len(flows)]
    at += len(flows)
    high, low = refs[at : at + 2]
    at += 2
    buffers = [refs[at + 9 * i : at + 9 * i + 9] for i in range(len(flows))]

    barrier = pltpu.get_barrier_semaphore()
    waits = 0
    for axis in sorted(set(axis for axis, _ in flows)):
        size = sizes[axis]
        me = lax.axis_index(axis)
        for step in range(1, size):
            peer = lax.rem(me + step, size)
            pl.semaphore_signal(barrier, inc=1, device_id=place(axis, peer), device_id_type=MESH)
        waits += size - 1
    high[...], low[...] = halves(matrix[...])
    pl.semaphore_wait(barrier, waits)

    def copies(flow, turn, c):
        axis, _ = flows[flow]
        size = sizes[axis]
        me = lax.axis_index(axis)
        sent, received = buffers[flow][2 * turn : 2 * turn + 2]
        send_sem, recv_sem = buffers[flow][4 + 2 * turn : 6 + 2 * turn]
        order = sorted(range(1, size), key=lambda step: abs(2 * step - size))
        for step in order:
            peer = lax.rem(me + step, size)
            yield pltpu.make_async_remote_copy(
                src_ref=sent.at[c, peer],
                dst_ref=received.at[c, me],
                send_sem=send_sem.at[c, step],
                recv_sem=recv_sem.at[c, step],
                device_id=place(axis, peer),
                device_id_type=MESH,
            )

    def launch(flow, turn, c):
        me = lax.axis_index(flows[flow][0])
        for copy in copies(flow, turn, c):
            copy.start()
        sent, received = buffers[flow][2 * turn : 2 * turn + 2]
        received[c, me] = sent[c, me]

    def lanes(area, c):
        if chunks == 1:
            return slice(None)
        return pl.ds(pl.multiple_of(c * (area // chunks), 128), area // chunks)

    def first(c, carry):
        for flow in range(len(flows)):
            source, sent = inputs[flow][0], buffers[flow][0]
            part = source[:, :, lanes(source.shape[2], c)]
            part = part.reshape(matrix.shape[0], part.shape[2])
            product = product_of((high[...], low[...]), halves(part))
            sent[c] = product.reshape(sent.shape[1:])
            launch(flow, 0, c)
        return carry

    def second(c, carry):
        for flow in range(len(flows)):
            _, sq_s, sq_k, sq_l = inputs[flow]
            vertical = flows[flow][1]
            held = buffers[flow][8]
            chunk, k, length = held.shape
            for copy in copies(flow, 0, c):
                copy.wait_recv()
            gather_pieces(buffers[flow][1].at[c], held)
            both = (high[...], low[...])
            values = product_of(halves(held[...].reshape(chunk * k, length)), both)
            parts = [sq_s[pl.ds(c * chunk, chunk)], sq_k[...][None], sq_l[...][None]]
            parts = [jnp.broadcast_to(part, held.shape) for part in parts]
            squares = parts[0] + parts[1] + parts[2]
            nonzero = jnp.where(squares > 0, squares, 1.0)
            weights = jnp.where(
                squares > 0, DIPOLE_STRENGTH * (3.0 * parts[vertical] - squares) / nonzero, 0.0
            )
            values = values * (weights / volume).reshape(chunk * k, length)
            held[...] = product_of(halves(values), both).reshape(held.shape)
            scatter_pieces(held, buffers[flow][2].at[c])
            launch(flow, 1, c)
        return carry

    def third(c, carry):
        for flow in range(len(flows)):
            for copy in copies(flow, 1, c):
                copy.wait_recv()
            received, out = buffers[flow][3], outs[flow]
            part = received[c].reshape(matrix.shape[0], received.shape[3])
            product = product_of((high[...], low[...]), halves(part))
            out[:, lanes(out.shape[1], c)] = product
            for turn in range(2):
                for copy in copies(flow, turn, c):
                    copy.wait_send()
        return carry

    for stage in (first, second, third):
        lax.fori_loop(0, chunks, stage, 0)


def planes(exchange, flows, matrix):
    sizes = exchange.sizes
    length = matrix.shape[0]
    counts = []
    for axis, _, received, sq_s, sq_k, _ in flows:
        spectators = sq_s.shape[0]
        width = received.shape[2] // spectators
        counts.append(spectators // chunk_of(spectators, width, sq_k.shape[0]))
    chunks = counts[0] if len(set(counts)) == 1 else 1
    operands, outs, scratch = [matrix], [], []
    scratch += [pltpu.VMEM((length, length), jnp.bfloat16)] * 2
    for axis, _, received, sq_s, sq_k, sq_l in flows:
        operands += [received, sq_s[:, None, None], sq_k[:, None], sq_l[None, :]]
        area, k, size = received.shape[2], sq_k.shape[0], sizes[axis]
        outs.append(jax.ShapeDtypeStruct((length, area), jnp.float32))
        scratch += [pltpu.VMEM((chunks, size, k, area // chunks), jnp.float32)] * 4
        scratch += [pltpu.SemaphoreType.DMA((chunks, size))] * 4
        scratch += [pltpu.VMEM((sq_s.shape[0] // chunks, k, length), jnp.float32)]
    exchange.calls += 1
    vmem = pl.BlockSpec(memory_space=pltpu.VMEM)
    return pl.pallas_call(
        functools.partial(
            planes_kernel,
            tuple((flow[0], flow[1]) for flow in flows),
            sizes,
            chunks,
            float(length) ** 3,
        ),
        out_shape=outs,
        in_specs=[vmem] * len(operands),
        out_specs=[vmem] * len(outs),
        scratch_shapes=scratch,
        compiler_params=pltpu.CompilerParams(
            collective_id=exchange.calls - 1,
            has_side_effects=True,
            vmem_limit_bytes=60 * 1024 * 1024,
        ),
        name=f"planes_{exchange.calls - 1}",
    )(*operands)


def blocks(turned, parts):
    first, length, last = turned.shape
    turned = turned.reshape(first, parts, length // parts, last).transpose(1, 0, 2, 3)
    return turned.reshape(parts, first, length // parts * last)


def product_blocks(matrix, received, parts):
    turned = jnp.dot(matrix, received.reshape(-1, received.shape[2]), precision=HIGH)
    return turned.reshape(parts, turned.shape[0] // parts, turned.shape[1])


def per_device_pencils(sizes, wave_coarse, potential_coarse, potential_fine):
    row, col = lax.axis_index("rows"), lax.axis_index("cols")
    rows, cols = sizes["rows"], sizes["cols"]
    nc, nf = wave_coarse.shape[2], potential_fine.shape[2]
    exchange = Exchanger(sizes)

    coarse_matrix = cas_matrix(nc)
    fine_matrix = cas_matrix(nf)
    decay = jnp.exp(-0.5 * TIME_STEP * wavenumbers(nc, nc, 0, 2.0) ** 2)[:, None] / nc
    evolve = jnp.dot(coarse_matrix, decay * coarse_matrix, precision=HIGHEST)
    lift = jnp.dot(coarse_matrix, decay * lift_matrix(nc), precision=HIGHEST)

    xr = yr = nc // rows
    spectators = nc // cols
    turned = jnp.einsum("xyz,zk->ykx", wave_coarse, evolve, precision=HIGH)
    (got,) = exchange((blocks(turned, cols), "cols"))
    (got,) = exchange((product_blocks(evolve.T, got, rows), "rows"))
    evolved = assemble(got, spectators, evolve)
    turned = jnp.einsum("zyx,xk->zky", evolved * evolved, coarse_matrix, precision=HIGH)
    got, back = exchange(
        (blocks(turned, cols), "cols"), (give(evolved.transpose(1, 0, 2), None, rows), "rows")
    )
    back = take(back, "rows", yr)
    got, back = exchange(
        (product_blocks(coarse_matrix, got, rows), "rows"), (give(back, None, cols), "cols")
    )
    spectrum, evolved = assemble(got, spectators, coarse_matrix), take(back, "cols", xr)
    z_block, x_block = nc // rows, nc // cols
    weights = dipolar_weights(
        wavenumbers(nc, x_block, col * x_block, 2.0)[:, None, None] ** 2,
        wavenumbers(nc, nc, 0, 2.0)[None, None, :] ** 2,
        wavenumbers(nc, z_block, row * z_block, 2.0)[None, :, None] ** 2,
        nc,
    )
    turned = jnp.einsum("xzy,yk->xkz", weights * spectrum, coarse_matrix, precision=HIGH)
    (got,) = exchange((blocks(turned, cols), "cols"))
    (got,) = exchange((product_blocks(coarse_matrix, got, rows), "rows"))
    field_dd = assemble(got, spectators, coarse_matrix).transpose(1, 0, 2)
    density = evolved * evolved
    damped = jnp.exp(-TIME_STEP * (potential_coarse + CONTACT * density + field_dd)) * evolved
    partial_sum = jnp.sum(damped * damped)

    got, sums = exchange(
        (blocks(jnp.einsum("xyz,zk->ykx", damped, lift, precision=HIGH), cols), "cols"),
        (jnp.full((cols, 8, 128), partial_sum, jnp.float32), "cols"),
    )
    partial_sum = jnp.sum(sums[:, 0, 0])
    got, sums = exchange(
        (product_blocks(lift.T, got, rows), "rows"),
        (jnp.full((rows, 8, 128), partial_sum, jnp.float32), "rows"),
    )
    scale = lax.rsqrt(jnp.sum(sums[:, 0, 0]) / float(nc) ** 3 + EPSILON)
    evolved = assemble(got, nf // cols, lift) * scale

    density = evolved * evolved
    half = nf // 2
    near, far = fine_matrix[:, :half], fine_matrix[:, half:]
    got_near, got_far = exchange(
        (blocks(jnp.einsum("zyx,xk->ykz", density, near, precision=HIGH), rows), "rows"),
        (blocks(jnp.einsum("zyx,xk->zky", density, far, precision=HIGH), cols), "cols"),
    )
    y_block, z_block = nf // cols, nf // rows
    near_block, far_block = half // rows, half // cols
    every = wavenumbers(nf, nf, 0, 1.0) ** 2
    near_flow = (
        "cols",
        2,
        got_near,
        wavenumbers(nf, near_block, row * near_block, 1.0) ** 2,
        wavenumbers(nf, y_block, col * y_block, 1.0) ** 2,
        every,
    )
    far_flow = (
        "rows",
        1,
        got_far,
        wavenumbers(nf, far_block, half + col * far_block, 1.0) ** 2,
        wavenumbers(nf, z_block, row * z_block, 1.0) ** 2,
        every,
    )
    got_far, got_near = planes(exchange, (far_flow, near_flow), fine_matrix)
    got_near, got_far = exchange(
        (got_near.reshape(rows, nf // rows, -1), "rows"),
        (got_far.reshape(cols, nf // cols, -1), "cols"),
    )
    z_extent, y_extent = nf // cols, nf // rows
    near_field = got_near.reshape(rows, y_extent, near_block, z_extent)
    near_field = near_field.transpose(3, 1, 0, 2).reshape(z_extent, y_extent, half)
    far_field = got_far.reshape(cols, z_extent, far_block, y_extent)
    far_field = far_field.transpose(1, 3, 0, 2).reshape(z_extent, y_extent, half)
    spectrum = jnp.concatenate([near_field, far_field], axis=2)
    field_dd = jnp.einsum("zyk,kx->zyx", spectrum, fine_matrix, precision=HIGH)
    damped = jnp.exp(-TIME_STEP * (potential_fine + CONTACT * density + field_dd)) * evolved
    total = jnp.sum(damped * damped)
    for axis in ("rows", "cols"):
        (sums,) = exchange((jnp.full((sizes[axis], 8, 128), total, jnp.float32), axis))
        total = jnp.sum(sums[:, 0, 0])
    return damped * lax.rsqrt(total / float(nf) ** 3 + EPSILON)


def slab_of(row, col, rows, cols):
    half = row // (rows // 2)
    pair = col // 2
    other = lax.rem(col + pair, 2)
    far = half + other - 2 * half * other
    return (cols // 2) * (far * (rows // 2) + lax.rem(row, rows // 2)) + pair


def peers_of(kind, row, col, rows, cols):
    me = row * cols + col
    middle = rows // 2
    order = [(a, b) for a in range(rows) for b in range(cols)]
    order.sort(key=lambda step: (step == (0, 0), abs(2 * step[0] - rows)))
    peers = []
    if kind == "all":
        for a, b in order:
            r, c = lax.rem(row + a, rows), lax.rem(col + b, cols)
            peers.append((r * cols + c, me, r, c))
    elif kind == "both":
        for a, b in order:
            r, c = lax.rem(row + a, rows), lax.rem(col + b, cols)
            peers.append((slab_of(r, c, rows, cols), me, r, c))
    elif kind == "half":
        base = row // middle * middle
        mine = slab_of(row, col, rows, cols)
        order = [(a, b) for a in range(middle) for b in range(cols)]
        order.sort(key=lambda step: (step == (0, 0), abs(2 * step[0] - middle)))
        for a, b in order:
            r, c = lax.rem(lax.rem(row, middle) + a, middle), lax.rem(col + b, cols)
            peers.append((r * cols + c, mine, base + r, c))
    elif kind == "cols":
        for b in list(range(1, cols)) + [0]:
            c = lax.rem(col + b, cols)
            peers.append((c, col, row, c))
    return peers


def swap_kernel(kinds, sizes, *refs):
    count = len(kinds)
    sources, targets = refs[:count], refs[count : 2 * count]
    send_sems, recv_sems, local_sems = refs[2 * count :]
    row, col = lax.axis_index("rows"), lax.axis_index("cols")
    rows, cols = sizes["rows"], sizes["cols"]
    lists = [peers_of(kind, row, col, rows, cols) for kind in kinds]

    barrier = pltpu.get_barrier_semaphore()
    widest = max(lists, key=len)
    for _, _, r, c in widest[:-1]:
        pl.semaphore_signal(barrier, inc=1, device_id=(r, c), device_id_type=MESH)
    pl.semaphore_wait(barrier, len(widest) - 1)
    copies = []
    for index, peers in enumerate(lists):
        for step, (source, target, r, c) in enumerate(peers[:-1]):
            copy = pltpu.make_async_remote_copy(
                src_ref=sources[index].at[source],
                dst_ref=targets[index].at[target],
                send_sem=send_sems.at[index, step],
                recv_sem=recv_sems.at[index, step],
                device_id=(r, c),
                device_id_type=MESH,
            )
            copy.start()
            copies.append(copy)
        source, target, _, _ = peers[-1]
        copy = pltpu.make_async_copy(
            sources[index].at[source], targets[index].at[target], local_sems.at[index]
        )
        copy.start()
        copies.append(copy)
    for copy in copies:
        copy.wait()


def swap(exchange, *pairs):
    arrays = [array for array, _ in pairs]
    kinds = tuple(kind for _, kind in pairs)
    count = len(arrays)
    rows, cols = exchange.sizes["rows"], exchange.sizes["cols"]
    slots = {"all": rows * cols, "both": rows * cols, "half": rows * cols // 2, "cols": cols}
    exchange.calls += 1
    return pl.pallas_call(
        functools.partial(swap_kernel, kinds, exchange.sizes),
        out_shape=[
            jax.ShapeDtypeStruct((slots[kind],) + a.shape[1:], a.dtype) for a, kind in pairs
        ],
        in_specs=[pl.BlockSpec(memory_space=pl.ANY)] * count,
        out_specs=[pl.BlockSpec(memory_space=pl.ANY)] * count,
        scratch_shapes=[
            pltpu.SemaphoreType.DMA((count, rows * cols)),
            pltpu.SemaphoreType.DMA((count, rows * cols)),
            pltpu.SemaphoreType.DMA((count,)),
        ],
        compiler_params=pltpu.CompilerParams(
            collective_id=exchange.calls - 1, has_side_effects=True
        ),
        name=f"swap_{exchange.calls - 1}",
    )(*arrays)


def along(values, matrix, spec):
    return jnp.einsum(spec, values, matrix, precision=HIGH)


def per_device(sizes, wave_coarse, potential_coarse, potential_fine):
    row, col = lax.axis_index("rows"), lax.axis_index("cols")
    rows, cols = sizes["rows"], sizes["cols"]
    devices, middle = rows * cols, rows // 2
    me, half = row * cols + col, row // middle
    nc, nf = wave_coarse.shape[2], potential_fine.shape[2]
    exchange = Exchanger(sizes)

    coarse_matrix = cas_matrix(nc)
    fine_matrix = cas_matrix(nf)
    decay = jnp.exp(-0.5 * TIME_STEP * wavenumbers(nc, nc, 0, 2.0) ** 2)[:, None] / nc
    evolve = jnp.dot(coarse_matrix, decay * coarse_matrix, precision=HIGHEST)
    lift = jnp.dot(coarse_matrix, decay * lift_matrix(nc), precision=HIGHEST)

    xb, yb, zb = nc // rows, nc // cols, nc // devices
    wave = along(wave_coarse, evolve, "xyz,zk->kxy").reshape(devices, -1, 128)
    trap = potential_coarse.transpose(2, 0, 1).reshape(devices, -1, 128)
    wave, trap = swap(exchange, (wave, "all"), (trap, "all"))

    def planes_of(got):
        got = got.reshape(rows, cols, zb, xb, yb).transpose(2, 0, 3, 1, 4)
        return got.reshape(zb, nc, nc)

    wave, trap = planes_of(wave), planes_of(trap)
    evolved = along(along(wave, evolve, "zxy,xk->zky"), evolve, "zky,yl->zkl")
    density = evolved * evolved
    spectrum = along(along(density, coarse_matrix, "zxy,xk->zky"), coarse_matrix, "zky,yl->zkl")
    sent = spectrum.reshape(zb, devices, zb, nc).transpose(1, 0, 2, 3).reshape(devices, -1, 128)
    (got,) = swap(exchange, (sent, "all"))
    got = along(got.reshape(nc, zb, nc), coarse_matrix, "zkl,zm->mkl")
    got = got * dipolar_weights(
        wavenumbers(nc, zb, me * zb, 2.0)[None, :, None] ** 2,
        wavenumbers(nc, nc, 0, 2.0)[None, None, :] ** 2,
        wavenumbers(nc, nc, 0, 2.0)[:, None, None] ** 2,
        nc,
    )
    got = along(along(got, coarse_matrix, "zkl,zm->mkl"), coarse_matrix, "zkl,ly->zky")
    (got,) = swap(exchange, (got.reshape(devices, -1, 128), "all"))
    got = got.reshape(devices, zb, zb, nc).transpose(1, 0, 2, 3).reshape(zb, nc, nc)
    field_dd = along(got, coarse_matrix, "zky,kx->zxy")
    damped = jnp.exp(-TIME_STEP * (trap + CONTACT * density + field_dd)) * evolved
    partial_sum = jnp.sum(damped * damped)

    slabs, yf, kb = devices // 2, nf // (devices // 2), nf // devices
    lifted = along(damped, lift, "zxy,yk->kzx").reshape(slabs, yf, zb, nc)
    lifted = lifted.transpose(0, 2, 1, 3).reshape(slabs, -1, 128)
    got, sums = swap(
        exchange,
        (lifted, "both"),
        (jnp.full((slabs, 8, 128), partial_sum, jnp.float32), "both"),
    )
    scale = lax.rsqrt(jnp.sum(sums[:, 0, 0]) / float(nc) ** 3 + EPSILON)
    slab = along(got.reshape(nc, yf, nc), lift, "zyx,zk->yxk") * scale

    density = along(slab, lift, "yxz,xk->ykz") ** 2
    columns = lax.dynamic_slice_in_dim(fine_matrix, half * (nf // 2), nf // 2, 1)
    spectrum = along(along(density, columns, "yxz,xk->ykz"), fine_matrix, "ykz,zm->ykm")
    sent = spectrum.transpose(1, 0, 2).reshape(slabs, kb, yf, nf)
    yo, zo = nf // rows, nf // cols
    given = slab.reshape(yf, nc, cols, zo).transpose(2, 3, 0, 1).reshape(cols, -1, 128)
    got, given = swap(exchange, (sent, "half"), (given, "cols"))
    got = got.transpose(1, 0, 2, 3).reshape(kb, nf, nf)
    got = along(got, fine_matrix, "kyz,yl->klz")
    every = wavenumbers(nf, nf, 0, 1.0) ** 2
    got = got * dipolar_weights(
        wavenumbers(nf, kb, me * kb, 1.0)[:, None, None] ** 2,
        every[None, :, None],
        every[None, None, :],
        nf,
    )
    got = along(along(got, fine_matrix, "kyz,yl->klz"), fine_matrix, "kyz,zm->kym")
    got = got.reshape(kb, rows, yo, cols, zo).transpose(1, 3, 0, 2, 4).reshape(devices, -1, 128)
    (got,) = swap(exchange, (got, "all"))
    field_dd = along(got.reshape(nf, yo, zo), fine_matrix, "kyz,kx->zyx")

    given = given.reshape(cols, zo, yf, nc)
    own = [2 * e + e % 2 for e in range(cols // 2)]
    given = jnp.stack([given[c] for c in own], 1).reshape(zo, yo, nc)
    evolved = along(given, lift, "zyx,xk->zyk")
    density = evolved * evolved
    damped = jnp.exp(-TIME_STEP * (potential_fine + CONTACT * density + field_dd)) * evolved
    total = jnp.full((devices, 8, 128), jnp.sum(damped * damped), jnp.float32)
    (sums,) = swap(exchange, (total, "all"))
    return damped * lax.rsqrt(jnp.sum(sums[:, 0, 0]) / float(nf) ** 3 + EPSILON)


def fits_slabs(sizes, nc, nf):
    devices = sizes["rows"] * sizes["cols"]
    return sizes["rows"] % 2 == 0 and sizes["cols"] % 2 == 0 and nc % devices == 0


def solution(mesh):
    sizes = {"rows": mesh.shape["rows"], "cols": mesh.shape["cols"]}
    placed = (P("rows", "cols", None), P("rows", "cols", None), P("cols", "rows", None))

    def run(wave_coarse, potential_coarse, potential_fine):
        nc, nf = wave_coarse.shape[0], potential_fine.shape[0]
        body = per_device if fits_slabs(sizes, nc, nf) else per_device_pencils
        return jax.shard_map(
            functools.partial(body, sizes),
            mesh=mesh,
            in_specs=placed,
            out_specs=P("cols", "rows", None),
            check_vma=False,
        )(wave_coarse, potential_coarse, potential_fine)

    return run
```

```python
import functools
import math

import jax
import jax.numpy as jnp
from jax import lax
from jax.experimental import pallas as pl
from jax.experimental.pallas import tpu as pltpu
from jax.sharding import PartitionSpec as P

TIME_STEP = 0.5
CONTACT = 0.4
DIPOLE_STRENGTH = 0.3
EPSILON = 1e-06
HIGH = lax.Precision.HIGH
HIGHEST = lax.Precision.HIGHEST
MESH = pl.DeviceIdType.MESH


def cas_values(product, length):
    phases = 2.0 * math.pi / length * (product % length).astype(jnp.float32)
    return jnp.cos(phases) + jnp.sin(phases)


def cas_matrix(length):
    positions = jnp.arange(length, dtype=jnp.int32)
    return cas_values(positions[:, None] * positions[None, :], length)


def lift_matrix(length):
    positions = jnp.arange(length, dtype=jnp.int32)
    lifted = jnp.where(positions < length // 2, positions, positions + length)
    fine_points = jnp.arange(2 * length, dtype=jnp.int32)
    return cas_values(lifted[:, None] * fine_points[None, :], 2 * length)


def wavenumbers(length, block_count, offset, spacing):
    positions = offset + jnp.arange(block_count, dtype=jnp.int32)
    signed = jnp.where(positions < length // 2, positions, positions - length)
    return 2.0 * math.pi / (length * spacing) * signed.astype(jnp.float32)


def dipolar_weights(along_x, along_y, along_z, length):
    squares = along_x + along_y + along_z
    nonzero = jnp.where(squares > 0, squares, 1.0)
    weights = jnp.where(squares > 0, DIPOLE_STRENGTH * (3.0 * along_z - squares) / nonzero, 0.0)
    return weights / float(length) ** 3


def exchange_kernel(axes, sizes, *refs):
    count = len(axes)
    sources, targets = refs[:count], refs[count : 2 * count]
    send_sems, recv_sems, local_sems = refs[2 * count :]
    row, col = lax.axis_index("rows"), lax.axis_index("cols")

    def place(axis, index):
        return (index, col) if axis == "rows" else (row, index)

    barrier = pltpu.get_barrier_semaphore()
    waits = 0
    for axis in sorted(set(axes)):
        size = sizes[axis]
        me = lax.axis_index(axis)
        for step in range(1, size):
            peer = lax.rem(me + step, size)
            pl.semaphore_signal(barrier, inc=1, device_id=place(axis, peer), device_id_type=MESH)
        waits += size - 1
    pl.semaphore_wait(barrier, waits)
    most = max(sizes[axis] for axis in axes)
    order = sorted(range(1, most), key=lambda step: abs(2 * step - most))
    copies = []
    for step in order:
        for index, axis in enumerate(axes):
            size = sizes[axis]
            if step >= size:
                continue
            me = lax.axis_index(axis)
            peer = lax.rem(me + step, size)
            copy = pltpu.make_async_remote_copy(
                src_ref=sources[index].at[peer],
                dst_ref=targets[index].at[me],
                send_sem=send_sems.at[index, step],
                recv_sem=recv_sems.at[index, step],
                device_id=place(axis, peer),
                device_id_type=MESH,
            )
            copy.start()
            copies.append(copy)
    for index, axis in enumerate(axes):
        me = lax.axis_index(axis)
        copy = pltpu.make_async_copy(
            sources[index].at[me], targets[index].at[me], local_sems.at[index]
        )
        copy.start()
        copies.append(copy)
    for copy in copies:
        copy.wait()


class Exchanger:
    def __init__(self, sizes):
        self.sizes = sizes
        self.calls = 0

    def __call__(self, *pairs):
        arrays = [array for array, _ in pairs]
        axes = tuple(axis for _, axis in pairs)
        most = max(self.sizes.values())
        count = len(arrays)
        self.calls += 1
        return pl.pallas_call(
            functools.partial(exchange_kernel, axes, self.sizes),
            out_shape=[jax.ShapeDtypeStruct(a.shape, a.dtype) for a in arrays],
            in_specs=[pl.BlockSpec(memory_space=pl.ANY)] * count,
            out_specs=[pl.BlockSpec(memory_space=pl.ANY)] * count,
            scratch_shapes=[
                pltpu.SemaphoreType.DMA((count, most)),
                pltpu.SemaphoreType.DMA((count, most)),
                pltpu.SemaphoreType.DMA((count,)),
            ],
            compiler_params=pltpu.CompilerParams(
                collective_id=self.calls - 1, has_side_effects=True
            ),
            name=f"exchange_{self.calls - 1}",
        )(*arrays)


def give(values, matrix, parts, precision=HIGH):
    if matrix is None:
        turned = jnp.transpose(values, (2, 0, 1))
    else:
        turned = jnp.einsum("abl,lk->kab", values, matrix, precision=precision)
    length, rows_extent, cols_extent = turned.shape
    return turned.reshape(parts, length // parts, rows_extent * cols_extent)


def take(received, axis, rows_extent):
    parts, block, area = received.shape
    cols_extent = area // rows_extent
    received = received.reshape(parts, block, rows_extent, cols_extent)
    if axis == "cols":
        return received.transpose(2, 1, 0, 3).reshape(rows_extent, block, parts * cols_extent)
    return received.transpose(1, 3, 0, 2).reshape(block, cols_extent, parts * rows_extent)


def apply(values, matrix, precision=HIGH):
    return jnp.einsum("abl,lk->abk", values, matrix, precision=precision)


def split_product(values, matrix):
    high = matrix.astype(jnp.bfloat16)
    low = (matrix - high.astype(jnp.float32)).astype(jnp.bfloat16)
    top = values.astype(jnp.bfloat16)
    rest = (values - top.astype(jnp.float32)).astype(jnp.bfloat16)
    product = functools.partial(jnp.dot, preferred_element_type=jnp.float32)
    return product(top, high) + (product(top, low) + product(rest, high))


def gather_pieces(received, held):
    parts, chunk = received.shape[0], held.shape[0]
    width = received.shape[2] // chunk
    for s in range(chunk):
        for p in range(parts):
            held[s, :, p * width : (p + 1) * width] = received[p, :, s * width : (s + 1) * width]


def scatter_pieces(held, sent):
    parts, chunk = sent.shape[0], held.shape[0]
    width = sent.shape[2] // chunk
    for s in range(chunk):
        for p in range(parts):
            sent[p, :, s * width : (s + 1) * width] = held[s, :, p * width : (p + 1) * width]


def assemble_kernel(received, matrix, out, held):
    gather_pieces(received, held)
    chunk, k, length = held.shape
    product = split_product(held[...].reshape(chunk * k, length), matrix[...])
    out[...] = product.reshape(out.shape)


def chunk_of(spectators, width, k):
    for chunk in range(1, spectators):
        if spectators % chunk == 0 and chunk * width % 128 == 0 and chunk * k >= 256:
            return chunk
    return spectators


def assemble(received, spectators, matrix):
    parts, k, area = received.shape
    chunk = chunk_of(spectators, area // spectators, k)
    length, points = matrix.shape
    if k % 8:
        held = received.reshape(parts, k, spectators, -1).transpose(2, 1, 0, 3)
        return apply(held.reshape(spectators, k, length), matrix)
    return pl.pallas_call(
        assemble_kernel,
        grid=(spectators // chunk,),
        in_specs=[
            pl.BlockSpec((parts, k, area // spectators * chunk), lambda i: (0, 0, i)),
            pl.BlockSpec((length, points), lambda i: (0, 0)),
        ],
        out_specs=pl.BlockSpec((chunk, k, points), lambda i: (i, 0, 0)),
        out_shape=jax.ShapeDtypeStruct((spectators, k, points), jnp.float32),
        scratch_shapes=[pltpu.VMEM((chunk, k, length), jnp.float32)],
    )(received, matrix)


def halves(values):
    high = values.astype(jnp.bfloat16)
    return high, (values - high.astype(jnp.float32)).astype(jnp.bfloat16)


def product_of(left, right):
    product = functools.partial(jnp.dot, preferred_element_type=jnp.float32)
    return product(left[0], right[0]) + (product(left[0], right[1]) + product(left[1], right[0]))


def planes_kernel(flows, sizes, chunks, volume, *refs):
    row, col = lax.axis_index("rows"), lax.axis_index("cols")

    def place(axis, index):
        return (index, col) if axis == "rows" else (row, index)

    matrix = refs[0]
    inputs = [refs[1 + 4 * i : 5 + 4 * i] for i in range(len(flows))]
    at = 1 + 4 * len(flows)
    outs = refs[at : at + len(flows)]
    at += len(flows)
    high, low = refs[at : at + 2]
    at += 2
    buffers = [refs[at + 9 * i : at + 9 * i + 9] for i in range(len(flows))]

    barrier = pltpu.get_barrier_semaphore()
    waits = 0
    for axis in sorted(set(axis for axis, _ in flows)):
        size = sizes[axis]
        me = lax.axis_index(axis)
        for step in range(1, size):
            peer = lax.rem(me + step, size)
            pl.semaphore_signal(barrier, inc=1, device_id=place(axis, peer), device_id_type=MESH)
        waits += size - 1
    high[...], low[...] = halves(matrix[...])
    pl.semaphore_wait(barrier, waits)

    def copies(flow, turn, c):
        axis, _ = flows[flow]
        size = sizes[axis]
        me = lax.axis_index(axis)
        sent, received = buffers[flow][2 * turn : 2 * turn + 2]
        send_sem, recv_sem = buffers[flow][4 + 2 * turn : 6 + 2 * turn]
        order = sorted(range(1, size), key=lambda step: abs(2 * step - size))
        for step in order:
            peer = lax.rem(me + step, size)
            yield pltpu.make_async_remote_copy(
                src_ref=sent.at[c, peer],
                dst_ref=received.at[c, me],
                send_sem=send_sem.at[c, step],
                recv_sem=recv_sem.at[c, step],
                device_id=place(axis, peer),
                device_id_type=MESH,
            )

    def launch(flow, turn, c):
        me = lax.axis_index(flows[flow][0])
        for copy in copies(flow, turn, c):
            copy.start()
        sent, received = buffers[flow][2 * turn : 2 * turn + 2]
        received[c, me] = sent[c, me]

    def lanes(area, c):
        if chunks == 1:
            return slice(None)
        return pl.ds(pl.multiple_of(c * (area // chunks), 128), area // chunks)

    def first(c, carry):
        for flow in range(len(flows)):
            source, sent = inputs[flow][0], buffers[flow][0]
            part = source[:, :, lanes(source.shape[2], c)]
            part = part.reshape(matrix.shape[0], part.shape[2])
            product = product_of((high[...], low[...]), halves(part))
            sent[c] = product.reshape(sent.shape[1:])
            launch(flow, 0, c)
        return carry

    def second(c, carry):
        for flow in range(len(flows)):
            _, sq_s, sq_k, sq_l = inputs[flow]
            vertical = flows[flow][1]
            held = buffers[flow][8]
            chunk, k, length = held.shape
            for copy in copies(flow, 0, c):
                copy.wait_recv()
            gather_pieces(buffers[flow][1].at[c], held)
            both = (high[...], low[...])
            values = product_of(halves(held[...].reshape(chunk * k, length)), both)
            parts = [sq_s[pl.ds(c * chunk, chunk)], sq_k[...][None], sq_l[...][None]]
            parts = [jnp.broadcast_to(part, held.shape) for part in parts]
            squares = parts[0] + parts[1] + parts[2]
            nonzero = jnp.where(squares > 0, squares, 1.0)
            weights = jnp.where(
                squares > 0, DIPOLE_STRENGTH * (3.0 * parts[vertical] - squares) / nonzero, 0.0
            )
            values = values * (weights / volume).reshape(chunk * k, length)
            held[...] = product_of(halves(values), both).reshape(held.shape)
            scatter_pieces(held, buffers[flow][2].at[c])
            launch(flow, 1, c)
        return carry

    def third(c, carry):
        for flow in range(len(flows)):
            for copy in copies(flow, 1, c):
                copy.wait_recv()
            received, out = buffers[flow][3], outs[flow]
            part = received[c].reshape(matrix.shape[0], received.shape[3])
            product = product_of((high[...], low[...]), halves(part))
            out[:, lanes(out.shape[1], c)] = product
            for turn in range(2):
                for copy in copies(flow, turn, c):
                    copy.wait_send()
        return carry

    for stage in (first, second, third):
        lax.fori_loop(0, chunks, stage, 0)


def planes(exchange, flows, matrix):
    sizes = exchange.sizes
    length = matrix.shape[0]
    counts = []
    for axis, _, received, sq_s, sq_k, _ in flows:
        spectators = sq_s.shape[0]
        width = received.shape[2] // spectators
        counts.append(spectators // chunk_of(spectators, width, sq_k.shape[0]))
    chunks = counts[0] if len(set(counts)) == 1 else 1
    operands, outs, scratch = [matrix], [], []
    scratch += [pltpu.VMEM((length, length), jnp.bfloat16)] * 2
    for axis, _, received, sq_s, sq_k, sq_l in flows:
        operands += [received, sq_s[:, None, None], sq_k[:, None], sq_l[None, :]]
        area, k, size = received.shape[2], sq_k.shape[0], sizes[axis]
        outs.append(jax.ShapeDtypeStruct((length, area), jnp.float32))
        scratch += [pltpu.VMEM((chunks, size, k, area // chunks), jnp.float32)] * 4
        scratch += [pltpu.SemaphoreType.DMA((chunks, size))] * 4
        scratch += [pltpu.VMEM((sq_s.shape[0] // chunks, k, length), jnp.float32)]
    exchange.calls += 1
    vmem = pl.BlockSpec(memory_space=pltpu.VMEM)
    return pl.pallas_call(
        functools.partial(
            planes_kernel,
            tuple((flow[0], flow[1]) for flow in flows),
            sizes,
            chunks,
            float(length) ** 3,
        ),
        out_shape=outs,
        in_specs=[vmem] * len(operands),
        out_specs=[vmem] * len(outs),
        scratch_shapes=scratch,
        compiler_params=pltpu.CompilerParams(
            collective_id=exchange.calls - 1,
            has_side_effects=True,
            vmem_limit_bytes=60 * 1024 * 1024,
        ),
        name=f"planes_{exchange.calls - 1}",
    )(*operands)


def blocks(turned, parts):
    first, length, last = turned.shape
    turned = turned.reshape(first, parts, length // parts, last).transpose(1, 0, 2, 3)
    return turned.reshape(parts, first, length // parts * last)


def product_blocks(matrix, received, parts):
    turned = jnp.dot(matrix, received.reshape(-1, received.shape[2]), precision=HIGH)
    return turned.reshape(parts, turned.shape[0] // parts, turned.shape[1])


def per_device_pencils(sizes, wave_coarse, potential_coarse, potential_fine):
    row, col = lax.axis_index("rows"), lax.axis_index("cols")
    rows, cols = sizes["rows"], sizes["cols"]
    nc, nf = wave_coarse.shape[2], potential_fine.shape[2]
    exchange = Exchanger(sizes)

    coarse_matrix = cas_matrix(nc)
    fine_matrix = cas_matrix(nf)
    decay = jnp.exp(-0.5 * TIME_STEP * wavenumbers(nc, nc, 0, 2.0) ** 2)[:, None] / nc
    evolve = jnp.dot(coarse_matrix, decay * coarse_matrix, precision=HIGHEST)
    lift = jnp.dot(coarse_matrix, decay * lift_matrix(nc), precision=HIGHEST)

    xr = yr = nc // rows
    spectators = nc // cols
    turned = jnp.einsum("xyz,zk->ykx", wave_coarse, evolve, precision=HIGH)
    (got,) = exchange((blocks(turned, cols), "cols"))
    (got,) = exchange((product_blocks(evolve.T, got, rows), "rows"))
    evolved = assemble(got, spectators, evolve)
    turned = jnp.einsum("zyx,xk->zky", evolved * evolved, coarse_matrix, precision=HIGH)
    got, back = exchange(
        (blocks(turned, cols), "cols"), (give(evolved.transpose(1, 0, 2), None, rows), "rows")
    )
    back = take(back, "rows", yr)
    got, back = exchange(
        (product_blocks(coarse_matrix, got, rows), "rows"), (give(back, None, cols), "cols")
    )
    spectrum, evolved = assemble(got, spectators, coarse_matrix), take(back, "cols", xr)
    z_block, x_block = nc // rows, nc // cols
    weights = dipolar_weights(
        wavenumbers(nc, x_block, col * x_block, 2.0)[:, None, None] ** 2,
        wavenumbers(nc, nc, 0, 2.0)[None, None, :] ** 2,
        wavenumbers(nc, z_block, row * z_block, 2.0)[None, :, None] ** 2,
        nc,
    )
    turned = jnp.einsum("xzy,yk->xkz", weights * spectrum, coarse_matrix, precision=HIGH)
    (got,) = exchange((blocks(turned, cols), "cols"))
    (got,) = exchange((product_blocks(coarse_matrix, got, rows), "rows"))
    field_dd = assemble(got, spectators, coarse_matrix).transpose(1, 0, 2)
    density = evolved * evolved
    damped = jnp.exp(-TIME_STEP * (potential_coarse + CONTACT * density + field_dd)) * evolved
    partial_sum = jnp.sum(damped * damped)

    got, sums = exchange(
        (blocks(jnp.einsum("xyz,zk->ykx", damped, lift, precision=HIGH), cols), "cols"),
        (jnp.full((cols, 8, 128), partial_sum, jnp.float32), "cols"),
    )
    partial_sum = jnp.sum(sums[:, 0, 0])
    got, sums = exchange(
        (product_blocks(lift.T, got, rows), "rows"),
        (jnp.full((rows, 8, 128), partial_sum, jnp.float32), "rows"),
    )
    scale = lax.rsqrt(jnp.sum(sums[:, 0, 0]) / float(nc) ** 3 + EPSILON)
    evolved = assemble(got, nf // cols, lift) * scale

    density = evolved * evolved
    half = nf // 2
    near, far = fine_matrix[:, :half], fine_matrix[:, half:]
    got_near, got_far = exchange(
        (blocks(jnp.einsum("zyx,xk->ykz", density, near, precision=HIGH), rows), "rows"),
        (blocks(jnp.einsum("zyx,xk->zky", density, far, precision=HIGH), cols), "cols"),
    )
    y_block, z_block = nf // cols, nf // rows
    near_block, far_block = half // rows, half // cols
    every = wavenumbers(nf, nf, 0, 1.0) ** 2
    near_flow = (
        "cols",
        2,
        got_near,
        wavenumbers(nf, near_block, row * near_block, 1.0) ** 2,
        wavenumbers(nf, y_block, col * y_block, 1.0) ** 2,
        every,
    )
    far_flow = (
        "rows",
        1,
        got_far,
        wavenumbers(nf, far_block, half + col * far_block, 1.0) ** 2,
        wavenumbers(nf, z_block, row * z_block, 1.0) ** 2,
        every,
    )
    got_far, got_near = planes(exchange, (far_flow, near_flow), fine_matrix)
    got_near, got_far = exchange(
        (got_near.reshape(rows, nf // rows, -1), "rows"),
        (got_far.reshape(cols, nf // cols, -1), "cols"),
    )
    z_extent, y_extent = nf // cols, nf // rows
    near_field = got_near.reshape(rows, y_extent, near_block, z_extent)
    near_field = near_field.transpose(3, 1, 0, 2).reshape(z_extent, y_extent, half)
    far_field = got_far.reshape(cols, z_extent, far_block, y_extent)
    far_field = far_field.transpose(1, 3, 0, 2).reshape(z_extent, y_extent, half)
    spectrum = jnp.concatenate([near_field, far_field], axis=2)
    field_dd = jnp.einsum("zyk,kx->zyx", spectrum, fine_matrix, precision=HIGH)
    damped = jnp.exp(-TIME_STEP * (potential_fine + CONTACT * density + field_dd)) * evolved
    total = jnp.sum(damped * damped)
    for axis in ("rows", "cols"):
        (sums,) = exchange((jnp.full((sizes[axis], 8, 128), total, jnp.float32), axis))
        total = jnp.sum(sums[:, 0, 0])
    return damped * lax.rsqrt(total / float(nf) ** 3 + EPSILON)


def slab_of(row, col, rows, cols):
    half = row // (rows // 2)
    pair = col // 2
    other = lax.rem(col + pair, 2)
    far = half + other - 2 * half * other
    return (cols // 2) * (far * (rows // 2) + lax.rem(row, rows // 2)) + pair


def peers_of(kind, row, col, rows, cols):
    me = row * cols + col
    middle = rows // 2
    order = [(a, b) for a in range(rows) for b in range(cols)]
    order.sort(key=lambda step: (step == (0, 0), abs(2 * step[0] - rows)))
    peers = []
    if kind == "all":
        for a, b in order:
            r, c = lax.rem(row + a, rows), lax.rem(col + b, cols)
            peers.append((r * cols + c, me, r, c))
    elif kind == "both":
        for a, b in order:
            r, c = lax.rem(row + a, rows), lax.rem(col + b, cols)
            peers.append((slab_of(r, c, rows, cols), me, r, c))
    elif kind == "half":
        base = row // middle * middle
        mine = slab_of(row, col, rows, cols)
        order = [(a, b) for a in range(middle) for b in range(cols)]
        order.sort(key=lambda step: (step == (0, 0), abs(2 * step[0] - middle)))
        for a, b in order:
            r, c = lax.rem(lax.rem(row, middle) + a, middle), lax.rem(col + b, cols)
            peers.append((r * cols + c, mine, base + r, c))
    elif kind == "cols":
        for b in list(range(1, cols)) + [0]:
            c = lax.rem(col + b, cols)
            peers.append((c, col, row, c))
    return peers


def swap_kernel(kinds, sizes, *refs):
    count = len(kinds)
    sources, targets = refs[:count], refs[count : 2 * count]
    send_sems, recv_sems, local_sems = refs[2 * count :]
    row, col = lax.axis_index("rows"), lax.axis_index("cols")
    rows, cols = sizes["rows"], sizes["cols"]
    lists = [peers_of(kind, row, col, rows, cols) for kind in kinds]

    barrier = pltpu.get_barrier_semaphore()
    widest = max(lists, key=len)
    for _, _, r, c in widest[:-1]:
        pl.semaphore_signal(barrier, inc=1, device_id=(r, c), device_id_type=MESH)
    pl.semaphore_wait(barrier, len(widest) - 1)
    copies = []
    for index, peers in enumerate(lists):
        for step, (source, target, r, c) in enumerate(peers[:-1]):
            copy = pltpu.make_async_remote_copy(
                src_ref=sources[index].at[source],
                dst_ref=targets[index].at[target],
                send_sem=send_sems.at[index, step],
                recv_sem=recv_sems.at[index, step],
                device_id=(r, c),
                device_id_type=MESH,
            )
            copy.start()
            copies.append(copy)
        source, target, _, _ = peers[-1]
        copy = pltpu.make_async_copy(
            sources[index].at[source], targets[index].at[target], local_sems.at[index]
        )
        copy.start()
        copies.append(copy)
    for copy in copies:
        copy.wait()


def swap(exchange, *pairs):
    arrays = [array for array, _ in pairs]
    kinds = tuple(kind for _, kind in pairs)
    count = len(arrays)
    rows, cols = exchange.sizes["rows"], exchange.sizes["cols"]
    slots = {"all": rows * cols, "both": rows * cols, "half": rows * cols // 2, "cols": cols}
    exchange.calls += 1
    return pl.pallas_call(
        functools.partial(swap_kernel, kinds, exchange.sizes),
        out_shape=[
            jax.ShapeDtypeStruct((slots[kind],) + a.shape[1:], a.dtype) for a, kind in pairs
        ],
        in_specs=[pl.BlockSpec(memory_space=pl.ANY)] * count,
        out_specs=[pl.BlockSpec(memory_space=pl.ANY)] * count,
        scratch_shapes=[
            pltpu.SemaphoreType.DMA((count, rows * cols)),
            pltpu.SemaphoreType.DMA((count, rows * cols)),
            pltpu.SemaphoreType.DMA((count,)),
        ],
        compiler_params=pltpu.CompilerParams(
            collective_id=exchange.calls - 1, has_side_effects=True
        ),
        name=f"swap_{exchange.calls - 1}",
    )(*arrays)


def split(matrix):
    high = lax.reduce_precision(matrix, 8, 7)
    return jnp.stack([high, matrix - high]).astype(jnp.bfloat16)


def pair_of(ref, *index):
    return ref[(*index, 0)], ref[(*index, 1)]


def product_with(left, right, contract):
    def product(a, b):
        return lax.dot_general(a, b, (contract, ((), ())), preferred_element_type=jnp.float32)

    return product(left[0], right[0]) + (product(left[0], right[1]) + product(left[1], right[0]))


def fine_kernel(sizes, volume, *refs):
    slab, given, lift, near, cas, spread, rolled, sq_k, sq_y, sq_z = refs[:10]
    packed, taken = refs[10:12]
    rows_of_slab, planes, sent, got, stage, turned, packing = refs[12:19]
    load_sem, send_sem, recv_sem, out_sem, in_sem, own_sem = refs[19:25]
    give_sem, take_sem = refs[25:27]
    rows, cols = sizes["rows"], sizes["cols"]
    row, col = lax.axis_index("rows"), lax.axis_index("cols")
    me, middle = row * cols + col, rows // 2
    base, local = row // middle * middle, lax.rem(row, middle)
    mine = slab_of(row, col, rows, cols)
    slabs = middle * cols
    kb, nf = got.shape[0], got.shape[1]
    yf = nf // slabs
    steps, rounds = rows_of_slab.shape[0], packed.shape[1]
    part, width = yf // steps, kb // rounds
    pair = col // 2
    gives = lax.rem(col + pair, 2) == 0

    def load(t):
        return pltpu.make_async_copy(
            slab.at[pl.ds(t * part, part)], rows_of_slab.at[t], load_sem.at[t]
        )

    for t in range(steps):
        load(t).start()

    barrier = pltpu.get_barrier_semaphore()

    def greet(step, carry):
        peer = lax.rem(me + step, rows * cols)
        pl.semaphore_signal(
            barrier, inc=1, device_id=(peer // cols, lax.rem(peer, cols)), device_id_type=MESH
        )
        return carry

    lax.fori_loop(1, rows * cols, greet, 0)

    def forward(chunk, t, step):
        r = lax.rem(local + step // cols, middle)
        c = lax.rem(col + lax.rem(step, cols), cols)
        first = (r * cols + c) * kb + chunk * width
        at = pl.multiple_of(mine * yf + t * part, 8)
        return pltpu.make_async_remote_copy(
            src_ref=sent.at[pl.ds(first, width), pl.ds(pl.multiple_of(t * part, 8), part)],
            dst_ref=got.at[pl.ds(chunk * width, width), pl.ds(at, part)],
            send_sem=send_sem.at[chunk, t, step],
            recv_sem=recv_sem.at[chunk, t, step],
            device_id=(base + r, c),
            device_id_type=MESH,
        )

    def launch(chunk, t):
        def start(step, carry):
            forward(chunk, t, step).start()
            return carry

        lax.fori_loop(1, slabs, start, 0)
        first = (local * cols + col) * kb + chunk * width
        at = pl.multiple_of(mine * yf + t * part, 8)
        got[pl.ds(chunk * width, width), pl.ds(at, part), :] = sent[
            pl.ds(first, width), pl.ds(pl.multiple_of(t * part, 8), part), :
        ]

    def front(t, carry):
        load(t).wait()

        def line(y, carry):
            field = product_with(pair_of(lift), halves(rows_of_slab[t, y]), ((1,), (0,)))
            density = halves(field * field)
            along_x = product_with(pair_of(near), density, ((1,), (0,)))
            planes[y] = product_with(halves(along_x), pair_of(cas), ((1,), (0,)))
            return carry

        lax.fori_loop(0, part, line, 0)
        place = pl.ds(pl.multiple_of(t * part, 8), part)
        sent[:, place, :] = jnp.transpose(planes[...], (1, 0, 2))

        @pl.when(t == 0)
        def _():
            pl.semaphore_wait(barrier, rows * cols - 1)

        launch(0, t)
        return carry

    lax.fori_loop(0, steps, front, 0)

    def later(index, carry):
        launch(1 + index // steps, lax.rem(index, steps))
        return carry

    lax.fori_loop(0, (rounds - 1) * steps, later, 0)

    def give(step):
        c = lax.rem(col + step, cols)
        return pltpu.make_async_remote_copy(
            src_ref=given.at[c],
            dst_ref=taken.at[pair],
            send_sem=give_sem.at[step],
            recv_sem=take_sem.at[pair],
            device_id=(row, c),
            device_id_type=MESH,
        )

    def keep():
        return pltpu.make_async_copy(given.at[col], taken.at[pair], give_sem.at[0])

    @pl.when(gives)
    def _():
        for step in range(1, cols):
            give(step).start()
        keep().start()

    def inverse(chunk, r, c):
        return pltpu.make_async_remote_copy(
            src_ref=packing.at[r, c, chunk],
            dst_ref=packed.at[me, chunk],
            send_sem=out_sem.at[chunk, r, c],
            recv_sem=in_sem.at[chunk, me],
            device_id=(r, c),
            device_id_type=MESH,
        )

    def stay(chunk):
        return pltpu.make_async_copy(
            packing.at[row, col, chunk], packed.at[me, chunk], own_sem.at[chunk]
        )

    zi = turned.shape[3] // 2
    yo = nf // rows

    def convolve(chunk, carry):
        def arrive(index, carry):
            t, step = index // slabs, lax.rem(index, slabs)

            @pl.when(step != 0)
            def _():
                forward(chunk, t, step).wait_recv()

            return carry

        lax.fori_loop(0, steps * slabs, arrive, 0)

        def couple(kp, carry):
            parts = []
            for b in range(2):
                k = chunk * width + 2 * kp + b
                values = product_with(pair_of(cas), halves(got[k]), ((1,), (0,)))
                squares = (sq_k[k] + sq_y[...]) + sq_z[...]
                nonzero = jnp.where(squares > 0, squares, 1.0)
                weights = jnp.where(
                    squares > 0, DIPOLE_STRENGTH * (3.0 * sq_z[...] - squares) / nonzero, 0.0
                )
                values = halves(values * (weights / volume))
                along_z = product_with(pair_of(spread, b), values, ((1,), (1,)))
                parts.append(along_z.reshape(rows, cols, -1, nf))
            turned[:, :, kp] = jnp.concatenate(
                [parts[0][:, :, :-8], parts[0][:, :, -8:] + parts[1][:, :, :8], parts[1][:, :, 8:]],
                axis=2,
            )
            return carry

        lax.fori_loop(0, width // 2, couple, 0)

        def roll(j, carry):
            block = turned[j].reshape(-1, nf)
            stage[j] = product_with(halves(block), pair_of(rolled, j), ((1,), (0,)))
            return carry

        lax.fori_loop(0, rows, roll, 0)

        def pack(index, carry):
            step = lax.rem(index + middle, rows)
            r = lax.rem(row + step, rows)
            for tile in range(nf // 128):
                lanes = lax.broadcasted_iota(jnp.int32, (1, 128), 1) + 128 * tile
                first, last = 128 * tile // yo, (128 * tile + 127) // yo
                value = None
                for p in range(last, first - 1, -1):
                    j = lax.rem(p - r + rows, rows)
                    block = stage[j, :, 128 * tile : 128 * tile + 128]
                    value = block if value is None else jnp.where(lanes < (p + 1) * yo, block, value)
                value = value.reshape(cols, width // 2, 2 * zi, 128)
                for c in range(cols):
                    packing[r, c, chunk, :, tile] = value[c]
            for b in range(cols - 1, -1, -1):
                c = lax.rem(col + b, cols)
                if b:
                    inverse(chunk, r, c).start()
                else:

                    @pl.when(step != 0)
                    def _():
                        inverse(chunk, r, c).start()

                    @pl.when(step == 0)
                    def _():
                        stay(chunk).start()

            return carry

        lax.fori_loop(0, rows, pack, 0)
        return carry

    lax.fori_loop(0, rounds, convolve, 0)

    def finish(chunk, carry):
        stay(chunk).wait()

        def one(source, carry):
            @pl.when(source != me)
            def _():
                r, c = source // cols, lax.rem(source, cols)
                pltpu.make_async_remote_copy(
                    src_ref=packing.at[r, c, chunk],
                    dst_ref=packed.at[source, chunk],
                    send_sem=out_sem.at[chunk, r, c],
                    recv_sem=in_sem.at[chunk, source],
                    device_id=(r, c),
                    device_id_type=MESH,
                ).wait()

            return carry

        lax.fori_loop(0, rows * cols, one, 0)

        def left(index, carry):
            t, step = index // slabs, lax.rem(index, slabs)

            @pl.when(step != 0)
            def _():
                forward(chunk, t, step).wait_send()

            return carry

        lax.fori_loop(0, steps * slabs, left, 0)
        return carry

    lax.fori_loop(0, rounds, finish, 0)

    @pl.when(gives)
    def _():
        for step in range(1, cols):
            give(step).wait_send()
        keep().wait()

    for e in range(cols // 2):
        source = 2 * e + e % 2

        @pl.when(col != source)
        def _():
            pltpu.make_async_remote_copy(
                src_ref=given.at[col],
                dst_ref=taken.at[e],
                send_sem=give_sem.at[0],
                recv_sem=take_sem.at[e],
                device_id=(row, source),
                device_id_type=MESH,
            ).wait_recv()


def out_kernel(sizes, packed, cas, lift, taken, trap, damped, total, fields):
    i = pl.program_id(0)
    rows = sizes["rows"]
    row = lax.axis_index("rows")
    zi, nf = pl.num_programs(0), cas.shape[1]
    halved = taken.shape[3]
    for e in range(taken.shape[0]):
        block = halves(taken[e, :, 0].reshape(rows * halved, nf))
        block = product_with(block, pair_of(lift, i // (zi // 2)), ((1,), (0,)))
        fields[:, e * halved : (e + 1) * halved, :] = block.reshape(rows, halved, nf)
    tiles = nf // 128
    run = tiles * 2 * zi
    columns = []
    for tile in range(tiles):
        pieces = [
            packed[pl.ds(tile * 2 * zi + b * zi + i, nf // 2, stride=run), :] for b in range(2)
        ]
        columns.append(jnp.concatenate(pieces, axis=0))
    values = halves(jnp.concatenate(columns, axis=1))
    field_dd = product_with(values, pair_of(cas), ((0,), (0,)))
    yo = nf // rows
    squares = jnp.zeros((8, nf), jnp.float32)
    for p in range(rows):
        j = lax.rem(p - row + rows, rows)
        evolved = fields[j]
        exponent = trap[j, 0] + CONTACT * (evolved * evolved) + field_dd[p * yo : (p + 1) * yo]
        result = jnp.exp(-TIME_STEP * exponent) * evolved
        damped[j, 0] = result
        squares += jnp.sum((result * result).reshape(yo // 8, 8, nf), axis=0)

    @pl.when(i == 0)
    def _():
        total[...] = squares

    @pl.when(i > 0)
    def _():
        total[...] += squares


def fine_step(exchange, slab, given, lift, potential, half, me):
    sizes = exchange.sizes
    rows, cols = sizes["rows"], sizes["cols"]
    devices = rows * cols
    yf, nc, nf = slab.shape
    slabs, kb = nf // yf, nf // devices
    yo, zo = nf // rows, nf // cols
    zi = zo // rows
    steps, rounds = yf // 8, kb // 4
    width, tiles = kb // rounds, nf // 128
    fine_matrix = cas_matrix(nf)
    near = lax.dynamic_slice_in_dim(fine_matrix, half * (nf // 2), nf // 2, 0)
    order = fine_matrix.reshape(cols, rows, zi, nf).transpose(1, 0, 2, 3)
    spread = [
        split(jnp.pad(order, ((0, 0), (0, 0), pads, (0, 0))).reshape(-1, nf))
        for pads in ((0, -zi % 8), (-zi % 8, 0))
    ]
    rolled = jnp.stack([split(jnp.roll(fine_matrix, yo * j, axis=1)) for j in range(rows)])
    every = wavenumbers(nf, nf, 0, 1.0) ** 2
    operands = [
        slab,
        given,
        split(lift.T),
        split(near),
        split(fine_matrix),
        jnp.stack(spread),
        rolled,
        (wavenumbers(nf, kb, me * kb, 1.0) ** 2)[:, None, None],
        every[:, None],
        every[None, :],
    ]
    exchange.calls += 1
    vmem, hbm = pl.BlockSpec(memory_space=pltpu.VMEM), pl.BlockSpec(memory_space=pl.ANY)
    f32 = jnp.float32
    packed, taken = pl.pallas_call(
        functools.partial(fine_kernel, sizes, float(nf) ** 3),
        out_shape=[
            jax.ShapeDtypeStruct((devices, rounds, width // 2, tiles, 2 * zi, 128), f32),
            jax.ShapeDtypeStruct((cols // 2,) + given.shape[1:], f32),
        ],
        in_specs=[hbm, hbm] + [vmem] * (len(operands) - 2),
        out_specs=[hbm, hbm],
        scratch_shapes=[
            pltpu.VMEM((steps, yf // steps, nc, nf), f32),
            pltpu.VMEM((yf // steps, nf // 2, nf), f32),
            pltpu.VMEM((nf // 2, yf, nf), f32),
            pltpu.VMEM((kb, nf, nf), f32),
            pltpu.VMEM((rows, cols * width * zi, nf), f32),
            pltpu.VMEM((rows, cols, width // 2, 2 * zi, nf), f32),
            pltpu.VMEM((rows, cols, rounds, width // 2, tiles, 2 * zi, 128), f32),
            pltpu.SemaphoreType.DMA((steps,)),
            pltpu.SemaphoreType.DMA((rounds, steps, slabs)),
            pltpu.SemaphoreType.DMA((rounds, steps, slabs)),
            pltpu.SemaphoreType.DMA((rounds, rows, cols)),
            pltpu.SemaphoreType.DMA((rounds, devices)),
            pltpu.SemaphoreType.DMA((rounds,)),
            pltpu.SemaphoreType.DMA((cols,)),
            pltpu.SemaphoreType.DMA((cols // 2,)),
        ],
        compiler_params=pltpu.CompilerParams(
            collective_id=exchange.calls - 1,
            has_side_effects=True,
            vmem_limit_bytes=60 * 1024 * 1024,
        ),
        name=f"fine_{exchange.calls - 1}",
    )(*operands)

    zeros = jnp.zeros_like(lift)
    lifts = jnp.stack(
        [split(jnp.concatenate([lift, zeros])), split(jnp.concatenate([zeros, lift]))]
    )
    cas = split(jnp.concatenate([fine_matrix[0::2], fine_matrix[1::2]]))
    block = pl.BlockSpec((rows, 1, yo, nf), lambda i: (0, i, 0, 0))
    damped, total = pl.pallas_call(
        functools.partial(out_kernel, sizes),
        grid=(zi,),
        in_specs=[
            vmem,
            vmem,
            vmem,
            pl.BlockSpec(
                (cols // 2, rows, 1, yf, nf), lambda i: (0, 0, lax.rem(i, zi // 2), 0, 0)
            ),
            block,
        ],
        out_specs=[block, pl.BlockSpec((8, nf), lambda i: (0, 0))],
        out_shape=[
            jax.ShapeDtypeStruct((rows, zi, yo, nf), f32),
            jax.ShapeDtypeStruct((8, nf), f32),
        ],
        scratch_shapes=[pltpu.VMEM((rows, yo, nf), f32)],
        compiler_params=pltpu.CompilerParams(vmem_limit_bytes=60 * 1024 * 1024),
        name="damp",
    )(
        packed.reshape(-1, 128),
        cas,
        lifts,
        taken.reshape(cols // 2, rows, zi // 2, yf, nf),
        potential.reshape(rows, zi, yo, nf),
    )
    return damped.reshape(zo, yo, nf), jnp.sum(total)


def along(values, matrix, spec):
    return jnp.einsum(spec, values, matrix, precision=HIGH)


def per_device(sizes, wave_coarse, potential_coarse, potential_fine):
    row, col = lax.axis_index("rows"), lax.axis_index("cols")
    rows, cols = sizes["rows"], sizes["cols"]
    devices, middle = rows * cols, rows // 2
    me, half = row * cols + col, row // middle
    nc, nf = wave_coarse.shape[2], potential_fine.shape[2]
    exchange = Exchanger(sizes)

    coarse_matrix = cas_matrix(nc)
    fine_matrix = cas_matrix(nf)
    decay = jnp.exp(-0.5 * TIME_STEP * wavenumbers(nc, nc, 0, 2.0) ** 2)[:, None] / nc
    evolve = jnp.dot(coarse_matrix, decay * coarse_matrix, precision=HIGHEST)
    lift = jnp.dot(coarse_matrix, decay * lift_matrix(nc), precision=HIGHEST)

    xb, yb, zb = nc // rows, nc // cols, nc // devices
    wave = along(wave_coarse, evolve, "xyz,zk->kxy").reshape(devices, -1, 128)
    trap = potential_coarse.transpose(2, 0, 1).reshape(devices, -1, 128)
    wave, trap = swap(exchange, (wave, "all"), (trap, "all"))

    def planes_of(got):
        got = got.reshape(rows, cols, zb, xb, yb).transpose(2, 0, 3, 1, 4)
        return got.reshape(zb, nc, nc)

    wave, trap = planes_of(wave), planes_of(trap)
    evolved = along(along(wave, evolve, "zxy,xk->zky"), evolve, "zky,yl->zkl")
    density = evolved * evolved
    spectrum = along(along(density, coarse_matrix, "zxy,xk->zky"), coarse_matrix, "zky,yl->zkl")
    sent = spectrum.reshape(zb, devices, zb, nc).transpose(1, 0, 2, 3).reshape(devices, -1, 128)
    (got,) = swap(exchange, (sent, "all"))
    got = along(got.reshape(nc, zb, nc), coarse_matrix, "zkl,zm->mkl")
    got = got * dipolar_weights(
        wavenumbers(nc, zb, me * zb, 2.0)[None, :, None] ** 2,
        wavenumbers(nc, nc, 0, 2.0)[None, None, :] ** 2,
        wavenumbers(nc, nc, 0, 2.0)[:, None, None] ** 2,
        nc,
    )
    got = along(along(got, coarse_matrix, "zkl,zm->mkl"), coarse_matrix, "zkl,ly->zky")
    (got,) = swap(exchange, (got.reshape(devices, -1, 128), "all"))
    got = got.reshape(devices, zb, zb, nc).transpose(1, 0, 2, 3).reshape(zb, nc, nc)
    field_dd = along(got, coarse_matrix, "zky,kx->zxy")
    damped = jnp.exp(-TIME_STEP * (trap + CONTACT * density + field_dd)) * evolved
    partial_sum = jnp.sum(damped * damped)

    slabs, yf, kb = devices // 2, nf // (devices // 2), nf // devices
    lifted = along(damped, lift, "zxy,yk->kzx").reshape(slabs, yf, zb, nc)
    lifted = lifted.transpose(0, 2, 1, 3).reshape(slabs, -1, 128)
    got, sums = swap(
        exchange,
        (lifted, "both"),
        (jnp.full((slabs, 8, 128), partial_sum, jnp.float32), "both"),
    )
    scale = lax.rsqrt(jnp.sum(sums[:, 0, 0]) / float(nc) ** 3 + EPSILON)
    got = got.reshape(nc, yf, nc)
    slab = along(got, lift, "zyx,zk->yxk") * scale
    zo = nf // cols
    zi = zo // rows
    order = lift.reshape(nc, cols, rows, 2, zi // 2).transpose(0, 3, 1, 2, 4).reshape(nc, nf)
    given = along(got, order, "zyx,zk->kyx") * scale
    given = jnp.concatenate([given[: nf // 2], given[nf // 2 :]], axis=2)
    given = given.reshape(cols, rows * zi // 2, yf, 2 * nc)
    damped, total = fine_step(exchange, slab, given, lift, potential_fine, half, me)
    total = jnp.full((devices, 8, 128), total, jnp.float32)
    (sums,) = swap(exchange, (total, "all"))
    return damped * lax.rsqrt(jnp.sum(sums[:, 0, 0]) / float(nf) ** 3 + EPSILON)


def fits_slabs(sizes, nc, nf):
    rows, cols = sizes["rows"], sizes["cols"]
    devices = rows * cols
    if rows % 2 or cols % 2 or nc % devices or nf % (8 * devices // 2) or nf % (4 * devices):
        return False
    return nf % (8 * rows) == 0 and nf % 128 == 0 and nf // devices % 8 == 4 and 2 * nc == nf


def solution(mesh):
    sizes = {"rows": mesh.shape["rows"], "cols": mesh.shape["cols"]}
    placed = (P("rows", "cols", None), P("rows", "cols", None), P("cols", "rows", None))

    def run(wave_coarse, potential_coarse, potential_fine):
        nc, nf = wave_coarse.shape[0], potential_fine.shape[0]
        body = per_device if fits_slabs(sizes, nc, nf) else per_device_pencils
        return jax.shard_map(
            functools.partial(body, sizes),
            mesh=mesh,
            in_specs=placed,
            out_specs=P("cols", "rows", None),
            check_vma=False,
        )(wave_coarse, potential_coarse, potential_fine)

    return run
```

```python
import functools
import math

import jax
import jax.numpy as jnp
import ml_dtypes
import numpy as np
from jax import lax
from jax.experimental import pallas as pl
from jax.experimental.pallas import tpu as pltpu
from jax.sharding import PartitionSpec as P

TIME_STEP = 0.5
CONTACT = 0.4
DIPOLE_STRENGTH = 0.3
EPSILON = 1e-06
HIGH = lax.Precision.HIGH
HIGHEST = lax.Precision.HIGHEST
MESH = pl.DeviceIdType.MESH


def cas_values(product, length):
    phases = 2.0 * math.pi / length * (product % length).astype(jnp.float32)
    return jnp.cos(phases) + jnp.sin(phases)


def cas_matrix(length):
    positions = jnp.arange(length, dtype=jnp.int32)
    return cas_values(positions[:, None] * positions[None, :], length)


def lift_matrix(length):
    positions = jnp.arange(length, dtype=jnp.int32)
    lifted = jnp.where(positions < length // 2, positions, positions + length)
    fine_points = jnp.arange(2 * length, dtype=jnp.int32)
    return cas_values(lifted[:, None] * fine_points[None, :], 2 * length)


def wavenumbers(length, block_count, offset, spacing):
    positions = offset + jnp.arange(block_count, dtype=jnp.int32)
    signed = jnp.where(positions < length // 2, positions, positions - length)
    return 2.0 * math.pi / (length * spacing) * signed.astype(jnp.float32)


def dipolar_weights(along_x, along_y, along_z, length):
    squares = along_x + along_y + along_z
    nonzero = jnp.where(squares > 0, squares, 1.0)
    weights = jnp.where(squares > 0, DIPOLE_STRENGTH * (3.0 * along_z - squares) / nonzero, 0.0)
    return weights / float(length) ** 3


def exchange_kernel(axes, sizes, *refs):
    count = len(axes)
    sources, targets = refs[:count], refs[count : 2 * count]
    send_sems, recv_sems, local_sems = refs[2 * count :]
    row, col = lax.axis_index("rows"), lax.axis_index("cols")

    def place(axis, index):
        return (index, col) if axis == "rows" else (row, index)

    barrier = pltpu.get_barrier_semaphore()
    waits = 0
    for axis in sorted(set(axes)):
        size = sizes[axis]
        me = lax.axis_index(axis)
        for step in range(1, size):
            peer = lax.rem(me + step, size)
            pl.semaphore_signal(barrier, inc=1, device_id=place(axis, peer), device_id_type=MESH)
        waits += size - 1
    pl.semaphore_wait(barrier, waits)
    most = max(sizes[axis] for axis in axes)
    order = sorted(range(1, most), key=lambda step: abs(2 * step - most))
    copies = []
    for step in order:
        for index, axis in enumerate(axes):
            size = sizes[axis]
            if step >= size:
                continue
            me = lax.axis_index(axis)
            peer = lax.rem(me + step, size)
            copy = pltpu.make_async_remote_copy(
                src_ref=sources[index].at[peer],
                dst_ref=targets[index].at[me],
                send_sem=send_sems.at[index, step],
                recv_sem=recv_sems.at[index, step],
                device_id=place(axis, peer),
                device_id_type=MESH,
            )
            copy.start()
            copies.append(copy)
    for index, axis in enumerate(axes):
        me = lax.axis_index(axis)
        copy = pltpu.make_async_copy(
            sources[index].at[me], targets[index].at[me], local_sems.at[index]
        )
        copy.start()
        copies.append(copy)
    for copy in copies:
        copy.wait()


class Exchanger:
    def __init__(self, sizes):
        self.sizes = sizes
        self.calls = 0

    def __call__(self, *pairs):
        arrays = [array for array, _ in pairs]
        axes = tuple(axis for _, axis in pairs)
        most = max(self.sizes.values())
        count = len(arrays)
        self.calls += 1
        return pl.pallas_call(
            functools.partial(exchange_kernel, axes, self.sizes),
            out_shape=[jax.ShapeDtypeStruct(a.shape, a.dtype) for a in arrays],
            in_specs=[pl.BlockSpec(memory_space=pl.ANY)] * count,
            out_specs=[pl.BlockSpec(memory_space=pl.ANY)] * count,
            scratch_shapes=[
                pltpu.SemaphoreType.DMA((count, most)),
                pltpu.SemaphoreType.DMA((count, most)),
                pltpu.SemaphoreType.DMA((count,)),
            ],
            compiler_params=pltpu.CompilerParams(
                collective_id=self.calls - 1, has_side_effects=True
            ),
            name=f"exchange_{self.calls - 1}",
        )(*arrays)


def give(values, matrix, parts, precision=HIGH):
    if matrix is None:
        turned = jnp.transpose(values, (2, 0, 1))
    else:
        turned = jnp.einsum("abl,lk->kab", values, matrix, precision=precision)
    length, rows_extent, cols_extent = turned.shape
    return turned.reshape(parts, length // parts, rows_extent * cols_extent)


def take(received, axis, rows_extent):
    parts, block, area = received.shape
    cols_extent = area // rows_extent
    received = received.reshape(parts, block, rows_extent, cols_extent)
    if axis == "cols":
        return received.transpose(2, 1, 0, 3).reshape(rows_extent, block, parts * cols_extent)
    return received.transpose(1, 3, 0, 2).reshape(block, cols_extent, parts * rows_extent)


def apply(values, matrix, precision=HIGH):
    return jnp.einsum("abl,lk->abk", values, matrix, precision=precision)


def split_product(values, matrix):
    high = matrix.astype(jnp.bfloat16)
    low = (matrix - high.astype(jnp.float32)).astype(jnp.bfloat16)
    top = values.astype(jnp.bfloat16)
    rest = (values - top.astype(jnp.float32)).astype(jnp.bfloat16)
    product = functools.partial(jnp.dot, preferred_element_type=jnp.float32)
    return product(top, high) + (product(top, low) + product(rest, high))


def gather_pieces(received, held):
    parts, chunk = received.shape[0], held.shape[0]
    width = received.shape[2] // chunk
    for s in range(chunk):
        for p in range(parts):
            held[s, :, p * width : (p + 1) * width] = received[p, :, s * width : (s + 1) * width]


def scatter_pieces(held, sent):
    parts, chunk = sent.shape[0], held.shape[0]
    width = sent.shape[2] // chunk
    for s in range(chunk):
        for p in range(parts):
            sent[p, :, s * width : (s + 1) * width] = held[s, :, p * width : (p + 1) * width]


def assemble_kernel(received, matrix, out, held):
    gather_pieces(received, held)
    chunk, k, length = held.shape
    product = split_product(held[...].reshape(chunk * k, length), matrix[...])
    out[...] = product.reshape(out.shape)


def chunk_of(spectators, width, k):
    for chunk in range(1, spectators):
        if spectators % chunk == 0 and chunk * width % 128 == 0 and chunk * k >= 256:
            return chunk
    return spectators


def assemble(received, spectators, matrix):
    parts, k, area = received.shape
    chunk = chunk_of(spectators, area // spectators, k)
    length, points = matrix.shape
    if k % 8:
        held = received.reshape(parts, k, spectators, -1).transpose(2, 1, 0, 3)
        return apply(held.reshape(spectators, k, length), matrix)
    return pl.pallas_call(
        assemble_kernel,
        grid=(spectators // chunk,),
        in_specs=[
            pl.BlockSpec((parts, k, area // spectators * chunk), lambda i: (0, 0, i)),
            pl.BlockSpec((length, points), lambda i: (0, 0)),
        ],
        out_specs=pl.BlockSpec((chunk, k, points), lambda i: (i, 0, 0)),
        out_shape=jax.ShapeDtypeStruct((spectators, k, points), jnp.float32),
        scratch_shapes=[pltpu.VMEM((chunk, k, length), jnp.float32)],
    )(received, matrix)


def halves(values):
    high = values.astype(jnp.bfloat16)
    return high, (values - high.astype(jnp.float32)).astype(jnp.bfloat16)


def product_of(left, right):
    product = functools.partial(jnp.dot, preferred_element_type=jnp.float32)
    return product(left[0], right[0]) + (product(left[0], right[1]) + product(left[1], right[0]))


def planes_kernel(flows, sizes, chunks, volume, *refs):
    row, col = lax.axis_index("rows"), lax.axis_index("cols")

    def place(axis, index):
        return (index, col) if axis == "rows" else (row, index)

    matrix = refs[0]
    inputs = [refs[1 + 4 * i : 5 + 4 * i] for i in range(len(flows))]
    at = 1 + 4 * len(flows)
    outs = refs[at : at + len(flows)]
    at += len(flows)
    high, low = refs[at : at + 2]
    at += 2
    buffers = [refs[at + 9 * i : at + 9 * i + 9] for i in range(len(flows))]

    barrier = pltpu.get_barrier_semaphore()
    waits = 0
    for axis in sorted(set(axis for axis, _ in flows)):
        size = sizes[axis]
        me = lax.axis_index(axis)
        for step in range(1, size):
            peer = lax.rem(me + step, size)
            pl.semaphore_signal(barrier, inc=1, device_id=place(axis, peer), device_id_type=MESH)
        waits += size - 1
    high[...], low[...] = halves(matrix[...])
    pl.semaphore_wait(barrier, waits)

    def copies(flow, turn, c):
        axis, _ = flows[flow]
        size = sizes[axis]
        me = lax.axis_index(axis)
        sent, received = buffers[flow][2 * turn : 2 * turn + 2]
        send_sem, recv_sem = buffers[flow][4 + 2 * turn : 6 + 2 * turn]
        order = sorted(range(1, size), key=lambda step: abs(2 * step - size))
        for step in order:
            peer = lax.rem(me + step, size)
            yield pltpu.make_async_remote_copy(
                src_ref=sent.at[c, peer],
                dst_ref=received.at[c, me],
                send_sem=send_sem.at[c, step],
                recv_sem=recv_sem.at[c, step],
                device_id=place(axis, peer),
                device_id_type=MESH,
            )

    def launch(flow, turn, c):
        me = lax.axis_index(flows[flow][0])
        for copy in copies(flow, turn, c):
            copy.start()
        sent, received = buffers[flow][2 * turn : 2 * turn + 2]
        received[c, me] = sent[c, me]

    def lanes(area, c):
        if chunks == 1:
            return slice(None)
        return pl.ds(pl.multiple_of(c * (area // chunks), 128), area // chunks)

    def first(c, carry):
        for flow in range(len(flows)):
            source, sent = inputs[flow][0], buffers[flow][0]
            part = source[:, :, lanes(source.shape[2], c)]
            part = part.reshape(matrix.shape[0], part.shape[2])
            product = product_of((high[...], low[...]), halves(part))
            sent[c] = product.reshape(sent.shape[1:])
            launch(flow, 0, c)
        return carry

    def second(c, carry):
        for flow in range(len(flows)):
            _, sq_s, sq_k, sq_l = inputs[flow]
            vertical = flows[flow][1]
            held = buffers[flow][8]
            chunk, k, length = held.shape
            for copy in copies(flow, 0, c):
                copy.wait_recv()
            gather_pieces(buffers[flow][1].at[c], held)
            both = (high[...], low[...])
            values = product_of(halves(held[...].reshape(chunk * k, length)), both)
            parts = [sq_s[pl.ds(c * chunk, chunk)], sq_k[...][None], sq_l[...][None]]
            parts = [jnp.broadcast_to(part, held.shape) for part in parts]
            squares = parts[0] + parts[1] + parts[2]
            nonzero = jnp.where(squares > 0, squares, 1.0)
            weights = jnp.where(
                squares > 0, DIPOLE_STRENGTH * (3.0 * parts[vertical] - squares) / nonzero, 0.0
            )
            values = values * (weights / volume).reshape(chunk * k, length)
            held[...] = product_of(halves(values), both).reshape(held.shape)
            scatter_pieces(held, buffers[flow][2].at[c])
            launch(flow, 1, c)
        return carry

    def third(c, carry):
        for flow in range(len(flows)):
            for copy in copies(flow, 1, c):
                copy.wait_recv()
            received, out = buffers[flow][3], outs[flow]
            part = received[c].reshape(matrix.shape[0], received.shape[3])
            product = product_of((high[...], low[...]), halves(part))
            out[:, lanes(out.shape[1], c)] = product
            for turn in range(2):
                for copy in copies(flow, turn, c):
                    copy.wait_send()
        return carry

    for stage in (first, second, third):
        lax.fori_loop(0, chunks, stage, 0)


def planes(exchange, flows, matrix):
    sizes = exchange.sizes
    length = matrix.shape[0]
    counts = []
    for axis, _, received, sq_s, sq_k, _ in flows:
        spectators = sq_s.shape[0]
        width = received.shape[2] // spectators
        counts.append(spectators // chunk_of(spectators, width, sq_k.shape[0]))
    chunks = counts[0] if len(set(counts)) == 1 else 1
    operands, outs, scratch = [matrix], [], []
    scratch += [pltpu.VMEM((length, length), jnp.bfloat16)] * 2
    for axis, _, received, sq_s, sq_k, sq_l in flows:
        operands += [received, sq_s[:, None, None], sq_k[:, None], sq_l[None, :]]
        area, k, size = received.shape[2], sq_k.shape[0], sizes[axis]
        outs.append(jax.ShapeDtypeStruct((length, area), jnp.float32))
        scratch += [pltpu.VMEM((chunks, size, k, area // chunks), jnp.float32)] * 4
        scratch += [pltpu.SemaphoreType.DMA((chunks, size))] * 4
        scratch += [pltpu.VMEM((sq_s.shape[0] // chunks, k, length), jnp.float32)]
    exchange.calls += 1
    vmem = pl.BlockSpec(memory_space=pltpu.VMEM)
    return pl.pallas_call(
        functools.partial(
            planes_kernel,
            tuple((flow[0], flow[1]) for flow in flows),
            sizes,
            chunks,
            float(length) ** 3,
        ),
        out_shape=outs,
        in_specs=[vmem] * len(operands),
        out_specs=[vmem] * len(outs),
        scratch_shapes=scratch,
        compiler_params=pltpu.CompilerParams(
            collective_id=exchange.calls - 1,
            has_side_effects=True,
            vmem_limit_bytes=60 * 1024 * 1024,
        ),
        name=f"planes_{exchange.calls - 1}",
    )(*operands)


def blocks(turned, parts):
    first, length, last = turned.shape
    turned = turned.reshape(first, parts, length // parts, last).transpose(1, 0, 2, 3)
    return turned.reshape(parts, first, length // parts * last)


def product_blocks(matrix, received, parts):
    turned = jnp.dot(matrix, received.reshape(-1, received.shape[2]), precision=HIGH)
    return turned.reshape(parts, turned.shape[0] // parts, turned.shape[1])


def per_device_pencils(sizes, wave_coarse, potential_coarse, potential_fine):
    row, col = lax.axis_index("rows"), lax.axis_index("cols")
    rows, cols = sizes["rows"], sizes["cols"]
    nc, nf = wave_coarse.shape[2], potential_fine.shape[2]
    exchange = Exchanger(sizes)

    coarse_matrix = cas_matrix(nc)
    fine_matrix = cas_matrix(nf)
    decay = jnp.exp(-0.5 * TIME_STEP * wavenumbers(nc, nc, 0, 2.0) ** 2)[:, None] / nc
    evolve = jnp.dot(coarse_matrix, decay * coarse_matrix, precision=HIGHEST)
    lift = jnp.dot(coarse_matrix, decay * lift_matrix(nc), precision=HIGHEST)

    xr = yr = nc // rows
    spectators = nc // cols
    turned = jnp.einsum("xyz,zk->ykx", wave_coarse, evolve, precision=HIGH)
    (got,) = exchange((blocks(turned, cols), "cols"))
    (got,) = exchange((product_blocks(evolve.T, got, rows), "rows"))
    evolved = assemble(got, spectators, evolve)
    turned = jnp.einsum("zyx,xk->zky", evolved * evolved, coarse_matrix, precision=HIGH)
    got, back = exchange(
        (blocks(turned, cols), "cols"), (give(evolved.transpose(1, 0, 2), None, rows), "rows")
    )
    back = take(back, "rows", yr)
    got, back = exchange(
        (product_blocks(coarse_matrix, got, rows), "rows"), (give(back, None, cols), "cols")
    )
    spectrum, evolved = assemble(got, spectators, coarse_matrix), take(back, "cols", xr)
    z_block, x_block = nc // rows, nc // cols
    weights = dipolar_weights(
        wavenumbers(nc, x_block, col * x_block, 2.0)[:, None, None] ** 2,
        wavenumbers(nc, nc, 0, 2.0)[None, None, :] ** 2,
        wavenumbers(nc, z_block, row * z_block, 2.0)[None, :, None] ** 2,
        nc,
    )
    turned = jnp.einsum("xzy,yk->xkz", weights * spectrum, coarse_matrix, precision=HIGH)
    (got,) = exchange((blocks(turned, cols), "cols"))
    (got,) = exchange((product_blocks(coarse_matrix, got, rows), "rows"))
    field_dd = assemble(got, spectators, coarse_matrix).transpose(1, 0, 2)
    density = evolved * evolved
    damped = jnp.exp(-TIME_STEP * (potential_coarse + CONTACT * density + field_dd)) * evolved
    partial_sum = jnp.sum(damped * damped)

    got, sums = exchange(
        (blocks(jnp.einsum("xyz,zk->ykx", damped, lift, precision=HIGH), cols), "cols"),
        (jnp.full((cols, 8, 128), partial_sum, jnp.float32), "cols"),
    )
    partial_sum = jnp.sum(sums[:, 0, 0])
    got, sums = exchange(
        (product_blocks(lift.T, got, rows), "rows"),
        (jnp.full((rows, 8, 128), partial_sum, jnp.float32), "rows"),
    )
    scale = lax.rsqrt(jnp.sum(sums[:, 0, 0]) / float(nc) ** 3 + EPSILON)
    evolved = assemble(got, nf // cols, lift) * scale

    density = evolved * evolved
    half = nf // 2
    near, far = fine_matrix[:, :half], fine_matrix[:, half:]
    got_near, got_far = exchange(
        (blocks(jnp.einsum("zyx,xk->ykz", density, near, precision=HIGH), rows), "rows"),
        (blocks(jnp.einsum("zyx,xk->zky", density, far, precision=HIGH), cols), "cols"),
    )
    y_block, z_block = nf // cols, nf // rows
    near_block, far_block = half // rows, half // cols
    every = wavenumbers(nf, nf, 0, 1.0) ** 2
    near_flow = (
        "cols",
        2,
        got_near,
        wavenumbers(nf, near_block, row * near_block, 1.0) ** 2,
        wavenumbers(nf, y_block, col * y_block, 1.0) ** 2,
        every,
    )
    far_flow = (
        "rows",
        1,
        got_far,
        wavenumbers(nf, far_block, half + col * far_block, 1.0) ** 2,
        wavenumbers(nf, z_block, row * z_block, 1.0) ** 2,
        every,
    )
    got_far, got_near = planes(exchange, (far_flow, near_flow), fine_matrix)
    got_near, got_far = exchange(
        (got_near.reshape(rows, nf // rows, -1), "rows"),
        (got_far.reshape(cols, nf // cols, -1), "cols"),
    )
    z_extent, y_extent = nf // cols, nf // rows
    near_field = got_near.reshape(rows, y_extent, near_block, z_extent)
    near_field = near_field.transpose(3, 1, 0, 2).reshape(z_extent, y_extent, half)
    far_field = got_far.reshape(cols, z_extent, far_block, y_extent)
    far_field = far_field.transpose(1, 3, 0, 2).reshape(z_extent, y_extent, half)
    spectrum = jnp.concatenate([near_field, far_field], axis=2)
    field_dd = jnp.einsum("zyk,kx->zyx", spectrum, fine_matrix, precision=HIGH)
    damped = jnp.exp(-TIME_STEP * (potential_fine + CONTACT * density + field_dd)) * evolved
    total = jnp.sum(damped * damped)
    for axis in ("rows", "cols"):
        (sums,) = exchange((jnp.full((sizes[axis], 8, 128), total, jnp.float32), axis))
        total = jnp.sum(sums[:, 0, 0])
    return damped * lax.rsqrt(total / float(nf) ** 3 + EPSILON)


def slab_of(row, col, rows, cols):
    half = row // (rows // 2)
    pair = col // 2
    other = lax.rem(col + pair, 2)
    far = half + other - 2 * half * other
    return (cols // 2) * (far * (rows // 2) + lax.rem(row, rows // 2)) + pair


def peers_of(kind, row, col, rows, cols):
    me = row * cols + col
    middle = rows // 2
    order = [(a, b) for a in range(rows) for b in range(cols)]
    order.sort(key=lambda step: (step == (0, 0), abs(2 * step[0] - rows)))
    peers = []
    if kind == "all":
        for a, b in order:
            r, c = lax.rem(row + a, rows), lax.rem(col + b, cols)
            peers.append((r * cols + c, me, r, c))
    elif kind == "both":
        for a, b in order:
            r, c = lax.rem(row + a, rows), lax.rem(col + b, cols)
            peers.append((slab_of(r, c, rows, cols), me, r, c))
    elif kind == "half":
        base = row // middle * middle
        mine = slab_of(row, col, rows, cols)
        order = [(a, b) for a in range(middle) for b in range(cols)]
        order.sort(key=lambda step: (step == (0, 0), abs(2 * step[0] - middle)))
        for a, b in order:
            r, c = lax.rem(lax.rem(row, middle) + a, middle), lax.rem(col + b, cols)
            peers.append((r * cols + c, mine, base + r, c))
    elif kind == "cols":
        for b in list(range(1, cols)) + [0]:
            c = lax.rem(col + b, cols)
            peers.append((c, col, row, c))
    return peers


def swap_kernel(kinds, sizes, *refs):
    count = len(kinds)
    sources, targets = refs[:count], refs[count : 2 * count]
    send_sems, recv_sems, local_sems = refs[2 * count :]
    row, col = lax.axis_index("rows"), lax.axis_index("cols")
    rows, cols = sizes["rows"], sizes["cols"]
    lists = [peers_of(kind, row, col, rows, cols) for kind in kinds]

    barrier = pltpu.get_barrier_semaphore()
    widest = max(lists, key=len)
    for _, _, r, c in widest[:-1]:
        pl.semaphore_signal(barrier, inc=1, device_id=(r, c), device_id_type=MESH)
    pl.semaphore_wait(barrier, len(widest) - 1)
    copies = []
    for index, peers in enumerate(lists):
        for step, (source, target, r, c) in enumerate(peers[:-1]):
            copy = pltpu.make_async_remote_copy(
                src_ref=sources[index].at[source],
                dst_ref=targets[index].at[target],
                send_sem=send_sems.at[index, step],
                recv_sem=recv_sems.at[index, step],
                device_id=(r, c),
                device_id_type=MESH,
            )
            copy.start()
            copies.append(copy)
        source, target, _, _ = peers[-1]
        copy = pltpu.make_async_copy(
            sources[index].at[source], targets[index].at[target], local_sems.at[index]
        )
        copy.start()
        copies.append(copy)
    for copy in copies:
        copy.wait()


def swap(exchange, *pairs):
    arrays = [array for array, _ in pairs]
    kinds = tuple(kind for _, kind in pairs)
    count = len(arrays)
    rows, cols = exchange.sizes["rows"], exchange.sizes["cols"]
    slots = {"all": rows * cols, "both": rows * cols, "half": rows * cols // 2, "cols": cols}
    exchange.calls += 1
    return pl.pallas_call(
        functools.partial(swap_kernel, kinds, exchange.sizes),
        out_shape=[
            jax.ShapeDtypeStruct((slots[kind],) + a.shape[1:], a.dtype) for a, kind in pairs
        ],
        in_specs=[pl.BlockSpec(memory_space=pl.ANY)] * count,
        out_specs=[pl.BlockSpec(memory_space=pl.ANY)] * count,
        scratch_shapes=[
            pltpu.SemaphoreType.DMA((count, rows * cols)),
            pltpu.SemaphoreType.DMA((count, rows * cols)),
            pltpu.SemaphoreType.DMA((count,)),
        ],
        compiler_params=pltpu.CompilerParams(
            collective_id=exchange.calls - 1, has_side_effects=True
        ),
        name=f"swap_{exchange.calls - 1}",
    )(*arrays)


def split(matrix):
    high = matrix.astype(np.float32).astype(ml_dtypes.bfloat16)
    low = (matrix - high.astype(np.float64)).astype(np.float32).astype(ml_dtypes.bfloat16)
    return np.stack([high, low])


def cas_table(rows, length):
    product = np.outer(rows, np.arange(length, dtype=np.int64)) % length
    phases = 2.0 * np.pi / length * product
    return np.cos(phases) + np.sin(phases)


def squared_waves(length, spacing):
    positions = np.arange(length)
    signed = np.where(positions < length // 2, positions, positions - length)
    return (2.0 * np.pi / (length * spacing) * signed) ** 2


def squared_wave(position, length, spacing):
    signed = jnp.where(position < length // 2, position, position - length)
    wave = signed.astype(jnp.float32) * (2.0 * math.pi / (length * spacing))
    return wave * wave


def pair_of(ref, *index):
    return ref[(*index, 0)], ref[(*index, 1)]


def product_with(left, right, contract):
    def product(a, b):
        return lax.dot_general(a, b, (contract, ((), ())), preferred_element_type=jnp.float32)

    return product(left[0], right[0]) + (product(left[0], right[1]) + product(left[1], right[0]))


def fine_kernel(sizes, volume, *refs):
    slab, scale, rise, lift, near, last, cas, spread, rolled, sq_y, sq_z = refs[:11]
    packed, taken = refs[11:13]
    raw, lines, plane, shares, given, planes, sent, got, stage, turned, packing = refs[13:24]
    load_sem, send_sem, recv_sem, out_sem, in_sem, own_sem = refs[24:30]
    give_sem, take_sem = refs[30:32]
    rows, cols = sizes["rows"], sizes["cols"]
    row, col = lax.axis_index("rows"), lax.axis_index("cols")
    me, middle = row * cols + col, rows // 2
    base, local = row // middle * middle, lax.rem(row, middle)
    mine = slab_of(row, col, rows, cols)
    slabs = middle * cols
    kb, nf = got.shape[0], got.shape[1]
    yf = nf // slabs
    steps, rounds = raw.shape[0], packed.shape[1]
    part, width = yf // steps, kb // rounds
    nc, depth = plane.shape[1], lines.shape[1]
    share = given.shape[0] // cols
    parity = row // middle
    sign = (1 - 2 * parity).astype(jnp.float32)
    pair = col // 2
    gives = lax.rem(col + pair, 2) == 0

    def load(t):
        return pltpu.make_async_copy(
            slab.at[:, pl.ds(pl.multiple_of(t * part, 8), part)], raw.at[t], load_sem.at[t]
        )

    for t in range(steps):
        load(t).start()

    barrier = pltpu.get_barrier_semaphore()

    def greet(step, carry):
        peer = lax.rem(me + step, rows * cols)
        pl.semaphore_signal(
            barrier, inc=1, device_id=(peer // cols, lax.rem(peer, cols)), device_id_type=MESH
        )
        return carry

    lax.fori_loop(1, rows * cols, greet, 0)

    def forward(chunk, t, step):
        r = lax.rem(local + step // cols, middle)
        c = lax.rem(col + lax.rem(step, cols), cols)
        first = (r * cols + c) * kb + chunk * width
        at = pl.multiple_of(mine * yf + t * part, 8)
        return pltpu.make_async_remote_copy(
            src_ref=sent.at[pl.ds(first, width), pl.ds(pl.multiple_of(t * part, 8), part)],
            dst_ref=got.at[pl.ds(chunk * width, width), pl.ds(at, part)],
            send_sem=send_sem.at[chunk, t, step],
            recv_sem=recv_sem.at[chunk, t, step],
            device_id=(base + r, c),
            device_id_type=MESH,
        )

    def launch(chunk, t):
        def start(step, carry):
            forward(chunk, t, step).start()
            return carry

        lax.fori_loop(1, slabs, start, 0)
        first = (local * cols + col) * kb + chunk * width
        at = pl.multiple_of(mine * yf + t * part, 8)
        got[pl.ds(chunk * width, width), pl.ds(at, part), :] = sent[
            pl.ds(first, width), pl.ds(pl.multiple_of(t * part, 8), part), :
        ]

    def front(t, carry):
        load(t).wait()
        lines[...] = jnp.transpose(raw[t], (1, 0, 2))

        def line(y, carry):
            for e in range(2):
                plane[e * depth : (e + 1) * depth] = lines[y, :, e * nc : (e + 1) * nc]
            high = product_with(pair_of(rise), halves(plane[...]), ((1,), (0,))) * scale[:1, :1]
            for e in range(2):
                shares[y, :, e * nc : (e + 1) * nc] = high[e * nc : (e + 1) * nc]
            field = product_with(pair_of(lift), halves(high), ((1,), (1,)))
            density = field * field
            density = halves(density[:nc] + sign * density[nc:])
            along_x = product_with(pair_of(near, parity), density, ((1,), (0,)))
            planes[y] = product_with(halves(along_x), pair_of(last), ((1,), (0,)))
            return carry

        lax.fori_loop(0, part, line, 0)
        place = pl.ds(pl.multiple_of(t * part, 8), part)
        sent[:, place, :] = jnp.transpose(planes[...], (1, 0, 2))
        given[:, place, :] = jnp.transpose(shares[...], (1, 0, 2))

        @pl.when(t == 0)
        def _():
            pl.semaphore_wait(barrier, rows * cols - 1)

        launch(0, t)
        return carry

    lax.fori_loop(0, steps, front, 0)

    def later(index, carry):
        launch(1 + index // steps, lax.rem(index, steps))
        return carry

    lax.fori_loop(0, (rounds - 1) * steps, later, 0)

    def give(step):
        c = lax.rem(col + step, cols)
        return pltpu.make_async_remote_copy(
            src_ref=given.at[pl.ds(c * share, share)],
            dst_ref=taken.at[pair],
            send_sem=give_sem.at[step],
            recv_sem=take_sem.at[pair],
            device_id=(row, c),
            device_id_type=MESH,
        )

    def keep():
        own = given.at[pl.ds(col * share, share)]
        return pltpu.make_async_copy(own, taken.at[pair], give_sem.at[0])

    @pl.when(gives)
    def _():
        for step in range(1, cols):
            give(step).start()
        keep().start()

    def inverse(chunk, r, c):
        return pltpu.make_async_remote_copy(
            src_ref=packing.at[r, c, chunk],
            dst_ref=packed.at[me, chunk],
            send_sem=out_sem.at[chunk, r, c],
            recv_sem=in_sem.at[chunk, me],
            device_id=(r, c),
            device_id_type=MESH,
        )

    def stay(chunk):
        return pltpu.make_async_copy(
            packing.at[row, col, chunk], packed.at[me, chunk], own_sem.at[chunk]
        )

    zi = turned.shape[3] // 2
    yo = nf // rows

    def convolve(chunk, carry):
        def arrive(index, carry):
            t, step = index // slabs, lax.rem(index, slabs)

            @pl.when(step != 0)
            def _():
                forward(chunk, t, step).wait_recv()

            return carry

        lax.fori_loop(0, steps * slabs, arrive, 0)

        def couple(kp, carry):
            parts = []
            for b in range(2):
                k = chunk * width + 2 * kp + b
                top, bottom = got[k, : nf // 2], got[k, nf // 2 :]
                values = jnp.concatenate(
                    [
                        product_with(pair_of(cas, 0), halves(top + bottom), ((1,), (0,))),
                        product_with(pair_of(cas, 1), halves(top - bottom), ((1,), (0,))),
                    ]
                )
                sq_x = squared_wave(2 * ((local * cols + col) * kb + k) + parity, nf, 1.0)
                squares = (sq_x + sq_y[...]) + sq_z[...]
                nonzero = jnp.where(squares > 0, squares, 1.0)
                weights = jnp.where(
                    squares > 0, DIPOLE_STRENGTH * (3.0 * sq_z[...] - squares) / nonzero, 0.0
                )
                values = halves(values * (weights / volume))
                along_z = product_with(pair_of(spread, b), values, ((1,), (1,)))
                parts.append(along_z.reshape(rows, cols, -1, nf))
            turned[:, :, kp] = jnp.concatenate(
                [parts[0][:, :, :-8], parts[0][:, :, -8:] + parts[1][:, :, :8], parts[1][:, :, 8:]],
                axis=2,
            )
            return carry

        lax.fori_loop(0, width // 2, couple, 0)

        def roll(j, carry):
            block = turned[j].reshape(-1, nf)
            stage[j] = product_with(halves(block), pair_of(rolled, j), ((1,), (0,)))
            return carry

        lax.fori_loop(0, rows, roll, 0)

        def pack(index, carry):
            step = lax.rem(index + middle, rows)
            r = lax.rem(row + step, rows)
            for tile in range(nf // 128):
                lanes = lax.broadcasted_iota(jnp.int32, (1, 128), 1) + 128 * tile
                first, last = 128 * tile // yo, (128 * tile + 127) // yo
                value = None
                for p in range(last, first - 1, -1):
                    j = lax.rem(p - r + rows, rows)
                    block = stage[j, :, 128 * tile : 128 * tile + 128]
                    value = block if value is None else jnp.where(lanes < (p + 1) * yo, block, value)
                value = value.reshape(cols, width // 2, 2 * zi, 128)
                for c in range(cols):
                    packing[r, c, chunk, :, tile] = value[c]
            for b in range(cols - 1, -1, -1):
                c = lax.rem(col + b, cols)
                if b:
                    inverse(chunk, r, c).start()
                else:

                    @pl.when(step != 0)
                    def _():
                        inverse(chunk, r, c).start()

                    @pl.when(step == 0)
                    def _():
                        stay(chunk).start()

            return carry

        lax.fori_loop(0, rows, pack, 0)
        return carry

    lax.fori_loop(0, rounds, convolve, 0)

    def finish(chunk, carry):
        stay(chunk).wait()

        def one(source, carry):
            @pl.when(source != me)
            def _():
                r, c = source // cols, lax.rem(source, cols)
                pltpu.make_async_remote_copy(
                    src_ref=packing.at[r, c, chunk],
                    dst_ref=packed.at[source, chunk],
                    send_sem=out_sem.at[chunk, r, c],
                    recv_sem=in_sem.at[chunk, source],
                    device_id=(r, c),
                    device_id_type=MESH,
                ).wait()

            return carry

        lax.fori_loop(0, rows * cols, one, 0)

        def left(index, carry):
            t, step = index // slabs, lax.rem(index, slabs)

            @pl.when(step != 0)
            def _():
                forward(chunk, t, step).wait_send()

            return carry

        lax.fori_loop(0, steps * slabs, left, 0)
        return carry

    lax.fori_loop(0, rounds, finish, 0)

    @pl.when(gives)
    def _():
        for step in range(1, cols):
            give(step).wait_send()
        keep().wait()

    for e in range(cols // 2):
        source = 2 * e + e % 2

        @pl.when(col != source)
        def _():
            pltpu.make_async_remote_copy(
                src_ref=given.at[pl.ds(col * share, share)],
                dst_ref=taken.at[e],
                send_sem=give_sem.at[0],
                recv_sem=take_sem.at[e],
                device_id=(row, source),
                device_id_type=MESH,
            ).wait_recv()


def out_kernel(sizes, packed, cas, lift, taken, trap, damped, total, fields):
    i = pl.program_id(0)
    rows = sizes["rows"]
    row = lax.axis_index("rows")
    zi, nf = pl.num_programs(0), cas.shape[1]
    halved = taken.shape[3]
    for e in range(taken.shape[0]):
        block = halves(taken[e, :, 0].reshape(rows * halved, nf))
        block = product_with(block, pair_of(lift, i // (zi // 2)), ((1,), (0,)))
        fields[:, e * halved : (e + 1) * halved, :] = block.reshape(rows, halved, nf)
    tiles = nf // 128
    run = tiles * 2 * zi
    columns = []
    for tile in range(tiles):
        pieces = [
            packed[pl.ds(tile * 2 * zi + b * zi + i, nf // 2, stride=run), :] for b in range(2)
        ]
        columns.append(jnp.concatenate(pieces, axis=0))
    values = halves(jnp.concatenate(columns, axis=1))
    field_dd = product_with(values, pair_of(cas), ((0,), (0,)))
    yo = nf // rows
    squares = jnp.zeros((8, nf), jnp.float32)
    for p in range(rows):
        j = lax.rem(p - row + rows, rows)
        evolved = fields[j]
        exponent = trap[j, 0] + CONTACT * (evolved * evolved) + field_dd[p * yo : (p + 1) * yo]
        result = jnp.exp(-TIME_STEP * exponent) * evolved
        damped[j, 0] = result
        squares += jnp.sum((result * result).reshape(yo // 8, 8, nf), axis=0)

    @pl.when(i == 0)
    def _():
        total[...] = squares

    @pl.when(i > 0)
    def _():
        total[...] += squares


def fine_step(exchange, slab, scale, lift, potential):
    sizes = exchange.sizes
    rows, cols = sizes["rows"], sizes["cols"]
    devices = rows * cols
    nc, nf = lift.shape
    depth, yf = slab.shape[:2]
    kb = nf // devices
    yo, zo = nf // rows, nf // cols
    zi = zo // rows
    steps, rounds = yf // 8, kb // 4
    width, tiles = kb // rounds, nf // 128
    natural = np.arange(nf)
    waves = np.concatenate([natural[0::2], natural[1::2]])
    fine_matrix = cas_table(natural, nf)
    order = fine_matrix.reshape(cols, rows, zi, nf).transpose(1, 0, 2, 3)
    spread = [
        split(np.pad(order, ((0, 0), (0, 0), pads, (0, 0))).reshape(-1, nf))
        for pads in ((0, -zi % 8), (-zi % 8, 0))
    ]
    rolled = np.stack([split(np.roll(fine_matrix[waves], yo * j, axis=1)) for j in range(rows)])
    slabs = nf // yf
    shape = (cols, rows, 2, zi // 2)
    rise = lift.reshape((nc // 2, 2) + shape).transpose(4, 2, 3, 5, 1, 0).reshape(nf, nc)
    last = fine_matrix.reshape(shape + (nf,)).transpose(2, 0, 1, 3, 4).reshape(nf, nf)
    every = squared_waves(nf, 1.0).astype(np.float32)
    folded = np.stack([split(fine_matrix[parity::2, : nf // 2]) for parity in range(2)])
    operands = [
        slab,
        scale,
        split(rise),
        split(lift.T),
        folded,
        split(last),
        folded,
        np.stack(spread),
        rolled,
        every[waves][:, None],
        every[None, :],
    ]
    exchange.calls += 1
    vmem, hbm = pl.BlockSpec(memory_space=pltpu.VMEM), pl.BlockSpec(memory_space=pl.ANY)
    f32 = jnp.float32
    packed, taken = pl.pallas_call(
        functools.partial(fine_kernel, sizes, float(nf) ** 3),
        out_shape=[
            jax.ShapeDtypeStruct((devices, rounds, width // 2, tiles, 2 * zi, 128), f32),
            jax.ShapeDtypeStruct((cols // 2, nc // cols, yf, nf), f32),
        ],
        in_specs=[hbm] + [vmem] * (len(operands) - 1),
        out_specs=[hbm, hbm],
        scratch_shapes=[
            pltpu.VMEM((steps, depth, yf // steps, nf), f32),
            pltpu.VMEM((yf // steps, depth, nf), f32),
            pltpu.VMEM((nc, nc), f32),
            pltpu.VMEM((yf // steps, nc, nf), f32),
            pltpu.VMEM((nc, yf, nf), f32),
            pltpu.VMEM((yf // steps, nf // 2, nf), f32),
            pltpu.VMEM((nf // 2, yf, nf), f32),
            pltpu.VMEM((kb, nf, nf), f32),
            pltpu.VMEM((rows, cols * width * zi, nf), f32),
            pltpu.VMEM((rows, cols, width // 2, 2 * zi, nf), f32),
            pltpu.VMEM((rows, cols, rounds, width // 2, tiles, 2 * zi, 128), f32),
            pltpu.SemaphoreType.DMA((steps,)),
            pltpu.SemaphoreType.DMA((rounds, steps, slabs)),
            pltpu.SemaphoreType.DMA((rounds, steps, slabs)),
            pltpu.SemaphoreType.DMA((rounds, rows, cols)),
            pltpu.SemaphoreType.DMA((rounds, devices)),
            pltpu.SemaphoreType.DMA((rounds,)),
            pltpu.SemaphoreType.DMA((cols,)),
            pltpu.SemaphoreType.DMA((cols // 2,)),
        ],
        compiler_params=pltpu.CompilerParams(
            collective_id=exchange.calls - 1,
            has_side_effects=True,
            vmem_limit_bytes=60 * 1024 * 1024,
        ),
        name=f"fine_{exchange.calls - 1}",
    )(*operands)

    zeros = np.zeros_like(lift)
    lifts = np.stack([split(np.concatenate([lift, zeros])), split(np.concatenate([zeros, lift]))])
    cas = split(fine_matrix[np.concatenate([waves[0::2], waves[1::2]])])
    block = pl.BlockSpec((rows, 1, yo, nf), lambda i: (0, i, 0, 0))
    damped, total = pl.pallas_call(
        functools.partial(out_kernel, sizes),
        grid=(zi,),
        in_specs=[
            vmem,
            vmem,
            vmem,
            pl.BlockSpec(
                (cols // 2, rows, 1, yf, nf), lambda i: (0, 0, lax.rem(i, zi // 2), 0, 0)
            ),
            block,
        ],
        out_specs=[block, pl.BlockSpec((8, nf), lambda i: (0, 0))],
        out_shape=[
            jax.ShapeDtypeStruct((rows, zi, yo, nf), f32),
            jax.ShapeDtypeStruct((8, nf), f32),
        ],
        scratch_shapes=[pltpu.VMEM((rows, yo, nf), f32)],
        compiler_params=pltpu.CompilerParams(vmem_limit_bytes=60 * 1024 * 1024),
        name="damp",
    )(
        packed.reshape(-1, 128),
        cas,
        lifts,
        taken.reshape(cols // 2, rows, zi // 2, yf, nf),
        potential.reshape(rows, zi, yo, nf),
    )
    return damped.reshape(zo, yo, nf), jnp.sum(total)


def coarse_kernel(sizes, volume, *refs):
    wave, trap, evolve, cas, deep, tall, twice, joint, lift, sq_y, sq_z = refs[:11]
    risen, scale = refs[11:13]
    column, given, taken, field, well, stack, sent, got, back, home = refs[13:23]
    folded, lifted, square, partial, partials = refs[23:28]
    send_sem, recv_sem, own_sem = refs[28:31]
    rows, cols = sizes["rows"], sizes["cols"]
    row, col = lax.axis_index("rows"), lax.axis_index("cols")
    devices, me = rows * cols, row * cols + col
    xb, yb, nc = wave.shape
    zb, nf = nc // devices, lift.shape[1]
    yf = risen.shape[1]
    pairs = zb // 2

    barrier = pltpu.get_barrier_semaphore()

    def greet(step, carry):
        peer = lax.rem(me + step, devices)
        pl.semaphore_signal(
            barrier, inc=1, device_id=(peer // cols, lax.rem(peer, cols)), device_id_type=MESH
        )
        return carry

    lax.fori_loop(1, devices, greet, 0)

    def ends(turn, device, slot):
        if turn < 2:
            return given.at[turn, device], taken.at[turn, slot]
        at, to = pl.ds(pairs * device, pairs), pl.ds(pairs * slot, pairs)
        if turn == 2:
            return sent.at[at], got.at[to]
        if turn == 3:
            return back.at[at], home.at[to]
        if turn == 4:
            return partial, partials.at[slot]
        block = slab_of(device // cols, lax.rem(device, cols), rows, cols)
        place = pl.ds(pl.multiple_of(block * yf, 8), yf)
        return lifted.at[turn - 5, place], risen.at[pairs * slot + turn - 5]

    def copy(turn, step):
        peer = lax.rem(me + step, devices)
        source, target = ends(turn, peer, me)
        return pltpu.make_async_remote_copy(
            src_ref=source,
            dst_ref=target,
            send_sem=send_sem.at[turn, step],
            recv_sem=recv_sem.at[turn, step],
            device_id=(peer // cols, lax.rem(peer, cols)),
            device_id_type=MESH,
        )

    def own(turn):
        source, target = ends(turn, me, me)
        return pltpu.make_async_copy(source, target, own_sem.at[turn])

    def launch(turn):
        def start(step, carry):
            copy(turn, step).start()
            return carry

        lax.fori_loop(1, devices, start, 0)
        own(turn).start()

    def arrive(turn):
        def wait(step, carry):
            copy(turn, step).wait_recv()
            return carry

        lax.fori_loop(1, devices, wait, 0)
        own(turn).wait()

    def scatter(turn, source):
        for high in range(xb // 8):
            for low in range(8):
                block = source[8 * high + low]
                if turn == 0:
                    column[low] = product_with(pair_of(evolve), halves(block), ((1,), (1,)))
                else:
                    column[low] = block.T
            turned = jnp.transpose(column[...], (1, 0, 2)).reshape(devices, zb, 8, yb)
            for z in range(zb):
                at = (high * zb + z) * yb
                given[turn, :, :, at : at + yb] = turned[:, z]

    def gather(turn, target):
        def one(r, carry):
            for c in range(cols):
                for high in range(xb // 8):
                    place = pl.ds(pl.multiple_of(r * xb + 8 * high, 8), 8)
                    for z in range(zb):
                        at = (high * zb + z) * yb
                        target[z, place, yb * c : yb * (c + 1)] = taken[
                            turn, r * cols + c, :, at : at + yb
                        ]
            return carry

        lax.fori_loop(0, rows, one, 0)

    scatter(0, wave)
    stack[zb:] = jnp.zeros((8 - zb, nc, nc), jnp.float32)
    pl.semaphore_wait(barrier, devices - 1)
    launch(0)
    scatter(1, trap)
    launch(1)
    arrive(0)
    gather(0, field)

    def left(matrix, values):
        return product_with(pair_of(matrix), halves(values), ((1,), (0,)))

    def right(values, matrix):
        return product_with(halves(values), pair_of(matrix), ((1,), (0,)))

    def forward(z, carry):
        evolved = right(left(evolve, field[z]), evolve)
        field[z] = evolved
        stack[z] = right(left(cas, evolved * evolved), cas)
        return carry

    lax.fori_loop(0, zb, forward, 0)
    turned = jnp.transpose(stack[...], (1, 0, 2)).reshape(nc // 2, 2, 8, nc)
    for e in range(2):
        sent[:, :, e * nc : (e + 1) * nc] = turned[:, e]
    launch(2)
    arrive(1)
    gather(1, well)
    arrive(2)
    for t in range(pairs):
        block = got[...].reshape(devices, pairs, 8, nf)[:, t].reshape(devices * 8, nf)
        values = left(deep, block)
        sq_x = [squared_wave(me * zb + 2 * t + e, nc, 2.0) for e in range(2)]
        lanes = lax.broadcasted_iota(jnp.int32, (1, 2 * nc), 1)
        squares = (jnp.where(lanes < nc, sq_x[0], sq_x[1]) + sq_y[...]) + sq_z[...]
        nonzero = jnp.where(squares > 0, squares, 1.0)
        weights = jnp.where(
            squares > 0, DIPOLE_STRENGTH * (3.0 * sq_z[...] - squares) / nonzero, 0.0
        )
        values = right(left(tall, values * (weights / volume)), twice)
        values = values.reshape(devices, 8, nf)
        for d in range(devices):
            back[pairs * d + t] = values[d]
    launch(3)
    arrive(3)
    folded[...] = jnp.transpose(home[...], (1, 0, 2))
    sums = jnp.zeros((8, nc), jnp.float32)
    for z in range(zb):
        square[...] = left(joint, folded[z])
        field_dd = square[:nc, :nc] + square[nc:, nc:]
        evolved = field[z]
        exponent = well[z] + CONTACT * (evolved * evolved) + field_dd
        damped = jnp.exp(-TIME_STEP * exponent) * evolved
        sums += jnp.sum((damped * damped).reshape(nc // 8, 8, nc), axis=0)
        high = product_with(pair_of(lift), halves(damped), ((1,), (1,)))
        lifted[z // 2, :, z % 2 * nc : (z % 2 + 1) * nc] = high
        if z % 2:
            launch(5 + z // 2)
    partial[...] = jnp.full(partial.shape, jnp.sum(sums), jnp.float32)
    launch(4)
    arrive(4)
    scale[...] = lax.rsqrt(jnp.sum(partials[...], axis=0) / volume + EPSILON)
    for turn in range(pairs):
        arrive(5 + turn)

    def settle(step, carry):
        for turn in range(5 + pairs):
            copy(turn, step).wait_send()
        return carry

    lax.fori_loop(1, devices, settle, 0)


def coarse_step(exchange, wave, potential, evolve, lift):
    sizes = exchange.sizes
    rows, cols = sizes["rows"], sizes["cols"]
    devices = rows * cols
    xb, yb, nc = wave.shape
    nf = lift.shape[1]
    zb, yf, pairs = nc // devices, 2 * nf // devices, nc // devices // 2
    cas = cas_table(np.arange(nc), nc)
    deep = np.pad(cas.reshape(nc, devices, zb), ((0, 0), (0, 0), (0, 8 - zb))).reshape(nc, -1)
    twice = np.kron(np.eye(2), cas)
    joint = np.concatenate([cas[:, 0::2], cas[:, 1::2]])
    every = squared_waves(nc, 2.0).astype(np.float32)
    operands = [wave, potential, split(evolve), split(cas), split(deep), split(deep.T)]
    operands += [split(twice), split(joint), split(lift.T)]
    operands += [np.tile(every, 2)[None, :], every[:, None]]
    exchange.calls += 1
    vmem, hbm = pl.BlockSpec(memory_space=pltpu.VMEM), pl.BlockSpec(memory_space=pl.ANY)
    f32 = jnp.float32
    lanes = zb * xb // 8 * yb
    half = (nc // 2, 8, 2 * nc)
    return pl.pallas_call(
        functools.partial(coarse_kernel, sizes, float(nc) ** 3),
        out_shape=[
            jax.ShapeDtypeStruct((nc // 2, yf, 2 * nc), f32),
            jax.ShapeDtypeStruct((8, 128), f32),
        ],
        in_specs=[vmem] * len(operands),
        out_specs=[hbm, vmem],
        scratch_shapes=[
            pltpu.VMEM((8, nc, yb), f32),
            pltpu.VMEM((2, devices, 8, lanes), f32),
            pltpu.VMEM((2, devices, 8, lanes), f32),
            pltpu.VMEM((zb, nc, nc), f32),
            pltpu.VMEM((zb, nc, nc), f32),
            pltpu.VMEM((8, nc, nc), f32),
            pltpu.VMEM(half, f32),
            pltpu.VMEM(half, f32),
            pltpu.VMEM(half, f32),
            pltpu.VMEM(half, f32),
            pltpu.VMEM((8, nc // 2, 2 * nc), f32),
            pltpu.VMEM((pairs, nf, 2 * nc), f32),
            pltpu.VMEM((2 * nc, 2 * nc), f32),
            pltpu.VMEM((8, 128), f32),
            pltpu.VMEM((devices, 8, 128), f32),
            pltpu.SemaphoreType.DMA((5 + pairs, devices)),
            pltpu.SemaphoreType.DMA((5 + pairs, devices)),
            pltpu.SemaphoreType.DMA((5 + pairs,)),
        ],
        compiler_params=pltpu.CompilerParams(
            collective_id=exchange.calls - 1,
            has_side_effects=True,
            vmem_limit_bytes=60 * 1024 * 1024,
        ),
        name=f"coarse_{exchange.calls - 1}",
    )(*operands)


def per_device(sizes, wave_coarse, potential_coarse, potential_fine):
    devices = sizes["rows"] * sizes["cols"]
    nc, nf = wave_coarse.shape[2], potential_fine.shape[2]
    exchange = Exchanger(sizes)

    positions = np.arange(nc)
    coarse_matrix = cas_table(positions, nc)
    decay = np.exp(-0.5 * TIME_STEP * squared_waves(nc, 2.0))[:, None] / nc
    evolve = coarse_matrix @ (decay * coarse_matrix)
    padded = np.where(positions < nc // 2, positions, positions + nc)
    lift = coarse_matrix @ (decay * cas_table(padded, 2 * nc))

    slab, scale = coarse_step(exchange, wave_coarse, potential_coarse, evolve, lift)
    damped, total = fine_step(exchange, slab, scale, lift, potential_fine)
    total = jnp.full((devices, 8, 128), total, jnp.float32)
    (sums,) = swap(exchange, (total, "all"))
    return damped * lax.rsqrt(jnp.sum(sums[:, 0, 0]) / float(nf) ** 3 + EPSILON)


def fits_slabs(sizes, nc, nf):
    rows, cols = sizes["rows"], sizes["cols"]
    devices = rows * cols
    if rows % 2 or cols % 2 or nc % devices or nf % (8 * devices // 2) or nf % (4 * devices):
        return False
    if nc // rows % 8 or nc // devices > 8 or nc // devices % 2:
        return False
    return nf % (8 * rows) == 0 and nf % 128 == 0 and nf // devices % 8 == 4 and 2 * nc == nf


def solution(mesh):
    sizes = {"rows": mesh.shape["rows"], "cols": mesh.shape["cols"]}
    placed = (P("rows", "cols", None), P("rows", "cols", None), P("cols", "rows", None))

    def run(wave_coarse, potential_coarse, potential_fine):
        nc, nf = wave_coarse.shape[0], potential_fine.shape[0]
        body = per_device if fits_slabs(sizes, nc, nf) else per_device_pencils
        return jax.shard_map(
            functools.partial(body, sizes),
            mesh=mesh,
            in_specs=placed,
            out_specs=P("cols", "rows", None),
            check_vma=False,
        )(wave_coarse, potential_coarse, potential_fine)

    return run
```

```python
import functools
import math

import jax
import jax.numpy as jnp
import ml_dtypes
import numpy as np
from jax import lax
from jax.experimental import pallas as pl
from jax.experimental.pallas import tpu as pltpu
from jax.sharding import PartitionSpec as P

TIME_STEP = 0.5
CONTACT = 0.4
DIPOLE_STRENGTH = 0.3
EPSILON = 1e-06
HIGH = lax.Precision.HIGH
HIGHEST = lax.Precision.HIGHEST
MESH = pl.DeviceIdType.MESH


def cas_values(product, length):
    phases = 2.0 * math.pi / length * (product % length).astype(jnp.float32)
    return jnp.cos(phases) + jnp.sin(phases)


def cas_matrix(length):
    positions = jnp.arange(length, dtype=jnp.int32)
    return cas_values(positions[:, None] * positions[None, :], length)


def lift_matrix(length):
    positions = jnp.arange(length, dtype=jnp.int32)
    lifted = jnp.where(positions < length // 2, positions, positions + length)
    fine_points = jnp.arange(2 * length, dtype=jnp.int32)
    return cas_values(lifted[:, None] * fine_points[None, :], 2 * length)


def wavenumbers(length, block_count, offset, spacing):
    positions = offset + jnp.arange(block_count, dtype=jnp.int32)
    signed = jnp.where(positions < length // 2, positions, positions - length)
    return 2.0 * math.pi / (length * spacing) * signed.astype(jnp.float32)


def dipolar_weights(along_x, along_y, along_z, length):
    squares = along_x + along_y + along_z
    nonzero = jnp.where(squares > 0, squares, 1.0)
    weights = jnp.where(squares > 0, DIPOLE_STRENGTH * (3.0 * along_z - squares) / nonzero, 0.0)
    return weights / float(length) ** 3


def exchange_kernel(axes, sizes, *refs):
    count = len(axes)
    sources, targets = refs[:count], refs[count : 2 * count]
    send_sems, recv_sems, local_sems = refs[2 * count :]
    row, col = lax.axis_index("rows"), lax.axis_index("cols")

    def place(axis, index):
        return (index, col) if axis == "rows" else (row, index)

    barrier = pltpu.get_barrier_semaphore()
    waits = 0
    for axis in sorted(set(axes)):
        size = sizes[axis]
        me = lax.axis_index(axis)
        for step in range(1, size):
            peer = lax.rem(me + step, size)
            pl.semaphore_signal(barrier, inc=1, device_id=place(axis, peer), device_id_type=MESH)
        waits += size - 1
    pl.semaphore_wait(barrier, waits)
    most = max(sizes[axis] for axis in axes)
    order = sorted(range(1, most), key=lambda step: abs(2 * step - most))
    copies = []
    for step in order:
        for index, axis in enumerate(axes):
            size = sizes[axis]
            if step >= size:
                continue
            me = lax.axis_index(axis)
            peer = lax.rem(me + step, size)
            copy = pltpu.make_async_remote_copy(
                src_ref=sources[index].at[peer],
                dst_ref=targets[index].at[me],
                send_sem=send_sems.at[index, step],
                recv_sem=recv_sems.at[index, step],
                device_id=place(axis, peer),
                device_id_type=MESH,
            )
            copy.start()
            copies.append(copy)
    for index, axis in enumerate(axes):
        me = lax.axis_index(axis)
        copy = pltpu.make_async_copy(
            sources[index].at[me], targets[index].at[me], local_sems.at[index]
        )
        copy.start()
        copies.append(copy)
    for copy in copies:
        copy.wait()


class Exchanger:
    def __init__(self, sizes):
        self.sizes = sizes
        self.calls = 0

    def __call__(self, *pairs):
        arrays = [array for array, _ in pairs]
        axes = tuple(axis for _, axis in pairs)
        most = max(self.sizes.values())
        count = len(arrays)
        self.calls += 1
        return pl.pallas_call(
            functools.partial(exchange_kernel, axes, self.sizes),
            out_shape=[jax.ShapeDtypeStruct(a.shape, a.dtype) for a in arrays],
            in_specs=[pl.BlockSpec(memory_space=pl.ANY)] * count,
            out_specs=[pl.BlockSpec(memory_space=pl.ANY)] * count,
            scratch_shapes=[
                pltpu.SemaphoreType.DMA((count, most)),
                pltpu.SemaphoreType.DMA((count, most)),
                pltpu.SemaphoreType.DMA((count,)),
            ],
            compiler_params=pltpu.CompilerParams(
                collective_id=self.calls - 1, has_side_effects=True
            ),
            name=f"exchange_{self.calls - 1}",
        )(*arrays)


def give(values, matrix, parts, precision=HIGH):
    if matrix is None:
        turned = jnp.transpose(values, (2, 0, 1))
    else:
        turned = jnp.einsum("abl,lk->kab", values, matrix, precision=precision)
    length, rows_extent, cols_extent = turned.shape
    return turned.reshape(parts, length // parts, rows_extent * cols_extent)


def take(received, axis, rows_extent):
    parts, block, area = received.shape
    cols_extent = area // rows_extent
    received = received.reshape(parts, block, rows_extent, cols_extent)
    if axis == "cols":
        return received.transpose(2, 1, 0, 3).reshape(rows_extent, block, parts * cols_extent)
    return received.transpose(1, 3, 0, 2).reshape(block, cols_extent, parts * rows_extent)


def apply(values, matrix, precision=HIGH):
    return jnp.einsum("abl,lk->abk", values, matrix, precision=precision)


def split_product(values, matrix):
    high = matrix.astype(jnp.bfloat16)
    low = (matrix - high.astype(jnp.float32)).astype(jnp.bfloat16)
    top = values.astype(jnp.bfloat16)
    rest = (values - top.astype(jnp.float32)).astype(jnp.bfloat16)
    product = functools.partial(jnp.dot, preferred_element_type=jnp.float32)
    return product(top, high) + (product(top, low) + product(rest, high))


def gather_pieces(received, held):
    parts, chunk = received.shape[0], held.shape[0]
    width = received.shape[2] // chunk
    for s in range(chunk):
        for p in range(parts):
            held[s, :, p * width : (p + 1) * width] = received[p, :, s * width : (s + 1) * width]


def scatter_pieces(held, sent):
    parts, chunk = sent.shape[0], held.shape[0]
    width = sent.shape[2] // chunk
    for s in range(chunk):
        for p in range(parts):
            sent[p, :, s * width : (s + 1) * width] = held[s, :, p * width : (p + 1) * width]


def assemble_kernel(received, matrix, out, held):
    gather_pieces(received, held)
    chunk, k, length = held.shape
    product = split_product(held[...].reshape(chunk * k, length), matrix[...])
    out[...] = product.reshape(out.shape)


def chunk_of(spectators, width, k):
    for chunk in range(1, spectators):
        if spectators % chunk == 0 and chunk * width % 128 == 0 and chunk * k >= 256:
            return chunk
    return spectators


def assemble(received, spectators, matrix):
    parts, k, area = received.shape
    chunk = chunk_of(spectators, area // spectators, k)
    length, points = matrix.shape
    if k % 8:
        held = received.reshape(parts, k, spectators, -1).transpose(2, 1, 0, 3)
        return apply(held.reshape(spectators, k, length), matrix)
    return pl.pallas_call(
        assemble_kernel,
        grid=(spectators // chunk,),
        in_specs=[
            pl.BlockSpec((parts, k, area // spectators * chunk), lambda i: (0, 0, i)),
            pl.BlockSpec((length, points), lambda i: (0, 0)),
        ],
        out_specs=pl.BlockSpec((chunk, k, points), lambda i: (i, 0, 0)),
        out_shape=jax.ShapeDtypeStruct((spectators, k, points), jnp.float32),
        scratch_shapes=[pltpu.VMEM((chunk, k, length), jnp.float32)],
    )(received, matrix)


def halves(values):
    high = values.astype(jnp.bfloat16)
    return high, (values - high.astype(jnp.float32)).astype(jnp.bfloat16)


def product_of(left, right):
    product = functools.partial(jnp.dot, preferred_element_type=jnp.float32)
    return product(left[0], right[0]) + (product(left[0], right[1]) + product(left[1], right[0]))


def planes_kernel(flows, sizes, chunks, volume, *refs):
    row, col = lax.axis_index("rows"), lax.axis_index("cols")

    def place(axis, index):
        return (index, col) if axis == "rows" else (row, index)

    matrix = refs[0]
    inputs = [refs[1 + 4 * i : 5 + 4 * i] for i in range(len(flows))]
    at = 1 + 4 * len(flows)
    outs = refs[at : at + len(flows)]
    at += len(flows)
    high, low = refs[at : at + 2]
    at += 2
    buffers = [refs[at + 9 * i : at + 9 * i + 9] for i in range(len(flows))]

    barrier = pltpu.get_barrier_semaphore()
    waits = 0
    for axis in sorted(set(axis for axis, _ in flows)):
        size = sizes[axis]
        me = lax.axis_index(axis)
        for step in range(1, size):
            peer = lax.rem(me + step, size)
            pl.semaphore_signal(barrier, inc=1, device_id=place(axis, peer), device_id_type=MESH)
        waits += size - 1
    high[...], low[...] = halves(matrix[...])
    pl.semaphore_wait(barrier, waits)

    def copies(flow, turn, c):
        axis, _ = flows[flow]
        size = sizes[axis]
        me = lax.axis_index(axis)
        sent, received = buffers[flow][2 * turn : 2 * turn + 2]
        send_sem, recv_sem = buffers[flow][4 + 2 * turn : 6 + 2 * turn]
        order = sorted(range(1, size), key=lambda step: abs(2 * step - size))
        for step in order:
            peer = lax.rem(me + step, size)
            yield pltpu.make_async_remote_copy(
                src_ref=sent.at[c, peer],
                dst_ref=received.at[c, me],
                send_sem=send_sem.at[c, step],
                recv_sem=recv_sem.at[c, step],
                device_id=place(axis, peer),
                device_id_type=MESH,
            )

    def launch(flow, turn, c):
        me = lax.axis_index(flows[flow][0])
        for copy in copies(flow, turn, c):
            copy.start()
        sent, received = buffers[flow][2 * turn : 2 * turn + 2]
        received[c, me] = sent[c, me]

    def lanes(area, c):
        if chunks == 1:
            return slice(None)
        return pl.ds(pl.multiple_of(c * (area // chunks), 128), area // chunks)

    def first(c, carry):
        for flow in range(len(flows)):
            source, sent = inputs[flow][0], buffers[flow][0]
            part = source[:, :, lanes(source.shape[2], c)]
            part = part.reshape(matrix.shape[0], part.shape[2])
            product = product_of((high[...], low[...]), halves(part))
            sent[c] = product.reshape(sent.shape[1:])
            launch(flow, 0, c)
        return carry

    def second(c, carry):
        for flow in range(len(flows)):
            _, sq_s, sq_k, sq_l = inputs[flow]
            vertical = flows[flow][1]
            held = buffers[flow][8]
            chunk, k, length = held.shape
            for copy in copies(flow, 0, c):
                copy.wait_recv()
            gather_pieces(buffers[flow][1].at[c], held)
            both = (high[...], low[...])
            values = product_of(halves(held[...].reshape(chunk * k, length)), both)
            parts = [sq_s[pl.ds(c * chunk, chunk)], sq_k[...][None], sq_l[...][None]]
            parts = [jnp.broadcast_to(part, held.shape) for part in parts]
            squares = parts[0] + parts[1] + parts[2]
            nonzero = jnp.where(squares > 0, squares, 1.0)
            weights = jnp.where(
                squares > 0, DIPOLE_STRENGTH * (3.0 * parts[vertical] - squares) / nonzero, 0.0
            )
            values = values * (weights / volume).reshape(chunk * k, length)
            held[...] = product_of(halves(values), both).reshape(held.shape)
            scatter_pieces(held, buffers[flow][2].at[c])
            launch(flow, 1, c)
        return carry

    def third(c, carry):
        for flow in range(len(flows)):
            for copy in copies(flow, 1, c):
                copy.wait_recv()
            received, out = buffers[flow][3], outs[flow]
            part = received[c].reshape(matrix.shape[0], received.shape[3])
            product = product_of((high[...], low[...]), halves(part))
            out[:, lanes(out.shape[1], c)] = product
            for turn in range(2):
                for copy in copies(flow, turn, c):
                    copy.wait_send()
        return carry

    for stage in (first, second, third):
        lax.fori_loop(0, chunks, stage, 0)


def planes(exchange, flows, matrix):
    sizes = exchange.sizes
    length = matrix.shape[0]
    counts = []
    for axis, _, received, sq_s, sq_k, _ in flows:
        spectators = sq_s.shape[0]
        width = received.shape[2] // spectators
        counts.append(spectators // chunk_of(spectators, width, sq_k.shape[0]))
    chunks = counts[0] if len(set(counts)) == 1 else 1
    operands, outs, scratch = [matrix], [], []
    scratch += [pltpu.VMEM((length, length), jnp.bfloat16)] * 2
    for axis, _, received, sq_s, sq_k, sq_l in flows:
        operands += [received, sq_s[:, None, None], sq_k[:, None], sq_l[None, :]]
        area, k, size = received.shape[2], sq_k.shape[0], sizes[axis]
        outs.append(jax.ShapeDtypeStruct((length, area), jnp.float32))
        scratch += [pltpu.VMEM((chunks, size, k, area // chunks), jnp.float32)] * 4
        scratch += [pltpu.SemaphoreType.DMA((chunks, size))] * 4
        scratch += [pltpu.VMEM((sq_s.shape[0] // chunks, k, length), jnp.float32)]
    exchange.calls += 1
    vmem = pl.BlockSpec(memory_space=pltpu.VMEM)
    return pl.pallas_call(
        functools.partial(
            planes_kernel,
            tuple((flow[0], flow[1]) for flow in flows),
            sizes,
            chunks,
            float(length) ** 3,
        ),
        out_shape=outs,
        in_specs=[vmem] * len(operands),
        out_specs=[vmem] * len(outs),
        scratch_shapes=scratch,
        compiler_params=pltpu.CompilerParams(
            collective_id=exchange.calls - 1,
            has_side_effects=True,
            vmem_limit_bytes=60 * 1024 * 1024,
        ),
        name=f"planes_{exchange.calls - 1}",
    )(*operands)


def blocks(turned, parts):
    first, length, last = turned.shape
    turned = turned.reshape(first, parts, length // parts, last).transpose(1, 0, 2, 3)
    return turned.reshape(parts, first, length // parts * last)


def product_blocks(matrix, received, parts):
    turned = jnp.dot(matrix, received.reshape(-1, received.shape[2]), precision=HIGH)
    return turned.reshape(parts, turned.shape[0] // parts, turned.shape[1])


def per_device_pencils(sizes, wave_coarse, potential_coarse, potential_fine):
    row, col = lax.axis_index("rows"), lax.axis_index("cols")
    rows, cols = sizes["rows"], sizes["cols"]
    nc, nf = wave_coarse.shape[2], potential_fine.shape[2]
    exchange = Exchanger(sizes)

    coarse_matrix = cas_matrix(nc)
    fine_matrix = cas_matrix(nf)
    decay = jnp.exp(-0.5 * TIME_STEP * wavenumbers(nc, nc, 0, 2.0) ** 2)[:, None] / nc
    evolve = jnp.dot(coarse_matrix, decay * coarse_matrix, precision=HIGHEST)
    lift = jnp.dot(coarse_matrix, decay * lift_matrix(nc), precision=HIGHEST)

    xr = yr = nc // rows
    spectators = nc // cols
    turned = jnp.einsum("xyz,zk->ykx", wave_coarse, evolve, precision=HIGH)
    (got,) = exchange((blocks(turned, cols), "cols"))
    (got,) = exchange((product_blocks(evolve.T, got, rows), "rows"))
    evolved = assemble(got, spectators, evolve)
    turned = jnp.einsum("zyx,xk->zky", evolved * evolved, coarse_matrix, precision=HIGH)
    got, back = exchange(
        (blocks(turned, cols), "cols"), (give(evolved.transpose(1, 0, 2), None, rows), "rows")
    )
    back = take(back, "rows", yr)
    got, back = exchange(
        (product_blocks(coarse_matrix, got, rows), "rows"), (give(back, None, cols), "cols")
    )
    spectrum, evolved = assemble(got, spectators, coarse_matrix), take(back, "cols", xr)
    z_block, x_block = nc // rows, nc // cols
    weights = dipolar_weights(
        wavenumbers(nc, x_block, col * x_block, 2.0)[:, None, None] ** 2,
        wavenumbers(nc, nc, 0, 2.0)[None, None, :] ** 2,
        wavenumbers(nc, z_block, row * z_block, 2.0)[None, :, None] ** 2,
        nc,
    )
    turned = jnp.einsum("xzy,yk->xkz", weights * spectrum, coarse_matrix, precision=HIGH)
    (got,) = exchange((blocks(turned, cols), "cols"))
    (got,) = exchange((product_blocks(coarse_matrix, got, rows), "rows"))
    field_dd = assemble(got, spectators, coarse_matrix).transpose(1, 0, 2)
    density = evolved * evolved
    damped = jnp.exp(-TIME_STEP * (potential_coarse + CONTACT * density + field_dd)) * evolved
    partial_sum = jnp.sum(damped * damped)

    got, sums = exchange(
        (blocks(jnp.einsum("xyz,zk->ykx", damped, lift, precision=HIGH), cols), "cols"),
        (jnp.full((cols, 8, 128), partial_sum, jnp.float32), "cols"),
    )
    partial_sum = jnp.sum(sums[:, 0, 0])
    got, sums = exchange(
        (product_blocks(lift.T, got, rows), "rows"),
        (jnp.full((rows, 8, 128), partial_sum, jnp.float32), "rows"),
    )
    scale = lax.rsqrt(jnp.sum(sums[:, 0, 0]) / float(nc) ** 3 + EPSILON)
    evolved = assemble(got, nf // cols, lift) * scale

    density = evolved * evolved
    half = nf // 2
    near, far = fine_matrix[:, :half], fine_matrix[:, half:]
    got_near, got_far = exchange(
        (blocks(jnp.einsum("zyx,xk->ykz", density, near, precision=HIGH), rows), "rows"),
        (blocks(jnp.einsum("zyx,xk->zky", density, far, precision=HIGH), cols), "cols"),
    )
    y_block, z_block = nf // cols, nf // rows
    near_block, far_block = half // rows, half // cols
    every = wavenumbers(nf, nf, 0, 1.0) ** 2
    near_flow = (
        "cols",
        2,
        got_near,
        wavenumbers(nf, near_block, row * near_block, 1.0) ** 2,
        wavenumbers(nf, y_block, col * y_block, 1.0) ** 2,
        every,
    )
    far_flow = (
        "rows",
        1,
        got_far,
        wavenumbers(nf, far_block, half + col * far_block, 1.0) ** 2,
        wavenumbers(nf, z_block, row * z_block, 1.0) ** 2,
        every,
    )
    got_far, got_near = planes(exchange, (far_flow, near_flow), fine_matrix)
    got_near, got_far = exchange(
        (got_near.reshape(rows, nf // rows, -1), "rows"),
        (got_far.reshape(cols, nf // cols, -1), "cols"),
    )
    z_extent, y_extent = nf // cols, nf // rows
    near_field = got_near.reshape(rows, y_extent, near_block, z_extent)
    near_field = near_field.transpose(3, 1, 0, 2).reshape(z_extent, y_extent, half)
    far_field = got_far.reshape(cols, z_extent, far_block, y_extent)
    far_field = far_field.transpose(1, 3, 0, 2).reshape(z_extent, y_extent, half)
    spectrum = jnp.concatenate([near_field, far_field], axis=2)
    field_dd = jnp.einsum("zyk,kx->zyx", spectrum, fine_matrix, precision=HIGH)
    damped = jnp.exp(-TIME_STEP * (potential_fine + CONTACT * density + field_dd)) * evolved
    total = jnp.sum(damped * damped)
    for axis in ("rows", "cols"):
        (sums,) = exchange((jnp.full((sizes[axis], 8, 128), total, jnp.float32), axis))
        total = jnp.sum(sums[:, 0, 0])
    return damped * lax.rsqrt(total / float(nf) ** 3 + EPSILON)


def strip_of(row, col, t, rows, cols, count):
    middle, odd = rows // 2, lax.rem(row, 2)
    first = (count * col + 1 - odd) // 2
    own = own_strips(row, col, count)
    other = (count * col + odd) // 2
    away = lax.rem(row + middle, rows)
    block = count * cols // 2
    return jnp.where(t < own, row * block + first + t, away * block + other + t - own)


def own_strips(row, col, count):
    odd = lax.rem(row, 2)
    return (count * (col + 1) + 1 - odd) // 2 - (count * col + 1 - odd) // 2


def split(matrix):
    high = matrix.astype(np.float32).astype(ml_dtypes.bfloat16)
    low = (matrix - high.astype(np.float64)).astype(np.float32).astype(ml_dtypes.bfloat16)
    return np.stack([high, low])


def cas_table(rows, length):
    product = np.outer(rows, np.arange(length, dtype=np.int64)) % length
    phases = 2.0 * np.pi / length * product
    return np.cos(phases) + np.sin(phases)


def squared_waves(length, spacing):
    positions = np.arange(length)
    signed = np.where(positions < length // 2, positions, positions - length)
    return (2.0 * np.pi / (length * spacing) * signed) ** 2


def squared_wave(position, length, spacing):
    signed = jnp.where(position < length // 2, position, position - length)
    wave = signed.astype(jnp.float32) * (2.0 * math.pi / (length * spacing))
    return wave * wave


def pair_of(ref, *index):
    return ref[(*index, 0)], ref[(*index, 1)]


def product_with(left, right, contract):
    def product(a, b):
        return lax.dot_general(a, b, (contract, ((), ())), preferred_element_type=jnp.float32)

    return product(left[0], right[0]) + (product(left[0], right[1]) + product(left[1], right[0]))


def fine_kernel(sizes, volume, *refs):
    slab, scale, rise, lift, near, last, cas, spread, rolled, sq_y, sq_z = refs[:11]
    packed, taken = refs[11:13]
    raw, lines, plane, shares, given, planes, sent, got, stage, turned, packing = refs[13:24]
    load_sem, send_sem, recv_sem, out_sem, in_sem, own_sem = refs[24:30]
    give_sem, take_sem = refs[30:32]
    rows, cols = sizes["rows"], sizes["cols"]
    row, col = lax.axis_index("rows"), lax.axis_index("cols")
    me, middle = row * cols + col, rows // 2
    base, local = row // middle * middle, lax.rem(row, middle)
    slabs = middle * cols
    kb, nf = got.shape[0], got.shape[1]
    yf = nf // slabs
    steps, rounds = raw.shape[0], packed.shape[1]
    part, width = yf // steps, kb // rounds
    nc, depth = plane.shape[1], lines.shape[1]
    share = given.shape[0] // cols
    parity = row // middle
    sign = (1 - 2 * parity).astype(jnp.float32)
    own = own_strips(row, col, steps)
    first_strip = lax.rem(strip_of(row, col, 0, rows, cols, steps), taken.shape[0])

    def place_of(t):
        return pl.ds(pl.multiple_of(8 * strip_of(row, col, t, rows, cols, steps), 8), 8)

    def load(t):
        return pltpu.make_async_copy(
            slab.at[:, pl.ds(pl.multiple_of(t * part, 8), part)], raw.at[t], load_sem.at[t]
        )

    for t in range(steps):
        load(t).start()

    barrier = pltpu.get_barrier_semaphore()

    def greet(step, carry):
        peer = lax.rem(me + step, rows * cols)
        pl.semaphore_signal(
            barrier, inc=1, device_id=(peer // cols, lax.rem(peer, cols)), device_id_type=MESH
        )
        return carry

    lax.fori_loop(1, rows * cols, greet, 0)

    def forward(chunk, t, step):
        r = lax.rem(local + step // cols, middle)
        c = lax.rem(col + lax.rem(step, cols), cols)
        first = (r * cols + c) * kb + chunk * width
        return pltpu.make_async_remote_copy(
            src_ref=sent.at[pl.ds(first, width), pl.ds(pl.multiple_of(t * part, 8), part)],
            dst_ref=got.at[pl.ds(chunk * width, width), place_of(t)],
            send_sem=send_sem.at[chunk, t, step],
            recv_sem=recv_sem.at[chunk, t, step],
            device_id=(base + r, c),
            device_id_type=MESH,
        )

    def launch(chunk, t):
        def start(step, carry):
            forward(chunk, t, step).start()
            return carry

        lax.fori_loop(1, slabs, start, 0)
        first = (local * cols + col) * kb + chunk * width
        got[pl.ds(chunk * width, width), place_of(t), :] = sent[
            pl.ds(first, width), pl.ds(pl.multiple_of(t * part, 8), part), :
        ]

    def front(t, carry):
        load(t).wait()
        lines[...] = jnp.transpose(raw[t], (1, 0, 2))

        def line(y, carry):
            for e in range(2):
                plane[e * depth : (e + 1) * depth] = lines[y, :, e * nc : (e + 1) * nc]
            high = product_with(pair_of(rise), halves(plane[...]), ((1,), (0,))) * scale[:1, :1]
            for e in range(2):
                shares[y, :, e * nc : (e + 1) * nc] = high[e * nc : (e + 1) * nc]
            field = product_with(pair_of(lift), halves(high), ((1,), (1,)))
            density = field * field
            density = halves(density[:nc] + sign * density[nc:])
            along_x = product_with(pair_of(near, parity), density, ((1,), (0,)))
            planes[y] = product_with(halves(along_x), pair_of(last), ((1,), (0,)))
            return carry

        lax.fori_loop(0, part, line, 0)
        place = pl.ds(pl.multiple_of(t * part, 8), part)
        sent[:, place, :] = jnp.transpose(planes[...], (1, 0, 2))

        @pl.when(t < given.shape[1] // 8)
        def _():
            given[:, place, :] = jnp.transpose(shares[...], (1, 0, 2))

        @pl.when(t == 0)
        def _():
            pl.semaphore_wait(barrier, rows * cols - 1)

        launch(0, t)

        @pl.when(t > 0)
        def _():
            launch(1, t - 1)

        return carry

    lax.fori_loop(0, steps, front, 0)

    launch(1, steps - 1)

    def later(index, carry):
        launch(2 + index // steps, lax.rem(index, steps))
        return carry

    lax.fori_loop(0, (rounds - 2) * steps, later, 0)

    def give(t, step):
        c = lax.rem(col + step, cols)
        return pltpu.make_async_remote_copy(
            src_ref=given.at[pl.ds(c * share, share), 8 * t : 8 * t + 8],
            dst_ref=taken.at[first_strip + t],
            send_sem=give_sem.at[t, step],
            recv_sem=take_sem.at[first_strip + t],
            device_id=(row, c),
            device_id_type=MESH,
        )

    def keep(t):
        return pltpu.make_async_copy(
            given.at[pl.ds(col * share, share), 8 * t : 8 * t + 8],
            taken.at[first_strip + t],
            give_sem.at[t, 0],
        )

    def give_all():
        for t in range(given.shape[1] // 8):

            @pl.when(t < own)
            def _():
                for step in range(1, cols):
                    give(t, step).start()
                keep(t).start()

    def inverse(chunk, r, c):
        return pltpu.make_async_remote_copy(
            src_ref=packing.at[r, c, chunk],
            dst_ref=packed.at[me, chunk],
            send_sem=out_sem.at[chunk, r, c],
            recv_sem=in_sem.at[chunk, me],
            device_id=(r, c),
            device_id_type=MESH,
        )

    def stay(chunk):
        return pltpu.make_async_copy(
            packing.at[row, col, chunk], packed.at[me, chunk], own_sem.at[chunk]
        )

    zi = turned.shape[3] // 2
    yo = nf // rows

    def convolve(chunk, carry):
        def arrive(index, carry):
            t, step = index // slabs, lax.rem(index, slabs)

            @pl.when(step != 0)
            def _():
                forward(chunk, t, step).wait_recv()

            return carry

        lax.fori_loop(0, steps * slabs, arrive, 0)

        def couple(kp, carry):
            parts = []
            for b in range(2):
                k = chunk * width + 2 * kp + b
                top, bottom = got[k, : nf // 2], got[k, nf // 2 :]
                values = jnp.concatenate(
                    [
                        product_with(pair_of(cas, 0), halves(top + bottom), ((1,), (0,))),
                        product_with(pair_of(cas, 1), halves(top - bottom), ((1,), (0,))),
                    ]
                )
                sq_x = squared_wave(2 * ((local * cols + col) * kb + k) + parity, nf, 1.0)
                squares = (sq_x + sq_y[...]) + sq_z[...]
                nonzero = jnp.where(squares > 0, squares, 1.0)
                weights = jnp.where(
                    squares > 0, DIPOLE_STRENGTH * (3.0 * sq_z[...] - squares) / nonzero, 0.0
                )
                values = halves(values * (weights / volume))
                along_z = product_with(pair_of(spread, b), values, ((1,), (1,)))
                parts.append(along_z.reshape(rows, cols, -1, nf))
            turned[:, :, kp] = jnp.concatenate(
                [parts[0][:, :, :-8], parts[0][:, :, -8:] + parts[1][:, :, :8], parts[1][:, :, 8:]],
                axis=2,
            )
            return carry

        lax.fori_loop(0, width // 2, couple, 0)

        def roll(j, carry):
            block = turned[j].reshape(-1, nf)
            stage[j] = product_with(halves(block), pair_of(rolled, j), ((1,), (0,)))
            return carry

        lax.fori_loop(0, rows, roll, 0)

        def pack(index, carry):
            step = lax.rem(index + middle, rows)
            r = lax.rem(row + step, rows)
            for tile in range(nf // 128):
                lanes = lax.broadcasted_iota(jnp.int32, (1, 128), 1) + 128 * tile
                first, last = 128 * tile // yo, (128 * tile + 127) // yo
                value = None
                for p in range(last, first - 1, -1):
                    j = lax.rem(p - r + rows, rows)
                    block = stage[j, :, 128 * tile : 128 * tile + 128]
                    value = block if value is None else jnp.where(lanes < (p + 1) * yo, block, value)
                value = value.reshape(cols, width // 2, 2 * zi, 128)
                for c in range(cols):
                    packing[r, c, chunk, :, tile] = value[c]
            for b in range(cols - 1, -1, -1):
                c = lax.rem(col + b, cols)
                if b:
                    inverse(chunk, r, c).start()
                else:

                    @pl.when(step != 0)
                    def _():
                        inverse(chunk, r, c).start()

                    @pl.when(step == 0)
                    def _():
                        stay(chunk).start()

            return carry

        lax.fori_loop(0, rows, pack, 0)

        @pl.when(chunk == 0)
        def _():
            give_all()

        return carry

    lax.fori_loop(0, rounds, convolve, 0)

    def finish(chunk, carry):
        stay(chunk).wait()

        def one(source, carry):
            @pl.when(source != me)
            def _():
                r, c = source // cols, lax.rem(source, cols)
                pltpu.make_async_remote_copy(
                    src_ref=packing.at[r, c, chunk],
                    dst_ref=packed.at[source, chunk],
                    send_sem=out_sem.at[chunk, r, c],
                    recv_sem=in_sem.at[chunk, source],
                    device_id=(r, c),
                    device_id_type=MESH,
                ).wait()

            return carry

        lax.fori_loop(0, rows * cols, one, 0)

        def left(index, carry):
            t, step = index // slabs, lax.rem(index, slabs)

            @pl.when(step != 0)
            def _():
                forward(chunk, t, step).wait_send()

            return carry

        lax.fori_loop(0, steps * slabs, left, 0)
        return carry

    lax.fori_loop(0, rounds, finish, 0)

    for t in range(given.shape[1] // 8):

        @pl.when(t < own)
        def _():
            for step in range(1, cols):
                give(t, step).wait_send()
            keep(t).wait()

    for strip in range(taken.shape[0]):
        source = (2 * strip + lax.rem(row, 2)) // steps

        @pl.when(col != source)
        def _():
            pltpu.make_async_remote_copy(
                src_ref=given.at[pl.ds(col * share, share), 0:8],
                dst_ref=taken.at[strip],
                send_sem=give_sem.at[0, 0],
                recv_sem=take_sem.at[strip],
                device_id=(row, source),
                device_id_type=MESH,
            ).wait_recv()


def out_kernel(sizes, volume, *refs):
    packed, cas, lift, taken, trap, damped, scale, fields, total, partial, partials = refs[:11]
    send_sem, recv_sem = refs[11:]
    i = pl.program_id(0)
    rows, cols = sizes["rows"], sizes["cols"]
    row, col = lax.axis_index("rows"), lax.axis_index("cols")
    devices, me = rows * cols, row * cols + col
    zi, nf = pl.num_programs(0), cas.shape[1]
    barrier = pltpu.get_barrier_semaphore()

    @pl.when(i == 0)
    def _():
        def greet(step, carry):
            peer = lax.rem(me + step, devices)
            pl.semaphore_signal(
                barrier, inc=1, device_id=(peer // cols, lax.rem(peer, cols)), device_id_type=MESH
            )
            return carry

        lax.fori_loop(1, devices, greet, 0)

    strips = taken.shape[0]
    block = halves(taken[:, :, 0].reshape(strips * rows * 8, nf))
    block = product_with(block, pair_of(lift, i // (zi // 2)), ((1,), (0,)))
    block = block.reshape(strips, rows, 8, nf)
    for strip in range(strips):
        fields[:, 8 * strip : 8 * strip + 8, :] = block[strip]
    tiles = nf // 128
    run = tiles * 2 * zi
    columns = []
    for tile in range(tiles):
        pieces = [
            packed[pl.ds(tile * 2 * zi + b * zi + i, nf // 2, stride=run), :] for b in range(2)
        ]
        columns.append(jnp.concatenate(pieces, axis=0))
    values = halves(jnp.concatenate(columns, axis=1))
    field_dd = product_with(values, pair_of(cas), ((0,), (0,)))
    yo = nf // rows
    squares = jnp.zeros((8, nf), jnp.float32)
    for p in range(rows):
        j = lax.rem(p - row + rows, rows)
        evolved = fields[j]
        exponent = trap[j, 0] + CONTACT * (evolved * evolved) + field_dd[p * yo : (p + 1) * yo]
        result = jnp.exp(-TIME_STEP * exponent) * evolved
        damped[j, 0] = result
        squares += jnp.sum((result * result).reshape(yo // 8, 8, nf), axis=0)

    @pl.when(i == 0)
    def _():
        total[...] = squares

    @pl.when(i > 0)
    def _():
        total[...] += squares

    def copy(step):
        peer = lax.rem(me + step, devices)
        return pltpu.make_async_remote_copy(
            src_ref=partial,
            dst_ref=partials.at[me],
            send_sem=send_sem.at[step],
            recv_sem=recv_sem.at[step],
            device_id=(peer // cols, lax.rem(peer, cols)),
            device_id_type=MESH,
        )

    @pl.when(i == zi - 1)
    def _():
        partial[...] = jnp.full(partial.shape, jnp.sum(total[...]), jnp.float32)
        pl.semaphore_wait(barrier, devices - 1)

        def start(step, carry):
            copy(step).start()
            return carry

        def wait(step, carry):
            copy(step).wait()
            return carry

        lax.fori_loop(1, devices, start, 0)
        partials[me] = partial[...]
        lax.fori_loop(1, devices, wait, 0)
        scale[...] = lax.rsqrt(jnp.sum(partials[...], axis=0) / volume + EPSILON)


def fine_step(exchange, slab, scale, lift, potential):
    sizes = exchange.sizes
    rows, cols = sizes["rows"], sizes["cols"]
    devices = rows * cols
    nc, nf = lift.shape
    depth, yf = slab.shape[:2]
    kb = nf // devices
    yo, zo = nf // rows, nf // cols
    zi = zo // rows
    steps, rounds = yf // 8, kb // 4
    width, tiles = kb // rounds, nf // 128
    natural = np.arange(nf)
    waves = np.concatenate([natural[0::2], natural[1::2]])
    fine_matrix = cas_table(natural, nf)
    order = fine_matrix.reshape(cols, rows, zi, nf).transpose(1, 0, 2, 3)
    spread = [
        split(np.pad(order, ((0, 0), (0, 0), pads, (0, 0))).reshape(-1, nf))
        for pads in ((0, -zi % 8), (-zi % 8, 0))
    ]
    rolled = np.stack([split(np.roll(fine_matrix[waves], yo * j, axis=1)) for j in range(rows)])
    slabs = nf // yf
    shape = (cols, rows, 2, zi // 2)
    rise = lift.reshape((nc // 2, 2) + shape).transpose(4, 2, 3, 5, 1, 0).reshape(nf, nc)
    last = fine_matrix.reshape(shape + (nf,)).transpose(2, 0, 1, 3, 4).reshape(nf, nf)
    every = squared_waves(nf, 1.0).astype(np.float32)
    folded = np.stack([split(fine_matrix[parity::2, : nf // 2]) for parity in range(2)])
    operands = [
        slab,
        scale,
        split(rise),
        split(lift.T),
        folded,
        split(last),
        folded,
        np.stack(spread),
        rolled,
        every[waves][:, None],
        every[None, :],
    ]
    exchange.calls += 1
    vmem, hbm = pl.BlockSpec(memory_space=pltpu.VMEM), pl.BlockSpec(memory_space=pl.ANY)
    f32 = jnp.float32
    packed, taken = pl.pallas_call(
        functools.partial(fine_kernel, sizes, float(nf) ** 3),
        out_shape=[
            jax.ShapeDtypeStruct((devices, rounds, width // 2, tiles, 2 * zi, 128), f32),
            jax.ShapeDtypeStruct((yo // 8, nc // cols, 8, nf), f32),
        ],
        in_specs=[hbm] + [vmem] * (len(operands) - 1),
        out_specs=[hbm, hbm],
        scratch_shapes=[
            pltpu.VMEM((steps, depth, yf // steps, nf), f32),
            pltpu.VMEM((yf // steps, depth, nf), f32),
            pltpu.VMEM((nc, nc), f32),
            pltpu.VMEM((yf // steps, nc, nf), f32),
            pltpu.VMEM((nc, (steps + 1) // 2 * 8, nf), f32),
            pltpu.VMEM((yf // steps, nf // 2, nf), f32),
            pltpu.VMEM((nf // 2, yf, nf), f32),
            pltpu.VMEM((kb, nf, nf), f32),
            pltpu.VMEM((rows, cols * width * zi, nf), f32),
            pltpu.VMEM((rows, cols, width // 2, 2 * zi, nf), f32),
            pltpu.VMEM((rows, cols, rounds, width // 2, tiles, 2 * zi, 128), f32),
            pltpu.SemaphoreType.DMA((steps,)),
            pltpu.SemaphoreType.DMA((rounds, steps, slabs)),
            pltpu.SemaphoreType.DMA((rounds, steps, slabs)),
            pltpu.SemaphoreType.DMA((rounds, rows, cols)),
            pltpu.SemaphoreType.DMA((rounds, devices)),
            pltpu.SemaphoreType.DMA((rounds,)),
            pltpu.SemaphoreType.DMA(((steps + 1) // 2, cols)),
            pltpu.SemaphoreType.DMA((yo // 8,)),
        ],
        compiler_params=pltpu.CompilerParams(
            collective_id=exchange.calls - 1,
            has_side_effects=True,
            vmem_limit_bytes=60 * 1024 * 1024,
        ),
        name=f"fine_{exchange.calls - 1}",
    )(*operands)

    zeros = np.zeros_like(lift)
    lifts = np.stack([split(np.concatenate([lift, zeros])), split(np.concatenate([zeros, lift]))])
    cas = split(fine_matrix[np.concatenate([waves[0::2], waves[1::2]])])
    block = pl.BlockSpec((rows, 1, yo, nf), lambda i: (0, i, 0, 0))
    exchange.calls += 1
    damped, scale = pl.pallas_call(
        functools.partial(out_kernel, sizes, float(nf) ** 3),
        grid=(zi,),
        in_specs=[
            vmem,
            vmem,
            vmem,
            pl.BlockSpec(
                (yo // 8, rows, 1, 8, nf), lambda i: (0, 0, lax.rem(i, zi // 2), 0, 0)
            ),
            block,
        ],
        out_specs=[block, pl.BlockSpec((8, 128), lambda i: (0, 0))],
        out_shape=[
            jax.ShapeDtypeStruct((rows, zi, yo, nf), f32),
            jax.ShapeDtypeStruct((8, 128), f32),
        ],
        scratch_shapes=[
            pltpu.VMEM((rows, yo, nf), f32),
            pltpu.VMEM((8, nf), f32),
            pltpu.VMEM((8, 128), f32),
            pltpu.VMEM((devices, 8, 128), f32),
            pltpu.SemaphoreType.DMA((devices,)),
            pltpu.SemaphoreType.DMA((devices,)),
        ],
        compiler_params=pltpu.CompilerParams(
            collective_id=exchange.calls - 1,
            has_side_effects=True,
            vmem_limit_bytes=60 * 1024 * 1024,
        ),
        name="damp",
    )(
        packed.reshape(-1, 128),
        cas,
        lifts,
        taken.reshape(yo // 8, rows, zi // 2, 8, nf),
        potential.reshape(rows, zi, yo, nf),
    )
    return damped.reshape(zo, yo, nf) * scale[0, 0]


def coarse_kernel(sizes, volume, *refs):
    wave, trap, evolve, cas, deep, tall, twice, joint, lift, sq_y, sq_z = refs[:11]
    risen, scale = refs[11:13]
    column, given, taken, field, well, stack, sent, got, back, home = refs[13:23]
    folded, lifted, square, partial, partials = refs[23:28]
    send_sem, recv_sem, own_sem = refs[28:31]
    rows, cols = sizes["rows"], sizes["cols"]
    row, col = lax.axis_index("rows"), lax.axis_index("cols")
    devices, me = rows * cols, row * cols + col
    xb, yb, nc = wave.shape
    zb, nf = nc // devices, lift.shape[1]
    strips = risen.shape[1] // 8
    pairs = zb // 2

    barrier = pltpu.get_barrier_semaphore()

    def greet(step, carry):
        peer = lax.rem(me + step, devices)
        pl.semaphore_signal(
            barrier, inc=1, device_id=(peer // cols, lax.rem(peer, cols)), device_id_type=MESH
        )
        return carry

    lax.fori_loop(1, devices, greet, 0)

    def ends(turn, device, slot):
        if turn < 2:
            return given.at[turn, device], taken.at[turn, slot]
        at, to = pl.ds(pairs * device, pairs), pl.ds(pairs * slot, pairs)
        if turn == 2:
            return sent.at[at], got.at[to]
        if turn == 3:
            return back.at[at], home.at[to]
        if turn == 4:
            return partial, partials.at[slot]
        t, z = (turn - 5) // pairs, (turn - 5) % pairs
        strip = strip_of(device // cols, lax.rem(device, cols), t, rows, cols, strips)
        place = pl.ds(pl.multiple_of(8 * strip, 8), 8)
        return lifted.at[z, place], risen.at[pairs * slot + z, 8 * t : 8 * t + 8]

    def copy(turn, step):
        peer = lax.rem(me + step, devices)
        source, target = ends(turn, peer, me)
        return pltpu.make_async_remote_copy(
            src_ref=source,
            dst_ref=target,
            send_sem=send_sem.at[turn, step],
            recv_sem=recv_sem.at[turn, step],
            device_id=(peer // cols, lax.rem(peer, cols)),
            device_id_type=MESH,
        )

    def own(turn):
        source, target = ends(turn, me, me)
        return pltpu.make_async_copy(source, target, own_sem.at[turn])

    def launch(turn):
        def start(step, carry):
            copy(turn, step).start()
            return carry

        lax.fori_loop(1, devices, start, 0)
        own(turn).start()

    def arrive(turn):
        def wait(step, carry):
            copy(turn, step).wait_recv()
            return carry

        lax.fori_loop(1, devices, wait, 0)
        own(turn).wait()

    def scatter(turn, source):
        for high in range(xb // 8):
            for low in range(8):
                block = source[8 * high + low]
                if turn == 0:
                    column[low] = product_with(pair_of(evolve), halves(block), ((1,), (1,)))
                else:
                    column[low] = block.T
            turned = jnp.transpose(column[...], (1, 0, 2)).reshape(devices, zb, 8, yb)
            for z in range(zb):
                at = (high * zb + z) * yb
                given[turn, :, :, at : at + yb] = turned[:, z]

    def gather(turn, target):
        def one(r, carry):
            for c in range(cols):
                for high in range(xb // 8):
                    place = pl.ds(pl.multiple_of(r * xb + 8 * high, 8), 8)
                    for z in range(zb):
                        at = (high * zb + z) * yb
                        target[z, place, yb * c : yb * (c + 1)] = taken[
                            turn, r * cols + c, :, at : at + yb
                        ]
            return carry

        lax.fori_loop(0, rows, one, 0)

    scatter(0, wave)
    stack[zb:] = jnp.zeros((8 - zb, nc, nc), jnp.float32)
    pl.semaphore_wait(barrier, devices - 1)
    launch(0)
    scatter(1, trap)
    launch(1)
    arrive(0)
    gather(0, field)

    def left(matrix, values):
        return product_with(pair_of(matrix), halves(values), ((1,), (0,)))

    def right(values, matrix):
        return product_with(halves(values), pair_of(matrix), ((1,), (0,)))

    def forward(z, carry):
        evolved = right(left(evolve, field[z]), evolve)
        field[z] = evolved
        stack[z] = right(left(cas, evolved * evolved), cas)
        return carry

    lax.fori_loop(0, zb, forward, 0)
    turned = jnp.transpose(stack[...], (1, 0, 2)).reshape(nc // 2, 2, 8, nc)
    for e in range(2):
        sent[:, :, e * nc : (e + 1) * nc] = turned[:, e]
    launch(2)
    arrive(1)
    gather(1, well)
    arrive(2)
    for t in range(pairs):
        block = got[...].reshape(devices, pairs, 8, nf)[:, t].reshape(devices * 8, nf)
        values = left(deep, block)
        sq_x = [squared_wave(me * zb + 2 * t + e, nc, 2.0) for e in range(2)]
        lanes = lax.broadcasted_iota(jnp.int32, (1, 2 * nc), 1)
        squares = (jnp.where(lanes < nc, sq_x[0], sq_x[1]) + sq_y[...]) + sq_z[...]
        nonzero = jnp.where(squares > 0, squares, 1.0)
        weights = jnp.where(
            squares > 0, DIPOLE_STRENGTH * (3.0 * sq_z[...] - squares) / nonzero, 0.0
        )
        values = right(left(tall, values * (weights / volume)), twice)
        values = values.reshape(devices, 8, nf)
        for d in range(devices):
            back[pairs * d + t] = values[d]
    launch(3)
    arrive(3)
    folded[...] = jnp.transpose(home[...], (1, 0, 2))
    sums = jnp.zeros((8, nc), jnp.float32)
    for z in range(zb):
        square[...] = left(joint, folded[z])
        field_dd = square[:nc, :nc] + square[nc:, nc:]
        evolved = field[z]
        exponent = well[z] + CONTACT * (evolved * evolved) + field_dd
        damped = jnp.exp(-TIME_STEP * exponent) * evolved
        sums += jnp.sum((damped * damped).reshape(nc // 8, 8, nc), axis=0)
        high = product_with(pair_of(lift), halves(damped), ((1,), (1,)))
        lifted[z // 2, :, z % 2 * nc : (z % 2 + 1) * nc] = high
        if z % 2:
            for t in range(strips):
                launch(5 + t * pairs + z // 2)
    partial[...] = jnp.full(partial.shape, jnp.sum(sums), jnp.float32)
    launch(4)
    arrive(4)
    scale[...] = lax.rsqrt(jnp.sum(partials[...], axis=0) / volume + EPSILON)
    for turn in range(strips * pairs):
        arrive(5 + turn)

    def settle(step, carry):
        for turn in range(5 + strips * pairs):
            copy(turn, step).wait_send()
        return carry

    lax.fori_loop(1, devices, settle, 0)


def coarse_step(exchange, wave, potential, evolve, lift):
    sizes = exchange.sizes
    rows, cols = sizes["rows"], sizes["cols"]
    devices = rows * cols
    xb, yb, nc = wave.shape
    nf = lift.shape[1]
    zb, yf, pairs = nc // devices, 2 * nf // devices, nc // devices // 2
    cas = cas_table(np.arange(nc), nc)
    deep = np.pad(cas.reshape(nc, devices, zb), ((0, 0), (0, 0), (0, 8 - zb))).reshape(nc, -1)
    twice = np.kron(np.eye(2), cas)
    joint = np.concatenate([cas[:, 0::2], cas[:, 1::2]])
    every = squared_waves(nc, 2.0).astype(np.float32)
    operands = [wave, potential, split(evolve), split(cas), split(deep), split(deep.T)]
    operands += [split(twice), split(joint), split(lift.T)]
    operands += [np.tile(every, 2)[None, :], every[:, None]]
    exchange.calls += 1
    vmem, hbm = pl.BlockSpec(memory_space=pltpu.VMEM), pl.BlockSpec(memory_space=pl.ANY)
    f32 = jnp.float32
    lanes = zb * xb // 8 * yb
    half = (nc // 2, 8, 2 * nc)
    turns = 5 + yf // 8 * pairs
    return pl.pallas_call(
        functools.partial(coarse_kernel, sizes, float(nc) ** 3),
        out_shape=[
            jax.ShapeDtypeStruct((nc // 2, yf, 2 * nc), f32),
            jax.ShapeDtypeStruct((8, 128), f32),
        ],
        in_specs=[vmem] * len(operands),
        out_specs=[hbm, vmem],
        scratch_shapes=[
            pltpu.VMEM((8, nc, yb), f32),
            pltpu.VMEM((2, devices, 8, lanes), f32),
            pltpu.VMEM((2, devices, 8, lanes), f32),
            pltpu.VMEM((zb, nc, nc), f32),
            pltpu.VMEM((zb, nc, nc), f32),
            pltpu.VMEM((8, nc, nc), f32),
            pltpu.VMEM(half, f32),
            pltpu.VMEM(half, f32),
            pltpu.VMEM(half, f32),
            pltpu.VMEM(half, f32),
            pltpu.VMEM((8, nc // 2, 2 * nc), f32),
            pltpu.VMEM((pairs, nf, 2 * nc), f32),
            pltpu.VMEM((2 * nc, 2 * nc), f32),
            pltpu.VMEM((8, 128), f32),
            pltpu.VMEM((devices, 8, 128), f32),
            pltpu.SemaphoreType.DMA((turns, devices)),
            pltpu.SemaphoreType.DMA((turns, devices)),
            pltpu.SemaphoreType.DMA((turns,)),
        ],
        compiler_params=pltpu.CompilerParams(
            collective_id=exchange.calls - 1,
            has_side_effects=True,
            vmem_limit_bytes=60 * 1024 * 1024,
        ),
        name=f"coarse_{exchange.calls - 1}",
    )(*operands)


def per_device(sizes, wave_coarse, potential_coarse, potential_fine):
    devices = sizes["rows"] * sizes["cols"]
    nc, nf = wave_coarse.shape[2], potential_fine.shape[2]
    exchange = Exchanger(sizes)

    positions = np.arange(nc)
    coarse_matrix = cas_table(positions, nc)
    decay = np.exp(-0.5 * TIME_STEP * squared_waves(nc, 2.0))[:, None] / nc
    evolve = coarse_matrix @ (decay * coarse_matrix)
    padded = np.where(positions < nc // 2, positions, positions + nc)
    lift = coarse_matrix @ (decay * cas_table(padded, 2 * nc))

    slab, scale = coarse_step(exchange, wave_coarse, potential_coarse, evolve, lift)
    return fine_step(exchange, slab, scale, lift, potential_fine)


def fits_slabs(sizes, nc, nf):
    rows, cols = sizes["rows"], sizes["cols"]
    devices = rows * cols
    if rows % 2 or cols % 2 or nc % devices or nf % (8 * devices // 2) or nf % (4 * devices):
        return False
    if nc // rows % 8 or nc // devices > 8 or nc // devices % 2:
        return False
    return nf % (8 * rows) == 0 and nf % 128 == 0 and nf // devices % 8 == 4 and 2 * nc == nf


def solution(mesh):
    sizes = {"rows": mesh.shape["rows"], "cols": mesh.shape["cols"]}
    placed = (P("rows", "cols", None), P("rows", "cols", None), P("cols", "rows", None))

    def run(wave_coarse, potential_coarse, potential_fine):
        nc, nf = wave_coarse.shape[0], potential_fine.shape[0]
        body = per_device if fits_slabs(sizes, nc, nf) else per_device_pencils
        return jax.shard_map(
            functools.partial(body, sizes),
            mesh=mesh,
            in_specs=placed,
            out_specs=P("cols", "rows", None),
            check_vma=False,
        )(wave_coarse, potential_coarse, potential_fine)

    return run
```

```python
import functools
import math

import jax
import jax.numpy as jnp
import ml_dtypes
import numpy as np
from jax import lax
from jax.experimental import pallas as pl
from jax.experimental.pallas import tpu as pltpu
from jax.sharding import PartitionSpec as P

TIME_STEP = 0.5
CONTACT = 0.4
DIPOLE_STRENGTH = 0.3
EPSILON = 1e-06
HIGH = lax.Precision.HIGH
HIGHEST = lax.Precision.HIGHEST
MESH = pl.DeviceIdType.MESH


def cas_values(product, length):
    phases = 2.0 * math.pi / length * (product % length).astype(jnp.float32)
    return jnp.cos(phases) + jnp.sin(phases)


def cas_matrix(length):
    positions = jnp.arange(length, dtype=jnp.int32)
    return cas_values(positions[:, None] * positions[None, :], length)


def lift_matrix(length):
    positions = jnp.arange(length, dtype=jnp.int32)
    lifted = jnp.where(positions < length // 2, positions, positions + length)
    fine_points = jnp.arange(2 * length, dtype=jnp.int32)
    return cas_values(lifted[:, None] * fine_points[None, :], 2 * length)


def wavenumbers(length, block_count, offset, spacing):
    positions = offset + jnp.arange(block_count, dtype=jnp.int32)
    signed = jnp.where(positions < length // 2, positions, positions - length)
    return 2.0 * math.pi / (length * spacing) * signed.astype(jnp.float32)


def dipolar_weights(along_x, along_y, along_z, length):
    squares = along_x + along_y + along_z
    nonzero = jnp.where(squares > 0, squares, 1.0)
    weights = jnp.where(squares > 0, DIPOLE_STRENGTH * (3.0 * along_z - squares) / nonzero, 0.0)
    return weights / float(length) ** 3


def exchange_kernel(axes, sizes, *refs):
    count = len(axes)
    sources, targets = refs[:count], refs[count : 2 * count]
    send_sems, recv_sems, local_sems = refs[2 * count :]
    row, col = lax.axis_index("rows"), lax.axis_index("cols")

    def place(axis, index):
        return (index, col) if axis == "rows" else (row, index)

    barrier = pltpu.get_barrier_semaphore()
    waits = 0
    for axis in sorted(set(axes)):
        size = sizes[axis]
        me = lax.axis_index(axis)
        for step in range(1, size):
            peer = lax.rem(me + step, size)
            pl.semaphore_signal(barrier, inc=1, device_id=place(axis, peer), device_id_type=MESH)
        waits += size - 1
    pl.semaphore_wait(barrier, waits)
    most = max(sizes[axis] for axis in axes)
    order = sorted(range(1, most), key=lambda step: abs(2 * step - most))
    copies = []
    for step in order:
        for index, axis in enumerate(axes):
            size = sizes[axis]
            if step >= size:
                continue
            me = lax.axis_index(axis)
            peer = lax.rem(me + step, size)
            copy = pltpu.make_async_remote_copy(
                src_ref=sources[index].at[peer],
                dst_ref=targets[index].at[me],
                send_sem=send_sems.at[index, step],
                recv_sem=recv_sems.at[index, step],
                device_id=place(axis, peer),
                device_id_type=MESH,
            )
            copy.start()
            copies.append(copy)
    for index, axis in enumerate(axes):
        me = lax.axis_index(axis)
        copy = pltpu.make_async_copy(
            sources[index].at[me], targets[index].at[me], local_sems.at[index]
        )
        copy.start()
        copies.append(copy)
    for copy in copies:
        copy.wait()


class Exchanger:
    def __init__(self, sizes):
        self.sizes = sizes
        self.calls = 0

    def __call__(self, *pairs):
        arrays = [array for array, _ in pairs]
        axes = tuple(axis for _, axis in pairs)
        most = max(self.sizes.values())
        count = len(arrays)
        self.calls += 1
        return pl.pallas_call(
            functools.partial(exchange_kernel, axes, self.sizes),
            out_shape=[jax.ShapeDtypeStruct(a.shape, a.dtype) for a in arrays],
            in_specs=[pl.BlockSpec(memory_space=pl.ANY)] * count,
            out_specs=[pl.BlockSpec(memory_space=pl.ANY)] * count,
            scratch_shapes=[
                pltpu.SemaphoreType.DMA((count, most)),
                pltpu.SemaphoreType.DMA((count, most)),
                pltpu.SemaphoreType.DMA((count,)),
            ],
            compiler_params=pltpu.CompilerParams(
                collective_id=self.calls - 1, has_side_effects=True
            ),
            name=f"exchange_{self.calls - 1}",
        )(*arrays)


def give(values, matrix, parts, precision=HIGH):
    if matrix is None:
        turned = jnp.transpose(values, (2, 0, 1))
    else:
        turned = jnp.einsum("abl,lk->kab", values, matrix, precision=precision)
    length, rows_extent, cols_extent = turned.shape
    return turned.reshape(parts, length // parts, rows_extent * cols_extent)


def take(received, axis, rows_extent):
    parts, block, area = received.shape
    cols_extent = area // rows_extent
    received = received.reshape(parts, block, rows_extent, cols_extent)
    if axis == "cols":
        return received.transpose(2, 1, 0, 3).reshape(rows_extent, block, parts * cols_extent)
    return received.transpose(1, 3, 0, 2).reshape(block, cols_extent, parts * rows_extent)


def apply(values, matrix, precision=HIGH):
    return jnp.einsum("abl,lk->abk", values, matrix, precision=precision)


def split_product(values, matrix):
    high = matrix.astype(jnp.bfloat16)
    low = (matrix - high.astype(jnp.float32)).astype(jnp.bfloat16)
    top = values.astype(jnp.bfloat16)
    rest = (values - top.astype(jnp.float32)).astype(jnp.bfloat16)
    product = functools.partial(jnp.dot, preferred_element_type=jnp.float32)
    return product(top, high) + (product(top, low) + product(rest, high))


def gather_pieces(received, held):
    parts, chunk = received.shape[0], held.shape[0]
    width = received.shape[2] // chunk
    for s in range(chunk):
        for p in range(parts):
            held[s, :, p * width : (p + 1) * width] = received[p, :, s * width : (s + 1) * width]


def scatter_pieces(held, sent):
    parts, chunk = sent.shape[0], held.shape[0]
    width = sent.shape[2] // chunk
    for s in range(chunk):
        for p in range(parts):
            sent[p, :, s * width : (s + 1) * width] = held[s, :, p * width : (p + 1) * width]


def assemble_kernel(received, matrix, out, held):
    gather_pieces(received, held)
    chunk, k, length = held.shape
    product = split_product(held[...].reshape(chunk * k, length), matrix[...])
    out[...] = product.reshape(out.shape)


def chunk_of(spectators, width, k):
    for chunk in range(1, spectators):
        if spectators % chunk == 0 and chunk * width % 128 == 0 and chunk * k >= 256:
            return chunk
    return spectators


def assemble(received, spectators, matrix):
    parts, k, area = received.shape
    chunk = chunk_of(spectators, area // spectators, k)
    length, points = matrix.shape
    if k % 8:
        held = received.reshape(parts, k, spectators, -1).transpose(2, 1, 0, 3)
        return apply(held.reshape(spectators, k, length), matrix)
    return pl.pallas_call(
        assemble_kernel,
        grid=(spectators // chunk,),
        in_specs=[
            pl.BlockSpec((parts, k, area // spectators * chunk), lambda i: (0, 0, i)),
            pl.BlockSpec((length, points), lambda i: (0, 0)),
        ],
        out_specs=pl.BlockSpec((chunk, k, points), lambda i: (i, 0, 0)),
        out_shape=jax.ShapeDtypeStruct((spectators, k, points), jnp.float32),
        scratch_shapes=[pltpu.VMEM((chunk, k, length), jnp.float32)],
    )(received, matrix)


def halves(values):
    high = values.astype(jnp.bfloat16)
    return high, (values - high.astype(jnp.float32)).astype(jnp.bfloat16)


def product_of(left, right):
    product = functools.partial(jnp.dot, preferred_element_type=jnp.float32)
    return product(left[0], right[0]) + (product(left[0], right[1]) + product(left[1], right[0]))


def planes_kernel(flows, sizes, chunks, volume, *refs):
    row, col = lax.axis_index("rows"), lax.axis_index("cols")

    def place(axis, index):
        return (index, col) if axis == "rows" else (row, index)

    matrix = refs[0]
    inputs = [refs[1 + 4 * i : 5 + 4 * i] for i in range(len(flows))]
    at = 1 + 4 * len(flows)
    outs = refs[at : at + len(flows)]
    at += len(flows)
    high, low = refs[at : at + 2]
    at += 2
    buffers = [refs[at + 9 * i : at + 9 * i + 9] for i in range(len(flows))]

    barrier = pltpu.get_barrier_semaphore()
    waits = 0
    for axis in sorted(set(axis for axis, _ in flows)):
        size = sizes[axis]
        me = lax.axis_index(axis)
        for step in range(1, size):
            peer = lax.rem(me + step, size)
            pl.semaphore_signal(barrier, inc=1, device_id=place(axis, peer), device_id_type=MESH)
        waits += size - 1
    high[...], low[...] = halves(matrix[...])
    pl.semaphore_wait(barrier, waits)

    def copies(flow, turn, c):
        axis, _ = flows[flow]
        size = sizes[axis]
        me = lax.axis_index(axis)
        sent, received = buffers[flow][2 * turn : 2 * turn + 2]
        send_sem, recv_sem = buffers[flow][4 + 2 * turn : 6 + 2 * turn]
        order = sorted(range(1, size), key=lambda step: abs(2 * step - size))
        for step in order:
            peer = lax.rem(me + step, size)
            yield pltpu.make_async_remote_copy(
                src_ref=sent.at[c, peer],
                dst_ref=received.at[c, me],
                send_sem=send_sem.at[c, step],
                recv_sem=recv_sem.at[c, step],
                device_id=place(axis, peer),
                device_id_type=MESH,
            )

    def launch(flow, turn, c):
        me = lax.axis_index(flows[flow][0])
        for copy in copies(flow, turn, c):
            copy.start()
        sent, received = buffers[flow][2 * turn : 2 * turn + 2]
        received[c, me] = sent[c, me]

    def lanes(area, c):
        if chunks == 1:
            return slice(None)
        return pl.ds(pl.multiple_of(c * (area // chunks), 128), area // chunks)

    def first(c, carry):
        for flow in range(len(flows)):
            source, sent = inputs[flow][0], buffers[flow][0]
            part = source[:, :, lanes(source.shape[2], c)]
            part = part.reshape(matrix.shape[0], part.shape[2])
            product = product_of((high[...], low[...]), halves(part))
            sent[c] = product.reshape(sent.shape[1:])
            launch(flow, 0, c)
        return carry

    def second(c, carry):
        for flow in range(len(flows)):
            _, sq_s, sq_k, sq_l = inputs[flow]
            vertical = flows[flow][1]
            held = buffers[flow][8]
            chunk, k, length = held.shape
            for copy in copies(flow, 0, c):
                copy.wait_recv()
            gather_pieces(buffers[flow][1].at[c], held)
            both = (high[...], low[...])
            values = product_of(halves(held[...].reshape(chunk * k, length)), both)
            parts = [sq_s[pl.ds(c * chunk, chunk)], sq_k[...][None], sq_l[...][None]]
            parts = [jnp.broadcast_to(part, held.shape) for part in parts]
            squares = parts[0] + parts[1] + parts[2]
            nonzero = jnp.where(squares > 0, squares, 1.0)
            weights = jnp.where(
                squares > 0, DIPOLE_STRENGTH * (3.0 * parts[vertical] - squares) / nonzero, 0.0
            )
            values = values * (weights / volume).reshape(chunk * k, length)
            held[...] = product_of(halves(values), both).reshape(held.shape)
            scatter_pieces(held, buffers[flow][2].at[c])
            launch(flow, 1, c)
        return carry

    def third(c, carry):
        for flow in range(len(flows)):
            for copy in copies(flow, 1, c):
                copy.wait_recv()
            received, out = buffers[flow][3], outs[flow]
            part = received[c].reshape(matrix.shape[0], received.shape[3])
            product = product_of((high[...], low[...]), halves(part))
            out[:, lanes(out.shape[1], c)] = product
            for turn in range(2):
                for copy in copies(flow, turn, c):
                    copy.wait_send()
        return carry

    for stage in (first, second, third):
        lax.fori_loop(0, chunks, stage, 0)


def planes(exchange, flows, matrix):
    sizes = exchange.sizes
    length = matrix.shape[0]
    counts = []
    for axis, _, received, sq_s, sq_k, _ in flows:
        spectators = sq_s.shape[0]
        width = received.shape[2] // spectators
        counts.append(spectators // chunk_of(spectators, width, sq_k.shape[0]))
    chunks = counts[0] if len(set(counts)) == 1 else 1
    operands, outs, scratch = [matrix], [], []
    scratch += [pltpu.VMEM((length, length), jnp.bfloat16)] * 2
    for axis, _, received, sq_s, sq_k, sq_l in flows:
        operands += [received, sq_s[:, None, None], sq_k[:, None], sq_l[None, :]]
        area, k, size = received.shape[2], sq_k.shape[0], sizes[axis]
        outs.append(jax.ShapeDtypeStruct((length, area), jnp.float32))
        scratch += [pltpu.VMEM((chunks, size, k, area // chunks), jnp.float32)] * 4
        scratch += [pltpu.SemaphoreType.DMA((chunks, size))] * 4
        scratch += [pltpu.VMEM((sq_s.shape[0] // chunks, k, length), jnp.float32)]
    exchange.calls += 1
    vmem = pl.BlockSpec(memory_space=pltpu.VMEM)
    return pl.pallas_call(
        functools.partial(
            planes_kernel,
            tuple((flow[0], flow[1]) for flow in flows),
            sizes,
            chunks,
            float(length) ** 3,
        ),
        out_shape=outs,
        in_specs=[vmem] * len(operands),
        out_specs=[vmem] * len(outs),
        scratch_shapes=scratch,
        compiler_params=pltpu.CompilerParams(
            collective_id=exchange.calls - 1,
            has_side_effects=True,
            vmem_limit_bytes=60 * 1024 * 1024,
        ),
        name=f"planes_{exchange.calls - 1}",
    )(*operands)


def blocks(turned, parts):
    first, length, last = turned.shape
    turned = turned.reshape(first, parts, length // parts, last).transpose(1, 0, 2, 3)
    return turned.reshape(parts, first, length // parts * last)


def product_blocks(matrix, received, parts):
    turned = jnp.dot(matrix, received.reshape(-1, received.shape[2]), precision=HIGH)
    return turned.reshape(parts, turned.shape[0] // parts, turned.shape[1])


def per_device_pencils(sizes, wave_coarse, potential_coarse, potential_fine):
    row, col = lax.axis_index("rows"), lax.axis_index("cols")
    rows, cols = sizes["rows"], sizes["cols"]
    nc, nf = wave_coarse.shape[2], potential_fine.shape[2]
    exchange = Exchanger(sizes)

    coarse_matrix = cas_matrix(nc)
    fine_matrix = cas_matrix(nf)
    decay = jnp.exp(-0.5 * TIME_STEP * wavenumbers(nc, nc, 0, 2.0) ** 2)[:, None] / nc
    evolve = jnp.dot(coarse_matrix, decay * coarse_matrix, precision=HIGHEST)
    lift = jnp.dot(coarse_matrix, decay * lift_matrix(nc), precision=HIGHEST)

    xr = yr = nc // rows
    spectators = nc // cols
    turned = jnp.einsum("xyz,zk->ykx", wave_coarse, evolve, precision=HIGH)
    (got,) = exchange((blocks(turned, cols), "cols"))
    (got,) = exchange((product_blocks(evolve.T, got, rows), "rows"))
    evolved = assemble(got, spectators, evolve)
    turned = jnp.einsum("zyx,xk->zky", evolved * evolved, coarse_matrix, precision=HIGH)
    got, back = exchange(
        (blocks(turned, cols), "cols"), (give(evolved.transpose(1, 0, 2), None, rows), "rows")
    )
    back = take(back, "rows", yr)
    got, back = exchange(
        (product_blocks(coarse_matrix, got, rows), "rows"), (give(back, None, cols), "cols")
    )
    spectrum, evolved = assemble(got, spectators, coarse_matrix), take(back, "cols", xr)
    z_block, x_block = nc // rows, nc // cols
    weights = dipolar_weights(
        wavenumbers(nc, x_block, col * x_block, 2.0)[:, None, None] ** 2,
        wavenumbers(nc, nc, 0, 2.0)[None, None, :] ** 2,
        wavenumbers(nc, z_block, row * z_block, 2.0)[None, :, None] ** 2,
        nc,
    )
    turned = jnp.einsum("xzy,yk->xkz", weights * spectrum, coarse_matrix, precision=HIGH)
    (got,) = exchange((blocks(turned, cols), "cols"))
    (got,) = exchange((product_blocks(coarse_matrix, got, rows), "rows"))
    field_dd = assemble(got, spectators, coarse_matrix).transpose(1, 0, 2)
    density = evolved * evolved
    damped = jnp.exp(-TIME_STEP * (potential_coarse + CONTACT * density + field_dd)) * evolved
    partial_sum = jnp.sum(damped * damped)

    got, sums = exchange(
        (blocks(jnp.einsum("xyz,zk->ykx", damped, lift, precision=HIGH), cols), "cols"),
        (jnp.full((cols, 8, 128), partial_sum, jnp.float32), "cols"),
    )
    partial_sum = jnp.sum(sums[:, 0, 0])
    got, sums = exchange(
        (product_blocks(lift.T, got, rows), "rows"),
        (jnp.full((rows, 8, 128), partial_sum, jnp.float32), "rows"),
    )
    scale = lax.rsqrt(jnp.sum(sums[:, 0, 0]) / float(nc) ** 3 + EPSILON)
    evolved = assemble(got, nf // cols, lift) * scale

    density = evolved * evolved
    half = nf // 2
    near, far = fine_matrix[:, :half], fine_matrix[:, half:]
    got_near, got_far = exchange(
        (blocks(jnp.einsum("zyx,xk->ykz", density, near, precision=HIGH), rows), "rows"),
        (blocks(jnp.einsum("zyx,xk->zky", density, far, precision=HIGH), cols), "cols"),
    )
    y_block, z_block = nf // cols, nf // rows
    near_block, far_block = half // rows, half // cols
    every = wavenumbers(nf, nf, 0, 1.0) ** 2
    near_flow = (
        "cols",
        2,
        got_near,
        wavenumbers(nf, near_block, row * near_block, 1.0) ** 2,
        wavenumbers(nf, y_block, col * y_block, 1.0) ** 2,
        every,
    )
    far_flow = (
        "rows",
        1,
        got_far,
        wavenumbers(nf, far_block, half + col * far_block, 1.0) ** 2,
        wavenumbers(nf, z_block, row * z_block, 1.0) ** 2,
        every,
    )
    got_far, got_near = planes(exchange, (far_flow, near_flow), fine_matrix)
    got_near, got_far = exchange(
        (got_near.reshape(rows, nf // rows, -1), "rows"),
        (got_far.reshape(cols, nf // cols, -1), "cols"),
    )
    z_extent, y_extent = nf // cols, nf // rows
    near_field = got_near.reshape(rows, y_extent, near_block, z_extent)
    near_field = near_field.transpose(3, 1, 0, 2).reshape(z_extent, y_extent, half)
    far_field = got_far.reshape(cols, z_extent, far_block, y_extent)
    far_field = far_field.transpose(1, 3, 0, 2).reshape(z_extent, y_extent, half)
    spectrum = jnp.concatenate([near_field, far_field], axis=2)
    field_dd = jnp.einsum("zyk,kx->zyx", spectrum, fine_matrix, precision=HIGH)
    damped = jnp.exp(-TIME_STEP * (potential_fine + CONTACT * density + field_dd)) * evolved
    total = jnp.sum(damped * damped)
    for axis in ("rows", "cols"):
        (sums,) = exchange((jnp.full((sizes[axis], 8, 128), total, jnp.float32), axis))
        total = jnp.sum(sums[:, 0, 0])
    return damped * lax.rsqrt(total / float(nf) ** 3 + EPSILON)


def strip_of(row, col, t, rows, cols, count):
    middle, odd = rows // 2, lax.rem(row, 2)
    first = (count * col + 1 - odd) // 2
    own = own_strips(row, col, count)
    other = (count * col + odd) // 2
    away = lax.rem(row + middle, rows)
    block = count * cols // 2
    return jnp.where(t < own, row * block + first + t, away * block + other + t - own)


def far_first(turn, count):
    return count // 2 + (1 - 2 * lax.rem(turn, 2)) * ((turn + 1) // 2)


def own_strips(row, col, count):
    odd = lax.rem(row, 2)
    return (count * (col + 1) + 1 - odd) // 2 - (count * col + 1 - odd) // 2


def split(matrix):
    high = matrix.astype(np.float32).astype(ml_dtypes.bfloat16)
    low = (matrix - high.astype(np.float64)).astype(np.float32).astype(ml_dtypes.bfloat16)
    return np.stack([high, low])


def cas_table(rows, length):
    product = np.outer(rows, np.arange(length, dtype=np.int64)) % length
    phases = 2.0 * np.pi / length * product
    return np.cos(phases) + np.sin(phases)


def squared_waves(length, spacing):
    positions = np.arange(length)
    signed = np.where(positions < length // 2, positions, positions - length)
    return (2.0 * np.pi / (length * spacing) * signed) ** 2


def squared_wave(position, length, spacing):
    signed = jnp.where(position < length // 2, position, position - length)
    wave = signed.astype(jnp.float32) * (2.0 * math.pi / (length * spacing))
    return wave * wave


def pair_of(ref, *index):
    return ref[(*index, 0)], ref[(*index, 1)]


def product_with(left, right, contract):
    def product(a, b):
        return lax.dot_general(a, b, (contract, ((), ())), preferred_element_type=jnp.float32)

    return product(left[0], right[0]) + (product(left[0], right[1]) + product(left[1], right[0]))


def fine_kernel(sizes, volume, *refs):
    slab, scale, rise, lift, near, last, cas, spread, rolled, sq_y, sq_z = refs[:11]
    packed, taken = refs[11:13]
    raw, lines, plane, shares, given, planes, sent, got, stage, turned, packing = refs[13:24]
    load_sem, send_sem, recv_sem, out_sem, in_sem, own_sem = refs[24:30]
    give_sem, take_sem = refs[30:32]
    rows, cols = sizes["rows"], sizes["cols"]
    row, col = lax.axis_index("rows"), lax.axis_index("cols")
    me, middle = row * cols + col, rows // 2
    base, local = row // middle * middle, lax.rem(row, middle)
    slabs = middle * cols
    kb, nf = got.shape[0], got.shape[1]
    yf = nf // slabs
    steps, rounds = raw.shape[0], packed.shape[1]
    part, width = yf // steps, kb // rounds
    nc, depth = plane.shape[1], lines.shape[1]
    share = given.shape[0] // cols
    parity = row // middle
    sign = (1 - 2 * parity).astype(jnp.float32)
    own = own_strips(row, col, steps)
    first_strip = lax.rem(strip_of(row, col, 0, rows, cols, steps), taken.shape[0])

    def place_of(t):
        return pl.ds(pl.multiple_of(8 * strip_of(row, col, t, rows, cols, steps), 8), 8)

    def load(t):
        return pltpu.make_async_copy(
            slab.at[:, pl.ds(pl.multiple_of(t * part, 8), part)], raw.at[t], load_sem.at[t]
        )

    for t in range(steps):
        load(t).start()

    barrier = pltpu.get_barrier_semaphore()

    def greet(step, carry):
        peer = lax.rem(me + step, rows * cols)
        pl.semaphore_signal(
            barrier, inc=1, device_id=(peer // cols, lax.rem(peer, cols)), device_id_type=MESH
        )
        return carry

    lax.fori_loop(1, rows * cols, greet, 0)

    def forward(chunk, t, step):
        r = lax.rem(local + step // cols, middle)
        c = lax.rem(col + lax.rem(step, cols), cols)
        first = (r * cols + c) * kb + chunk * width
        return pltpu.make_async_remote_copy(
            src_ref=sent.at[pl.ds(first, width), pl.ds(pl.multiple_of(t * part, 8), part)],
            dst_ref=got.at[pl.ds(chunk * width, width), place_of(t)],
            send_sem=send_sem.at[chunk, t, step],
            recv_sem=recv_sem.at[chunk, t, step],
            device_id=(base + r, c),
            device_id_type=MESH,
        )

    def launch(chunk, t):
        def start(index, carry):
            forward(chunk, t, far_first(index, slabs)).start()
            return carry

        lax.fori_loop(0, slabs - 1, start, 0)
        first = (local * cols + col) * kb + chunk * width
        got[pl.ds(chunk * width, width), place_of(t), :] = sent[
            pl.ds(first, width), pl.ds(pl.multiple_of(t * part, 8), part), :
        ]

    def front(t, carry):
        load(t).wait()
        lines[...] = jnp.transpose(raw[t], (1, 0, 2))

        def line(y, carry):
            for e in range(2):
                plane[e * depth : (e + 1) * depth] = lines[y, :, e * nc : (e + 1) * nc]
            high = product_with(pair_of(rise), halves(plane[...]), ((1,), (0,))) * scale[:1, :1]
            for e in range(2):
                shares[y, :, e * nc : (e + 1) * nc] = high[e * nc : (e + 1) * nc]
            field = product_with(pair_of(lift), halves(high), ((1,), (1,)))
            density = field * field
            density = halves(density[:nc] + sign * density[nc:])
            along_x = product_with(pair_of(near, parity), density, ((1,), (0,)))
            planes[y] = product_with(halves(along_x), pair_of(last), ((1,), (0,)))
            return carry

        lax.fori_loop(0, part, line, 0)
        place = pl.ds(pl.multiple_of(t * part, 8), part)
        sent[:, place, :] = jnp.transpose(planes[...], (1, 0, 2))

        @pl.when(t < given.shape[1] // 8)
        def _():
            given[:, place, :] = jnp.transpose(shares[...], (1, 0, 2))

        @pl.when(t == 0)
        def _():
            pl.semaphore_wait(barrier, rows * cols - 1)

        launch(0, t)

        @pl.when(t > 0)
        def _():
            launch(1, t - 1)

        return carry

    lax.fori_loop(0, steps, front, 0)

    launch(1, steps - 1)

    def later(index, carry):
        launch(2 + index // steps, lax.rem(index, steps))
        return carry

    lax.fori_loop(0, (rounds - 2) * steps, later, 0)

    def give(t, step):
        c = lax.rem(col + step, cols)
        return pltpu.make_async_remote_copy(
            src_ref=given.at[pl.ds(c * share, share), 8 * t : 8 * t + 8],
            dst_ref=taken.at[first_strip + t],
            send_sem=give_sem.at[t, step],
            recv_sem=take_sem.at[first_strip + t],
            device_id=(row, c),
            device_id_type=MESH,
        )

    def keep(t):
        return pltpu.make_async_copy(
            given.at[pl.ds(col * share, share), 8 * t : 8 * t + 8],
            taken.at[first_strip + t],
            give_sem.at[t, 0],
        )

    def give_all():
        for t in range(given.shape[1] // 8):

            @pl.when(t < own)
            def _():
                for step in range(1, cols):
                    give(t, step).start()
                keep(t).start()

    def inverse(chunk, r, c):
        return pltpu.make_async_remote_copy(
            src_ref=packing.at[r, c, chunk],
            dst_ref=packed.at[me, chunk],
            send_sem=out_sem.at[chunk, r, c],
            recv_sem=in_sem.at[chunk, me],
            device_id=(r, c),
            device_id_type=MESH,
        )

    def stay(chunk):
        return pltpu.make_async_copy(
            packing.at[row, col, chunk], packed.at[me, chunk], own_sem.at[chunk]
        )

    zi = turned.shape[3] // 2
    yo = nf // rows

    def convolve(chunk, carry):
        def arrive(index, carry):
            t, step = index // slabs, lax.rem(index, slabs)

            @pl.when(step != 0)
            def _():
                forward(chunk, t, step).wait_recv()

            return carry

        lax.fori_loop(0, steps * slabs, arrive, 0)

        def couple(kp, carry):
            parts = []
            for b in range(2):
                k = chunk * width + 2 * kp + b
                top, bottom = got[k, : nf // 2], got[k, nf // 2 :]
                values = jnp.concatenate(
                    [
                        product_with(pair_of(cas, 0), halves(top + bottom), ((1,), (0,))),
                        product_with(pair_of(cas, 1), halves(top - bottom), ((1,), (0,))),
                    ]
                )
                sq_x = squared_wave(2 * ((local * cols + col) * kb + k) + parity, nf, 1.0)
                squares = (sq_x + sq_y[...]) + sq_z[...]
                nonzero = jnp.where(squares > 0, squares, 1.0)
                weights = jnp.where(
                    squares > 0, DIPOLE_STRENGTH * (3.0 * sq_z[...] - squares) / nonzero, 0.0
                )
                values = halves(values * (weights / volume))
                along_z = product_with(pair_of(spread, b), values, ((1,), (1,)))
                parts.append(along_z.reshape(rows, cols, -1, nf))
            turned[:, :, kp] = jnp.concatenate(
                [parts[0][:, :, :-8], parts[0][:, :, -8:] + parts[1][:, :, :8], parts[1][:, :, 8:]],
                axis=2,
            )
            return carry

        lax.fori_loop(0, width // 2, couple, 0)

        def roll(j, carry):
            block = turned[j].reshape(-1, nf)
            stage[j] = product_with(halves(block), pair_of(rolled, j), ((1,), (0,)))
            return carry

        lax.fori_loop(0, rows, roll, 0)

        def pack(index, carry):
            step = far_first(index, rows)
            r = lax.rem(row + step, rows)
            for tile in range(nf // 128):
                lanes = lax.broadcasted_iota(jnp.int32, (1, 128), 1) + 128 * tile
                first, last = 128 * tile // yo, (128 * tile + 127) // yo
                value = None
                for p in range(last, first - 1, -1):
                    j = lax.rem(p - r + rows, rows)
                    block = stage[j, :, 128 * tile : 128 * tile + 128]
                    value = block if value is None else jnp.where(lanes < (p + 1) * yo, block, value)
                value = value.reshape(cols, width // 2, 2 * zi, 128)
                for c in range(cols):
                    packing[r, c, chunk, :, tile] = value[c]
            for b in range(cols - 1, -1, -1):
                c = lax.rem(col + b, cols)
                if b:
                    inverse(chunk, r, c).start()
                else:

                    @pl.when(step != 0)
                    def _():
                        inverse(chunk, r, c).start()

                    @pl.when(step == 0)
                    def _():
                        stay(chunk).start()

            return carry

        lax.fori_loop(0, rows, pack, 0)

        @pl.when(chunk == 0)
        def _():
            give_all()

        return carry

    lax.fori_loop(0, rounds, convolve, 0)

    def finish(chunk, carry):
        stay(chunk).wait()

        def one(source, carry):
            @pl.when(source != me)
            def _():
                r, c = source // cols, lax.rem(source, cols)
                pltpu.make_async_remote_copy(
                    src_ref=packing.at[r, c, chunk],
                    dst_ref=packed.at[source, chunk],
                    send_sem=out_sem.at[chunk, r, c],
                    recv_sem=in_sem.at[chunk, source],
                    device_id=(r, c),
                    device_id_type=MESH,
                ).wait()

            return carry

        lax.fori_loop(0, rows * cols, one, 0)

        def left(index, carry):
            t, step = index // slabs, lax.rem(index, slabs)

            @pl.when(step != 0)
            def _():
                forward(chunk, t, step).wait_send()

            return carry

        lax.fori_loop(0, steps * slabs, left, 0)
        return carry

    lax.fori_loop(0, rounds, finish, 0)

    for t in range(given.shape[1] // 8):

        @pl.when(t < own)
        def _():
            for step in range(1, cols):
                give(t, step).wait_send()
            keep(t).wait()

    for strip in range(taken.shape[0]):
        source = (2 * strip + lax.rem(row, 2)) // steps

        @pl.when(col != source)
        def _():
            pltpu.make_async_remote_copy(
                src_ref=given.at[pl.ds(col * share, share), 0:8],
                dst_ref=taken.at[strip],
                send_sem=give_sem.at[0, 0],
                recv_sem=take_sem.at[strip],
                device_id=(row, source),
                device_id_type=MESH,
            ).wait_recv()


def out_kernel(sizes, volume, *refs):
    packed, cas, lift, taken, trap, damped, scale, fields, total, partial, partials = refs[:11]
    send_sem, recv_sem = refs[11:]
    i = pl.program_id(0)
    rows, cols = sizes["rows"], sizes["cols"]
    row, col = lax.axis_index("rows"), lax.axis_index("cols")
    devices, me = rows * cols, row * cols + col
    zi, nf = pl.num_programs(0), cas.shape[1]
    barrier = pltpu.get_barrier_semaphore()

    @pl.when(i == 0)
    def _():
        def greet(step, carry):
            peer = lax.rem(me + step, devices)
            pl.semaphore_signal(
                barrier, inc=1, device_id=(peer // cols, lax.rem(peer, cols)), device_id_type=MESH
            )
            return carry

        lax.fori_loop(1, devices, greet, 0)

    strips = taken.shape[0]
    block = halves(taken[:, :, 0].reshape(strips * rows * 8, nf))
    block = product_with(block, pair_of(lift, i // (zi // 2)), ((1,), (0,)))
    block = block.reshape(strips, rows, 8, nf)
    for strip in range(strips):
        fields[:, 8 * strip : 8 * strip + 8, :] = block[strip]
    tiles = nf // 128
    run = tiles * 2 * zi
    columns = []
    for tile in range(tiles):
        pieces = [
            packed[pl.ds(tile * 2 * zi + b * zi + i, nf // 2, stride=run), :] for b in range(2)
        ]
        columns.append(jnp.concatenate(pieces, axis=0))
    values = halves(jnp.concatenate(columns, axis=1))
    field_dd = product_with(values, pair_of(cas), ((0,), (0,)))
    yo = nf // rows
    squares = jnp.zeros((8, nf), jnp.float32)
    for p in range(rows):
        j = lax.rem(p - row + rows, rows)
        evolved = fields[j]
        exponent = trap[j, 0] + CONTACT * (evolved * evolved) + field_dd[p * yo : (p + 1) * yo]
        result = jnp.exp(-TIME_STEP * exponent) * evolved
        damped[j, 0] = result
        squares += jnp.sum((result * result).reshape(yo // 8, 8, nf), axis=0)

    @pl.when(i == 0)
    def _():
        total[...] = squares

    @pl.when(i > 0)
    def _():
        total[...] += squares

    def copy(step):
        peer = lax.rem(me + step, devices)
        return pltpu.make_async_remote_copy(
            src_ref=partial,
            dst_ref=partials.at[me],
            send_sem=send_sem.at[step],
            recv_sem=recv_sem.at[step],
            device_id=(peer // cols, lax.rem(peer, cols)),
            device_id_type=MESH,
        )

    @pl.when(i == zi - 1)
    def _():
        partial[...] = jnp.full(partial.shape, jnp.sum(total[...]), jnp.float32)
        pl.semaphore_wait(barrier, devices - 1)

        def start(step, carry):
            copy(step).start()
            return carry

        def wait(step, carry):
            copy(step).wait()
            return carry

        lax.fori_loop(1, devices, start, 0)
        partials[me] = partial[...]
        lax.fori_loop(1, devices, wait, 0)
        scale[...] = lax.rsqrt(jnp.sum(partials[...], axis=0) / volume + EPSILON)


def fine_step(exchange, slab, scale, lift, potential):
    sizes = exchange.sizes
    rows, cols = sizes["rows"], sizes["cols"]
    devices = rows * cols
    nc, nf = lift.shape
    depth, yf = slab.shape[:2]
    kb = nf // devices
    yo, zo = nf // rows, nf // cols
    zi = zo // rows
    steps, rounds = yf // 8, kb // 4
    width, tiles = kb // rounds, nf // 128
    natural = np.arange(nf)
    waves = np.concatenate([natural[0::2], natural[1::2]])
    fine_matrix = cas_table(natural, nf)
    order = fine_matrix.reshape(cols, rows, zi, nf).transpose(1, 0, 2, 3)
    spread = [
        split(np.pad(order, ((0, 0), (0, 0), pads, (0, 0))).reshape(-1, nf))
        for pads in ((0, -zi % 8), (-zi % 8, 0))
    ]
    rolled = np.stack([split(np.roll(fine_matrix[waves], yo * j, axis=1)) for j in range(rows)])
    slabs = nf // yf
    shape = (cols, rows, 2, zi // 2)
    rise = lift.reshape((nc // 2, 2) + shape).transpose(4, 2, 3, 5, 1, 0).reshape(nf, nc)
    last = fine_matrix.reshape(shape + (nf,)).transpose(2, 0, 1, 3, 4).reshape(nf, nf)
    every = squared_waves(nf, 1.0).astype(np.float32)
    folded = np.stack([split(fine_matrix[parity::2, : nf // 2]) for parity in range(2)])
    operands = [
        slab,
        scale,
        split(rise),
        split(lift.T),
        folded,
        split(last),
        folded,
        np.stack(spread),
        rolled,
        every[waves][:, None],
        every[None, :],
    ]
    exchange.calls += 1
    vmem, hbm = pl.BlockSpec(memory_space=pltpu.VMEM), pl.BlockSpec(memory_space=pl.ANY)
    f32 = jnp.float32
    packed, taken = pl.pallas_call(
        functools.partial(fine_kernel, sizes, float(nf) ** 3),
        out_shape=[
            jax.ShapeDtypeStruct((devices, rounds, width // 2, tiles, 2 * zi, 128), f32),
            jax.ShapeDtypeStruct((yo // 8, nc // cols, 8, nf), f32),
        ],
        in_specs=[hbm] + [vmem] * (len(operands) - 1),
        out_specs=[hbm, hbm],
        scratch_shapes=[
            pltpu.VMEM((steps, depth, yf // steps, nf), f32),
            pltpu.VMEM((yf // steps, depth, nf), f32),
            pltpu.VMEM((nc, nc), f32),
            pltpu.VMEM((yf // steps, nc, nf), f32),
            pltpu.VMEM((nc, (steps + 1) // 2 * 8, nf), f32),
            pltpu.VMEM((yf // steps, nf // 2, nf), f32),
            pltpu.VMEM((nf // 2, yf, nf), f32),
            pltpu.VMEM((kb, nf, nf), f32),
            pltpu.VMEM((rows, cols * width * zi, nf), f32),
            pltpu.VMEM((rows, cols, width // 2, 2 * zi, nf), f32),
            pltpu.VMEM((rows, cols, rounds, width // 2, tiles, 2 * zi, 128), f32),
            pltpu.SemaphoreType.DMA((steps,)),
            pltpu.SemaphoreType.DMA((rounds, steps, slabs)),
            pltpu.SemaphoreType.DMA((rounds, steps, slabs)),
            pltpu.SemaphoreType.DMA((rounds, rows, cols)),
            pltpu.SemaphoreType.DMA((rounds, devices)),
            pltpu.SemaphoreType.DMA((rounds,)),
            pltpu.SemaphoreType.DMA(((steps + 1) // 2, cols)),
            pltpu.SemaphoreType.DMA((yo // 8,)),
        ],
        compiler_params=pltpu.CompilerParams(
            collective_id=exchange.calls - 1,
            has_side_effects=True,
            vmem_limit_bytes=60 * 1024 * 1024,
        ),
        name=f"fine_{exchange.calls - 1}",
    )(*operands)

    zeros = np.zeros_like(lift)
    lifts = np.stack([split(np.concatenate([lift, zeros])), split(np.concatenate([zeros, lift]))])
    cas = split(fine_matrix[np.concatenate([waves[0::2], waves[1::2]])])
    block = pl.BlockSpec((rows, 1, yo, nf), lambda i: (0, i, 0, 0))
    exchange.calls += 1
    damped, scale = pl.pallas_call(
        functools.partial(out_kernel, sizes, float(nf) ** 3),
        grid=(zi,),
        in_specs=[
            vmem,
            vmem,
            vmem,
            pl.BlockSpec(
                (yo // 8, rows, 1, 8, nf), lambda i: (0, 0, lax.rem(i, zi // 2), 0, 0)
            ),
            block,
        ],
        out_specs=[block, pl.BlockSpec((8, 128), lambda i: (0, 0))],
        out_shape=[
            jax.ShapeDtypeStruct((rows, zi, yo, nf), f32),
            jax.ShapeDtypeStruct((8, 128), f32),
        ],
        scratch_shapes=[
            pltpu.VMEM((rows, yo, nf), f32),
            pltpu.VMEM((8, nf), f32),
            pltpu.VMEM((8, 128), f32),
            pltpu.VMEM((devices, 8, 128), f32),
            pltpu.SemaphoreType.DMA((devices,)),
            pltpu.SemaphoreType.DMA((devices,)),
        ],
        compiler_params=pltpu.CompilerParams(
            collective_id=exchange.calls - 1,
            has_side_effects=True,
            vmem_limit_bytes=60 * 1024 * 1024,
        ),
        name="damp",
    )(
        packed.reshape(-1, 128),
        cas,
        lifts,
        taken.reshape(yo // 8, rows, zi // 2, 8, nf),
        potential.reshape(rows, zi, yo, nf),
    )
    return damped.reshape(zo, yo, nf) * scale[0, 0]


def coarse_kernel(sizes, volume, *refs):
    wave, trap, evolve, cas, deep, tall, twice, joint, lift, sq_y, sq_z = refs[:11]
    risen, scale = refs[11:13]
    column, given, taken, field, well, stack, sent, got, back, home = refs[13:23]
    folded, lifted, square, partial, partials, mate_sent, mate_got = refs[23:30]
    send_sem, recv_sem, own_sem, mate_send, mate_recv = refs[30:35]
    rows, cols = sizes["rows"], sizes["cols"]
    row, col = lax.axis_index("rows"), lax.axis_index("cols")
    devices, me = rows * cols, row * cols + col
    xb, yb, nc = wave.shape
    zb, nf = nc // devices, lift.shape[1]
    strips = risen.shape[1] // 8
    pairs = zb // 2

    barrier = pltpu.get_barrier_semaphore()

    def greet(step, carry):
        peer = lax.rem(me + step, devices)
        pl.semaphore_signal(
            barrier, inc=1, device_id=(peer // cols, lax.rem(peer, cols)), device_id_type=MESH
        )
        return carry

    lax.fori_loop(1, devices, greet, 0)

    def ends(turn, device, slot):
        if turn < 2:
            return given.at[turn, device], taken.at[turn, slot]
        at, to = pl.ds(pairs * device, pairs), pl.ds(pairs * slot, pairs)
        if turn == 2:
            return sent.at[at], got.at[to]
        if turn == 3:
            return back.at[at], home.at[to]
        return partial, partials.at[slot]

    def copy(turn, step):
        peer = lax.rem(me + step, devices)
        source, target = ends(turn, peer, me)
        return pltpu.make_async_remote_copy(
            src_ref=source,
            dst_ref=target,
            send_sem=send_sem.at[turn, step],
            recv_sem=recv_sem.at[turn, step],
            device_id=(peer // cols, lax.rem(peer, cols)),
            device_id_type=MESH,
        )

    middle = rows // 2
    base, local = row // middle * middle, lax.rem(row, middle)
    mate_row = lax.rem(row + middle, rows)

    def to_mate(z):
        return pltpu.make_async_remote_copy(
            src_ref=mate_sent.at[z],
            dst_ref=mate_got.at[z],
            send_sem=mate_send.at[z],
            recv_sem=mate_recv.at[z],
            device_id=(mate_row, col),
            device_id_type=MESH,
        )

    def place_of(r, c, t):
        return pl.ds(pl.multiple_of(8 * strip_of(r, c, t, rows, cols, strips), 8), 8)

    def spread_ends(turn, r, c):
        index = turn - 5
        if index < strips:
            source = lifted.at[0, :, place_of(r, c, index)]
            return source, risen.at[pl.ds(pairs * me, pairs), 8 * index : 8 * index + 8]
        z, t = (index - strips) // strips, (index - strips) % strips
        at = pairs * (mate_row * cols + col) + z
        return lifted.at[1, z, place_of(r, c, t)], risen.at[at, 8 * t : 8 * t + 8]

    def spread(turn, step):
        r = base + lax.rem(local + step // cols, middle)
        c = lax.rem(col + lax.rem(step, cols), cols)
        source, target = spread_ends(turn, r, c)
        return pltpu.make_async_remote_copy(
            src_ref=source,
            dst_ref=target,
            send_sem=send_sem.at[turn, step],
            recv_sem=recv_sem.at[turn, step],
            device_id=(r, c),
            device_id_type=MESH,
        )

    def spread_own(turn):
        source, target = spread_ends(turn, row, col)
        return pltpu.make_async_copy(source, target, own_sem.at[turn])

    def spread_out(turns):
        def start(index, carry):
            for turn in turns:
                spread(turn, far_first(index, middle * cols)).start()
            return carry

        lax.fori_loop(0, middle * cols - 1, start, 0)
        for turn in turns:
            spread_own(turn).start()

    def own(turn):
        source, target = ends(turn, me, me)
        return pltpu.make_async_copy(source, target, own_sem.at[turn])

    def launch(turn):
        def start(index, carry):
            copy(turn, far_first(index, devices)).start()
            return carry

        lax.fori_loop(0, devices - 1, start, 0)
        own(turn).start()

    def arrive(turn):
        def wait(step, carry):
            copy(turn, step).wait_recv()
            return carry

        lax.fori_loop(1, devices, wait, 0)
        own(turn).wait()

    def scatter(turn, source):
        for high in range(xb // 8):
            for low in range(8):
                block = source[8 * high + low]
                if turn == 0:
                    column[low] = product_with(pair_of(evolve), halves(block), ((1,), (1,)))
                else:
                    column[low] = block.T
            turned = jnp.transpose(column[...], (1, 0, 2)).reshape(devices, zb, 8, yb)
            for z in range(zb):
                at = (high * zb + z) * yb
                given[turn, :, :, at : at + yb] = turned[:, z]

    def gather(turn, target):
        def one(r, carry):
            for c in range(cols):
                for high in range(xb // 8):
                    place = pl.ds(pl.multiple_of(r * xb + 8 * high, 8), 8)
                    for z in range(zb):
                        at = (high * zb + z) * yb
                        target[z, place, yb * c : yb * (c + 1)] = taken[
                            turn, r * cols + c, :, at : at + yb
                        ]
            return carry

        lax.fori_loop(0, rows, one, 0)

    scatter(0, wave)
    stack[zb:] = jnp.zeros((8 - zb, nc, nc), jnp.float32)
    pl.semaphore_wait(barrier, devices - 1)
    launch(0)
    scatter(1, trap)
    launch(1)
    arrive(0)
    gather(0, field)

    def left(matrix, values):
        return product_with(pair_of(matrix), halves(values), ((1,), (0,)))

    def right(values, matrix):
        return product_with(halves(values), pair_of(matrix), ((1,), (0,)))

    def forward(z, carry):
        evolved = right(left(evolve, field[z]), evolve)
        field[z] = evolved
        stack[z] = right(left(cas, evolved * evolved), cas)
        return carry

    lax.fori_loop(0, zb, forward, 0)
    turned = jnp.transpose(stack[...], (1, 0, 2)).reshape(nc // 2, 2, 8, nc)
    for e in range(2):
        sent[:, :, e * nc : (e + 1) * nc] = turned[:, e]
    launch(2)
    arrive(1)
    gather(1, well)
    arrive(2)
    for t in range(pairs):
        block = got[...].reshape(devices, pairs, 8, nf)[:, t].reshape(devices * 8, nf)
        values = left(deep, block)
        sq_x = [squared_wave(me * zb + 2 * t + e, nc, 2.0) for e in range(2)]
        lanes = lax.broadcasted_iota(jnp.int32, (1, 2 * nc), 1)
        squares = (jnp.where(lanes < nc, sq_x[0], sq_x[1]) + sq_y[...]) + sq_z[...]
        nonzero = jnp.where(squares > 0, squares, 1.0)
        weights = jnp.where(
            squares > 0, DIPOLE_STRENGTH * (3.0 * sq_z[...] - squares) / nonzero, 0.0
        )
        values = right(left(tall, values * (weights / volume)), twice)
        values = values.reshape(devices, 8, nf)
        for d in range(devices):
            back[pairs * d + t] = values[d]
    launch(3)
    arrive(3)
    folded[...] = jnp.transpose(home[...], (1, 0, 2))
    sums = jnp.zeros((8, nc), jnp.float32)
    for z in range(zb):
        square[...] = left(joint, folded[z])
        field_dd = square[:nc, :nc] + square[nc:, nc:]
        evolved = field[z]
        exponent = well[z] + CONTACT * (evolved * evolved) + field_dd
        damped = jnp.exp(-TIME_STEP * exponent) * evolved
        sums += jnp.sum((damped * damped).reshape(nc // 8, 8, nc), axis=0)
        mate_sent[z // 2, :, z % 2 * nc : (z % 2 + 1) * nc] = damped
        if z % 2:
            to_mate(z // 2).start()
    partial[...] = jnp.full(partial.shape, jnp.sum(sums), jnp.float32)
    launch(4)

    def raise_pair(slot, z, planes):
        for e in range(2):
            half = halves(planes[z, :, e * nc : (e + 1) * nc])
            high = product_with(pair_of(lift), half, ((1,), (1,)))
            lifted[slot, z, :, e * nc : (e + 1) * nc] = high

    for z in range(pairs):
        raise_pair(0, z, mate_sent)
    spread_out(range(5, 5 + strips))
    for z in range(pairs):
        to_mate(z).wait_recv()
        raise_pair(1, z, mate_got)
        first = 5 + strips + z * strips
        spread_out(range(first, first + strips))
    arrive(4)
    scale[...] = lax.rsqrt(jnp.sum(partials[...], axis=0) / volume + EPSILON)
    last = 5 + strips * (1 + pairs)

    def landed(step, carry):
        for turn in range(5, last):
            spread(turn, step).wait()
        return carry

    lax.fori_loop(1, middle * cols, landed, 0)
    for turn in range(5, last):
        spread_own(turn).wait()
    for z in range(pairs):
        to_mate(z).wait_send()

    def settle(step, carry):
        for turn in range(5):
            copy(turn, step).wait_send()
        return carry

    lax.fori_loop(1, devices, settle, 0)


def coarse_step(exchange, wave, potential, evolve, lift):
    sizes = exchange.sizes
    rows, cols = sizes["rows"], sizes["cols"]
    devices = rows * cols
    xb, yb, nc = wave.shape
    nf = lift.shape[1]
    zb, yf, pairs = nc // devices, 2 * nf // devices, nc // devices // 2
    cas = cas_table(np.arange(nc), nc)
    deep = np.pad(cas.reshape(nc, devices, zb), ((0, 0), (0, 0), (0, 8 - zb))).reshape(nc, -1)
    twice = np.kron(np.eye(2), cas)
    joint = np.concatenate([cas[:, 0::2], cas[:, 1::2]])
    every = squared_waves(nc, 2.0).astype(np.float32)
    operands = [wave, potential, split(evolve), split(cas), split(deep), split(deep.T)]
    operands += [split(twice), split(joint), split(lift.T)]
    operands += [np.tile(every, 2)[None, :], every[:, None]]
    exchange.calls += 1
    vmem, hbm = pl.BlockSpec(memory_space=pltpu.VMEM), pl.BlockSpec(memory_space=pl.ANY)
    f32 = jnp.float32
    lanes = zb * xb // 8 * yb
    half = (nc // 2, 8, 2 * nc)
    turns = 5 + yf // 8 * (1 + pairs)
    return pl.pallas_call(
        functools.partial(coarse_kernel, sizes, float(nc) ** 3),
        out_shape=[
            jax.ShapeDtypeStruct((nc // 2, yf, 2 * nc), f32),
            jax.ShapeDtypeStruct((8, 128), f32),
        ],
        in_specs=[vmem] * len(operands),
        out_specs=[hbm, vmem],
        scratch_shapes=[
            pltpu.VMEM((8, nc, yb), f32),
            pltpu.VMEM((2, devices, 8, lanes), f32),
            pltpu.VMEM((2, devices, 8, lanes), f32),
            pltpu.VMEM((zb, nc, nc), f32),
            pltpu.VMEM((zb, nc, nc), f32),
            pltpu.VMEM((8, nc, nc), f32),
            pltpu.VMEM(half, f32),
            pltpu.VMEM(half, f32),
            pltpu.VMEM(half, f32),
            pltpu.VMEM(half, f32),
            pltpu.VMEM((8, nc // 2, 2 * nc), f32),
            pltpu.VMEM((2, pairs, nf, 2 * nc), f32),
            pltpu.VMEM((2 * nc, 2 * nc), f32),
            pltpu.VMEM((8, 128), f32),
            pltpu.VMEM((devices, 8, 128), f32),
            pltpu.VMEM((pairs, nc, 2 * nc), f32),
            pltpu.VMEM((pairs, nc, 2 * nc), f32),
            pltpu.SemaphoreType.DMA((turns, devices)),
            pltpu.SemaphoreType.DMA((turns, devices)),
            pltpu.SemaphoreType.DMA((turns,)),
            pltpu.SemaphoreType.DMA((pairs,)),
            pltpu.SemaphoreType.DMA((pairs,)),
        ],
        compiler_params=pltpu.CompilerParams(
            collective_id=exchange.calls - 1,
            has_side_effects=True,
            vmem_limit_bytes=60 * 1024 * 1024,
        ),
        name=f"coarse_{exchange.calls - 1}",
    )(*operands)


def per_device(sizes, wave_coarse, potential_coarse, potential_fine):
    devices = sizes["rows"] * sizes["cols"]
    nc, nf = wave_coarse.shape[2], potential_fine.shape[2]
    exchange = Exchanger(sizes)

    positions = np.arange(nc)
    coarse_matrix = cas_table(positions, nc)
    decay = np.exp(-0.5 * TIME_STEP * squared_waves(nc, 2.0))[:, None] / nc
    evolve = coarse_matrix @ (decay * coarse_matrix)
    padded = np.where(positions < nc // 2, positions, positions + nc)
    lift = coarse_matrix @ (decay * cas_table(padded, 2 * nc))

    slab, scale = coarse_step(exchange, wave_coarse, potential_coarse, evolve, lift)
    return fine_step(exchange, slab, scale, lift, potential_fine)


def fits_slabs(sizes, nc, nf):
    rows, cols = sizes["rows"], sizes["cols"]
    devices = rows * cols
    if rows % 2 or cols % 2 or nc % devices or nf % (8 * devices // 2) or nf % (4 * devices):
        return False
    if nc // rows % 8 or nc // devices > 8 or nc // devices % 2:
        return False
    return nf % (8 * rows) == 0 and nf % 128 == 0 and nf // devices % 8 == 4 and 2 * nc == nf


def solution(mesh):
    sizes = {"rows": mesh.shape["rows"], "cols": mesh.shape["cols"]}
    placed = (P("rows", "cols", None), P("rows", "cols", None), P("cols", "rows", None))

    def run(wave_coarse, potential_coarse, potential_fine):
        nc, nf = wave_coarse.shape[0], potential_fine.shape[0]
        body = per_device if fits_slabs(sizes, nc, nf) else per_device_pencils
        return jax.shard_map(
            functools.partial(body, sizes),
            mesh=mesh,
            in_specs=placed,
            out_specs=P("cols", "rows", None),
            check_vma=False,
        )(wave_coarse, potential_coarse, potential_fine)

    return run
```

```python
import functools
import math

import jax
import jax.numpy as jnp
import ml_dtypes
import numpy as np
from jax import lax
from jax.experimental import pallas as pl
from jax.experimental.pallas import tpu as pltpu
from jax.sharding import PartitionSpec as P

TIME_STEP = 0.5
CONTACT = 0.4
DIPOLE_STRENGTH = 0.3
EPSILON = 1e-06
HIGH = lax.Precision.HIGH
HIGHEST = lax.Precision.HIGHEST
MESH = pl.DeviceIdType.MESH


def cas_values(product, length):
    phases = 2.0 * math.pi / length * (product % length).astype(jnp.float32)
    return jnp.cos(phases) + jnp.sin(phases)


def cas_matrix(length):
    positions = jnp.arange(length, dtype=jnp.int32)
    return cas_values(positions[:, None] * positions[None, :], length)


def lift_matrix(length):
    positions = jnp.arange(length, dtype=jnp.int32)
    lifted = jnp.where(positions < length // 2, positions, positions + length)
    fine_points = jnp.arange(2 * length, dtype=jnp.int32)
    return cas_values(lifted[:, None] * fine_points[None, :], 2 * length)


def wavenumbers(length, block_count, offset, spacing):
    positions = offset + jnp.arange(block_count, dtype=jnp.int32)
    signed = jnp.where(positions < length // 2, positions, positions - length)
    return 2.0 * math.pi / (length * spacing) * signed.astype(jnp.float32)


def dipolar_weights(along_x, along_y, along_z, length):
    squares = along_x + along_y + along_z
    nonzero = jnp.where(squares > 0, squares, 1.0)
    weights = jnp.where(squares > 0, DIPOLE_STRENGTH * (3.0 * along_z - squares) / nonzero, 0.0)
    return weights / float(length) ** 3


def exchange_kernel(axes, sizes, *refs):
    count = len(axes)
    sources, targets = refs[:count], refs[count : 2 * count]
    send_sems, recv_sems, local_sems = refs[2 * count :]
    row, col = lax.axis_index("rows"), lax.axis_index("cols")

    def place(axis, index):
        return (index, col) if axis == "rows" else (row, index)

    barrier = pltpu.get_barrier_semaphore()
    waits = 0
    for axis in sorted(set(axes)):
        size = sizes[axis]
        me = lax.axis_index(axis)
        for step in range(1, size):
            peer = lax.rem(me + step, size)
            pl.semaphore_signal(barrier, inc=1, device_id=place(axis, peer), device_id_type=MESH)
        waits += size - 1
    pl.semaphore_wait(barrier, waits)
    most = max(sizes[axis] for axis in axes)
    order = sorted(range(1, most), key=lambda step: abs(2 * step - most))
    copies = []
    for step in order:
        for index, axis in enumerate(axes):
            size = sizes[axis]
            if step >= size:
                continue
            me = lax.axis_index(axis)
            peer = lax.rem(me + step, size)
            copy = pltpu.make_async_remote_copy(
                src_ref=sources[index].at[peer],
                dst_ref=targets[index].at[me],
                send_sem=send_sems.at[index, step],
                recv_sem=recv_sems.at[index, step],
                device_id=place(axis, peer),
                device_id_type=MESH,
            )
            copy.start()
            copies.append(copy)
    for index, axis in enumerate(axes):
        me = lax.axis_index(axis)
        copy = pltpu.make_async_copy(
            sources[index].at[me], targets[index].at[me], local_sems.at[index]
        )
        copy.start()
        copies.append(copy)
    for copy in copies:
        copy.wait()


class Exchanger:
    def __init__(self, sizes):
        self.sizes = sizes
        self.calls = 0

    def __call__(self, *pairs):
        arrays = [array for array, _ in pairs]
        axes = tuple(axis for _, axis in pairs)
        most = max(self.sizes.values())
        count = len(arrays)
        self.calls += 1
        return pl.pallas_call(
            functools.partial(exchange_kernel, axes, self.sizes),
            out_shape=[jax.ShapeDtypeStruct(a.shape, a.dtype) for a in arrays],
            in_specs=[pl.BlockSpec(memory_space=pl.ANY)] * count,
            out_specs=[pl.BlockSpec(memory_space=pl.ANY)] * count,
            scratch_shapes=[
                pltpu.SemaphoreType.DMA((count, most)),
                pltpu.SemaphoreType.DMA((count, most)),
                pltpu.SemaphoreType.DMA((count,)),
            ],
            compiler_params=pltpu.CompilerParams(
                collective_id=self.calls - 1, has_side_effects=True
            ),
            name=f"exchange_{self.calls - 1}",
        )(*arrays)


def give(values, matrix, parts, precision=HIGH):
    if matrix is None:
        turned = jnp.transpose(values, (2, 0, 1))
    else:
        turned = jnp.einsum("abl,lk->kab", values, matrix, precision=precision)
    length, rows_extent, cols_extent = turned.shape
    return turned.reshape(parts, length // parts, rows_extent * cols_extent)


def take(received, axis, rows_extent):
    parts, block, area = received.shape
    cols_extent = area // rows_extent
    received = received.reshape(parts, block, rows_extent, cols_extent)
    if axis == "cols":
        return received.transpose(2, 1, 0, 3).reshape(rows_extent, block, parts * cols_extent)
    return received.transpose(1, 3, 0, 2).reshape(block, cols_extent, parts * rows_extent)


def apply(values, matrix, precision=HIGH):
    return jnp.einsum("abl,lk->abk", values, matrix, precision=precision)


def split_product(values, matrix):
    high = matrix.astype(jnp.bfloat16)
    low = (matrix - high.astype(jnp.float32)).astype(jnp.bfloat16)
    top = values.astype(jnp.bfloat16)
    rest = (values - top.astype(jnp.float32)).astype(jnp.bfloat16)
    product = functools.partial(jnp.dot, preferred_element_type=jnp.float32)
    return product(top, high) + (product(top, low) + product(rest, high))


def gather_pieces(received, held):
    parts, chunk = received.shape[0], held.shape[0]
    width = received.shape[2] // chunk
    for s in range(chunk):
        for p in range(parts):
            held[s, :, p * width : (p + 1) * width] = received[p, :, s * width : (s + 1) * width]


def scatter_pieces(held, sent):
    parts, chunk = sent.shape[0], held.shape[0]
    width = sent.shape[2] // chunk
    for s in range(chunk):
        for p in range(parts):
            sent[p, :, s * width : (s + 1) * width] = held[s, :, p * width : (p + 1) * width]


def assemble_kernel(received, matrix, out, held):
    gather_pieces(received, held)
    chunk, k, length = held.shape
    product = split_product(held[...].reshape(chunk * k, length), matrix[...])
    out[...] = product.reshape(out.shape)


def chunk_of(spectators, width, k):
    for chunk in range(1, spectators):
        if spectators % chunk == 0 and chunk * width % 128 == 0 and chunk * k >= 256:
            return chunk
    return spectators


def assemble(received, spectators, matrix):
    parts, k, area = received.shape
    chunk = chunk_of(spectators, area // spectators, k)
    length, points = matrix.shape
    if k % 8:
        held = received.reshape(parts, k, spectators, -1).transpose(2, 1, 0, 3)
        return apply(held.reshape(spectators, k, length), matrix)
    return pl.pallas_call(
        assemble_kernel,
        grid=(spectators // chunk,),
        in_specs=[
            pl.BlockSpec((parts, k, area // spectators * chunk), lambda i: (0, 0, i)),
            pl.BlockSpec((length, points), lambda i: (0, 0)),
        ],
        out_specs=pl.BlockSpec((chunk, k, points), lambda i: (i, 0, 0)),
        out_shape=jax.ShapeDtypeStruct((spectators, k, points), jnp.float32),
        scratch_shapes=[pltpu.VMEM((chunk, k, length), jnp.float32)],
    )(received, matrix)


def halves(values):
    high = values.astype(jnp.bfloat16)
    return high, (values - high.astype(jnp.float32)).astype(jnp.bfloat16)


def product_of(left, right):
    product = functools.partial(jnp.dot, preferred_element_type=jnp.float32)
    return product(left[0], right[0]) + (product(left[0], right[1]) + product(left[1], right[0]))


def planes_kernel(flows, sizes, chunks, volume, *refs):
    row, col = lax.axis_index("rows"), lax.axis_index("cols")

    def place(axis, index):
        return (index, col) if axis == "rows" else (row, index)

    matrix = refs[0]
    inputs = [refs[1 + 4 * i : 5 + 4 * i] for i in range(len(flows))]
    at = 1 + 4 * len(flows)
    outs = refs[at : at + len(flows)]
    at += len(flows)
    high, low = refs[at : at + 2]
    at += 2
    buffers = [refs[at + 9 * i : at + 9 * i + 9] for i in range(len(flows))]

    barrier = pltpu.get_barrier_semaphore()
    waits = 0
    for axis in sorted(set(axis for axis, _ in flows)):
        size = sizes[axis]
        me = lax.axis_index(axis)
        for step in range(1, size):
            peer = lax.rem(me + step, size)
            pl.semaphore_signal(barrier, inc=1, device_id=place(axis, peer), device_id_type=MESH)
        waits += size - 1
    high[...], low[...] = halves(matrix[...])
    pl.semaphore_wait(barrier, waits)

    def copies(flow, turn, c):
        axis, _ = flows[flow]
        size = sizes[axis]
        me = lax.axis_index(axis)
        sent, received = buffers[flow][2 * turn : 2 * turn + 2]
        send_sem, recv_sem = buffers[flow][4 + 2 * turn : 6 + 2 * turn]
        order = sorted(range(1, size), key=lambda step: abs(2 * step - size))
        for step in order:
            peer = lax.rem(me + step, size)
            yield pltpu.make_async_remote_copy(
                src_ref=sent.at[c, peer],
                dst_ref=received.at[c, me],
                send_sem=send_sem.at[c, step],
                recv_sem=recv_sem.at[c, step],
                device_id=place(axis, peer),
                device_id_type=MESH,
            )

    def launch(flow, turn, c):
        me = lax.axis_index(flows[flow][0])
        for copy in copies(flow, turn, c):
            copy.start()
        sent, received = buffers[flow][2 * turn : 2 * turn + 2]
        received[c, me] = sent[c, me]

    def lanes(area, c):
        if chunks == 1:
            return slice(None)
        return pl.ds(pl.multiple_of(c * (area // chunks), 128), area // chunks)

    def first(c, carry):
        for flow in range(len(flows)):
            source, sent = inputs[flow][0], buffers[flow][0]
            part = source[:, :, lanes(source.shape[2], c)]
            part = part.reshape(matrix.shape[0], part.shape[2])
            product = product_of((high[...], low[...]), halves(part))
            sent[c] = product.reshape(sent.shape[1:])
            launch(flow, 0, c)
        return carry

    def second(c, carry):
        for flow in range(len(flows)):
            _, sq_s, sq_k, sq_l = inputs[flow]
            vertical = flows[flow][1]
            held = buffers[flow][8]
            chunk, k, length = held.shape
            for copy in copies(flow, 0, c):
                copy.wait_recv()
            gather_pieces(buffers[flow][1].at[c], held)
            both = (high[...], low[...])
            values = product_of(halves(held[...].reshape(chunk * k, length)), both)
            parts = [sq_s[pl.ds(c * chunk, chunk)], sq_k[...][None], sq_l[...][None]]
            parts = [jnp.broadcast_to(part, held.shape) for part in parts]
            squares = parts[0] + parts[1] + parts[2]
            nonzero = jnp.where(squares > 0, squares, 1.0)
            weights = jnp.where(
                squares > 0, DIPOLE_STRENGTH * (3.0 * parts[vertical] - squares) / nonzero, 0.0
            )
            values = values * (weights / volume).reshape(chunk * k, length)
            held[...] = product_of(halves(values), both).reshape(held.shape)
            scatter_pieces(held, buffers[flow][2].at[c])
            launch(flow, 1, c)
        return carry

    def third(c, carry):
        for flow in range(len(flows)):
            for copy in copies(flow, 1, c):
                copy.wait_recv()
            received, out = buffers[flow][3], outs[flow]
            part = received[c].reshape(matrix.shape[0], received.shape[3])
            product = product_of((high[...], low[...]), halves(part))
            out[:, lanes(out.shape[1], c)] = product
            for turn in range(2):
                for copy in copies(flow, turn, c):
                    copy.wait_send()
        return carry

    for stage in (first, second, third):
        lax.fori_loop(0, chunks, stage, 0)


def planes(exchange, flows, matrix):
    sizes = exchange.sizes
    length = matrix.shape[0]
    counts = []
    for axis, _, received, sq_s, sq_k, _ in flows:
        spectators = sq_s.shape[0]
        width = received.shape[2] // spectators
        counts.append(spectators // chunk_of(spectators, width, sq_k.shape[0]))
    chunks = counts[0] if len(set(counts)) == 1 else 1
    operands, outs, scratch = [matrix], [], []
    scratch += [pltpu.VMEM((length, length), jnp.bfloat16)] * 2
    for axis, _, received, sq_s, sq_k, sq_l in flows:
        operands += [received, sq_s[:, None, None], sq_k[:, None], sq_l[None, :]]
        area, k, size = received.shape[2], sq_k.shape[0], sizes[axis]
        outs.append(jax.ShapeDtypeStruct((length, area), jnp.float32))
        scratch += [pltpu.VMEM((chunks, size, k, area // chunks), jnp.float32)] * 4
        scratch += [pltpu.SemaphoreType.DMA((chunks, size))] * 4
        scratch += [pltpu.VMEM((sq_s.shape[0] // chunks, k, length), jnp.float32)]
    exchange.calls += 1
    vmem = pl.BlockSpec(memory_space=pltpu.VMEM)
    return pl.pallas_call(
        functools.partial(
            planes_kernel,
            tuple((flow[0], flow[1]) for flow in flows),
            sizes,
            chunks,
            float(length) ** 3,
        ),
        out_shape=outs,
        in_specs=[vmem] * len(operands),
        out_specs=[vmem] * len(outs),
        scratch_shapes=scratch,
        compiler_params=pltpu.CompilerParams(
            collective_id=exchange.calls - 1,
            has_side_effects=True,
            vmem_limit_bytes=60 * 1024 * 1024,
        ),
        name=f"planes_{exchange.calls - 1}",
    )(*operands)


def blocks(turned, parts):
    first, length, last = turned.shape
    turned = turned.reshape(first, parts, length // parts, last).transpose(1, 0, 2, 3)
    return turned.reshape(parts, first, length // parts * last)


def product_blocks(matrix, received, parts):
    turned = jnp.dot(matrix, received.reshape(-1, received.shape[2]), precision=HIGH)
    return turned.reshape(parts, turned.shape[0] // parts, turned.shape[1])


def per_device_pencils(sizes, wave_coarse, potential_coarse, potential_fine):
    row, col = lax.axis_index("rows"), lax.axis_index("cols")
    rows, cols = sizes["rows"], sizes["cols"]
    nc, nf = wave_coarse.shape[2], potential_fine.shape[2]
    exchange = Exchanger(sizes)

    coarse_matrix = cas_matrix(nc)
    fine_matrix = cas_matrix(nf)
    decay = jnp.exp(-0.5 * TIME_STEP * wavenumbers(nc, nc, 0, 2.0) ** 2)[:, None] / nc
    evolve = jnp.dot(coarse_matrix, decay * coarse_matrix, precision=HIGHEST)
    lift = jnp.dot(coarse_matrix, decay * lift_matrix(nc), precision=HIGHEST)

    xr = yr = nc // rows
    spectators = nc // cols
    turned = jnp.einsum("xyz,zk->ykx", wave_coarse, evolve, precision=HIGH)
    (got,) = exchange((blocks(turned, cols), "cols"))
    (got,) = exchange((product_blocks(evolve.T, got, rows), "rows"))
    evolved = assemble(got, spectators, evolve)
    turned = jnp.einsum("zyx,xk->zky", evolved * evolved, coarse_matrix, precision=HIGH)
    got, back = exchange(
        (blocks(turned, cols), "cols"), (give(evolved.transpose(1, 0, 2), None, rows), "rows")
    )
    back = take(back, "rows", yr)
    got, back = exchange(
        (product_blocks(coarse_matrix, got, rows), "rows"), (give(back, None, cols), "cols")
    )
    spectrum, evolved = assemble(got, spectators, coarse_matrix), take(back, "cols", xr)
    z_block, x_block = nc // rows, nc // cols
    weights = dipolar_weights(
        wavenumbers(nc, x_block, col * x_block, 2.0)[:, None, None] ** 2,
        wavenumbers(nc, nc, 0, 2.0)[None, None, :] ** 2,
        wavenumbers(nc, z_block, row * z_block, 2.0)[None, :, None] ** 2,
        nc,
    )
    turned = jnp.einsum("xzy,yk->xkz", weights * spectrum, coarse_matrix, precision=HIGH)
    (got,) = exchange((blocks(turned, cols), "cols"))
    (got,) = exchange((product_blocks(coarse_matrix, got, rows), "rows"))
    field_dd = assemble(got, spectators, coarse_matrix).transpose(1, 0, 2)
    density = evolved * evolved
    damped = jnp.exp(-TIME_STEP * (potential_coarse + CONTACT * density + field_dd)) * evolved
    partial_sum = jnp.sum(damped * damped)

    got, sums = exchange(
        (blocks(jnp.einsum("xyz,zk->ykx", damped, lift, precision=HIGH), cols), "cols"),
        (jnp.full((cols, 8, 128), partial_sum, jnp.float32), "cols"),
    )
    partial_sum = jnp.sum(sums[:, 0, 0])
    got, sums = exchange(
        (product_blocks(lift.T, got, rows), "rows"),
        (jnp.full((rows, 8, 128), partial_sum, jnp.float32), "rows"),
    )
    scale = lax.rsqrt(jnp.sum(sums[:, 0, 0]) / float(nc) ** 3 + EPSILON)
    evolved = assemble(got, nf // cols, lift) * scale

    density = evolved * evolved
    half = nf // 2
    near, far = fine_matrix[:, :half], fine_matrix[:, half:]
    got_near, got_far = exchange(
        (blocks(jnp.einsum("zyx,xk->ykz", density, near, precision=HIGH), rows), "rows"),
        (blocks(jnp.einsum("zyx,xk->zky", density, far, precision=HIGH), cols), "cols"),
    )
    y_block, z_block = nf // cols, nf // rows
    near_block, far_block = half // rows, half // cols
    every = wavenumbers(nf, nf, 0, 1.0) ** 2
    near_flow = (
        "cols",
        2,
        got_near,
        wavenumbers(nf, near_block, row * near_block, 1.0) ** 2,
        wavenumbers(nf, y_block, col * y_block, 1.0) ** 2,
        every,
    )
    far_flow = (
        "rows",
        1,
        got_far,
        wavenumbers(nf, far_block, half + col * far_block, 1.0) ** 2,
        wavenumbers(nf, z_block, row * z_block, 1.0) ** 2,
        every,
    )
    got_far, got_near = planes(exchange, (far_flow, near_flow), fine_matrix)
    got_near, got_far = exchange(
        (got_near.reshape(rows, nf // rows, -1), "rows"),
        (got_far.reshape(cols, nf // cols, -1), "cols"),
    )
    z_extent, y_extent = nf // cols, nf // rows
    near_field = got_near.reshape(rows, y_extent, near_block, z_extent)
    near_field = near_field.transpose(3, 1, 0, 2).reshape(z_extent, y_extent, half)
    far_field = got_far.reshape(cols, z_extent, far_block, y_extent)
    far_field = far_field.transpose(1, 3, 0, 2).reshape(z_extent, y_extent, half)
    spectrum = jnp.concatenate([near_field, far_field], axis=2)
    field_dd = jnp.einsum("zyk,kx->zyx", spectrum, fine_matrix, precision=HIGH)
    damped = jnp.exp(-TIME_STEP * (potential_fine + CONTACT * density + field_dd)) * evolved
    total = jnp.sum(damped * damped)
    for axis in ("rows", "cols"):
        (sums,) = exchange((jnp.full((sizes[axis], 8, 128), total, jnp.float32), axis))
        total = jnp.sum(sums[:, 0, 0])
    return damped * lax.rsqrt(total / float(nf) ** 3 + EPSILON)


def strip_of(row, col, t, rows, cols, count):
    middle, odd = rows // 2, lax.rem(row, 2)
    first = (count * col + 1 - odd) // 2
    own = own_strips(row, col, count)
    other = (count * col + odd) // 2
    away = lax.rem(row + middle, rows)
    block = count * cols // 2
    return jnp.where(t < own, row * block + first + t, away * block + other + t - own)


def far_first(turn, count):
    return count // 2 + (1 - 2 * lax.rem(turn, 2)) * ((turn + 1) // 2)


def own_strips(row, col, count):
    odd = lax.rem(row, 2)
    return (count * (col + 1) + 1 - odd) // 2 - (count * col + 1 - odd) // 2


def split(matrix):
    high = matrix.astype(np.float32).astype(ml_dtypes.bfloat16)
    low = (matrix - high.astype(np.float64)).astype(np.float32).astype(ml_dtypes.bfloat16)
    return np.stack([high, low])


def cas_table(rows, length):
    product = np.outer(rows, np.arange(length, dtype=np.int64)) % length
    phases = 2.0 * np.pi / length * product
    return np.cos(phases) + np.sin(phases)


def squared_waves(length, spacing):
    positions = np.arange(length)
    signed = np.where(positions < length // 2, positions, positions - length)
    return (2.0 * np.pi / (length * spacing) * signed) ** 2


def squared_wave(position, length, spacing):
    signed = jnp.where(position < length // 2, position, position - length)
    wave = signed.astype(jnp.float32) * (2.0 * math.pi / (length * spacing))
    return wave * wave


def pair_of(ref, *index):
    return ref[(*index, 0)], ref[(*index, 1)]


def product_with(left, right, contract):
    def product(a, b):
        return lax.dot_general(a, b, (contract, ((), ())), preferred_element_type=jnp.float32)

    return product(left[0], right[0]) + (product(left[0], right[1]) + product(left[1], right[0]))


def fine_kernel(sizes, volume, *refs):
    slab, scale, rise, lift, near, last, cas, spread, rolled, sq_y, sq_z = refs[:11]
    packed, taken = refs[11:13]
    raw, lines, plane, shares, given, planes, sent, got, stage, turned, packing = refs[13:24]
    load_sem, send_sem, recv_sem, out_sem, in_sem, own_sem = refs[24:30]
    give_sem, take_sem = refs[30:32]
    rows, cols = sizes["rows"], sizes["cols"]
    row, col = lax.axis_index("rows"), lax.axis_index("cols")
    me, middle = row * cols + col, rows // 2
    base, local = row // middle * middle, lax.rem(row, middle)
    slabs = middle * cols
    kb, nf = got.shape[0], got.shape[1]
    yf = nf // slabs
    steps, rounds = raw.shape[0], packed.shape[1]
    part, width = yf // steps, kb // rounds
    nc, depth = plane.shape[1], lines.shape[1]
    share = given.shape[0] // cols
    parity = row // middle
    sign = (1 - 2 * parity).astype(jnp.float32)
    own = own_strips(row, col, steps)
    first_strip = lax.rem(strip_of(row, col, 0, rows, cols, steps), taken.shape[0])

    def place_of(t):
        return pl.ds(pl.multiple_of(8 * strip_of(row, col, t, rows, cols, steps), 8), 8)

    def load(t):
        return pltpu.make_async_copy(
            slab.at[:, pl.ds(pl.multiple_of(t * part, 8), part)], raw.at[t], load_sem.at[t]
        )

    for t in range(steps):
        load(t).start()

    barrier = pltpu.get_barrier_semaphore()

    def greet(step, carry):
        peer = lax.rem(me + step, rows * cols)
        pl.semaphore_signal(
            barrier, inc=1, device_id=(peer // cols, lax.rem(peer, cols)), device_id_type=MESH
        )
        return carry

    lax.fori_loop(1, rows * cols, greet, 0)

    def forward(chunk, t, step):
        r = lax.rem(local + step // cols, middle)
        c = lax.rem(col + lax.rem(step, cols), cols)
        first = (r * cols + c) * kb + chunk * width
        return pltpu.make_async_remote_copy(
            src_ref=sent.at[pl.ds(first, width), pl.ds(pl.multiple_of(t * part, 8), part)],
            dst_ref=got.at[pl.ds(chunk * width, width), place_of(t)],
            send_sem=send_sem.at[chunk, t, step],
            recv_sem=recv_sem.at[chunk, t, step],
            device_id=(base + r, c),
            device_id_type=MESH,
        )

    def launch(chunk, t):
        def start(index, carry):
            forward(chunk, t, far_first(index, slabs)).start()
            return carry

        lax.fori_loop(0, slabs - 1, start, 0)
        first = (local * cols + col) * kb + chunk * width
        got[pl.ds(chunk * width, width), place_of(t), :] = sent[
            pl.ds(first, width), pl.ds(pl.multiple_of(t * part, 8), part), :
        ]

    def front(t, carry):
        load(t).wait()
        lines[...] = jnp.transpose(raw[t], (1, 0, 2))

        def line(y, carry):
            for e in range(2):
                plane[e * depth : (e + 1) * depth] = lines[y, :, e * nc : (e + 1) * nc]
            high = product_with(pair_of(rise), halves(plane[...]), ((1,), (0,))) * scale[:1, :1]
            for e in range(2):
                shares[y, :, e * nc : (e + 1) * nc] = high[e * nc : (e + 1) * nc]
            field = product_with(pair_of(lift), halves(high), ((1,), (1,)))
            density = field * field
            density = halves(density[:nc] + sign * density[nc:])
            along_x = product_with(pair_of(near, parity), density, ((1,), (0,)))
            planes[y] = product_with(halves(along_x), pair_of(last), ((1,), (0,)))
            return carry

        lax.fori_loop(0, part, line, 0)
        place = pl.ds(pl.multiple_of(t * part, 8), part)
        sent[:, place, :] = jnp.transpose(planes[...], (1, 0, 2))

        @pl.when(t < given.shape[1] // 8)
        def _():
            given[:, place, :] = jnp.transpose(shares[...], (1, 0, 2))

        @pl.when(t == 0)
        def _():
            pl.semaphore_wait(barrier, rows * cols - 1)

        launch(0, t)
        launch(1, t)

        @pl.when(t > 0)
        def _():
            launch(2, t - 1)
            launch(3, t - 1)

        return carry

    lax.fori_loop(0, steps, front, 0)

    launch(2, steps - 1)
    launch(3, steps - 1)

    def later(index, carry):
        launch(4 + index // steps, lax.rem(index, steps))
        return carry

    lax.fori_loop(0, (rounds - 4) * steps, later, 0)

    def give(t, step):
        c = lax.rem(col + step, cols)
        return pltpu.make_async_remote_copy(
            src_ref=given.at[pl.ds(c * share, share), 8 * t : 8 * t + 8],
            dst_ref=taken.at[first_strip + t],
            send_sem=give_sem.at[t, step],
            recv_sem=take_sem.at[first_strip + t],
            device_id=(row, c),
            device_id_type=MESH,
        )

    def keep(t):
        return pltpu.make_async_copy(
            given.at[pl.ds(col * share, share), 8 * t : 8 * t + 8],
            taken.at[first_strip + t],
            give_sem.at[t, 0],
        )

    def give_all():
        for t in range(given.shape[1] // 8):

            @pl.when(t < own)
            def _():
                for step in range(1, cols):
                    give(t, step).start()
                keep(t).start()

    def inverse(chunk, r, c):
        return pltpu.make_async_remote_copy(
            src_ref=packing.at[r, c, chunk],
            dst_ref=packed.at[me, chunk],
            send_sem=out_sem.at[chunk, r, c],
            recv_sem=in_sem.at[chunk, me],
            device_id=(r, c),
            device_id_type=MESH,
        )

    def stay(chunk):
        return pltpu.make_async_copy(
            packing.at[row, col, chunk], packed.at[me, chunk], own_sem.at[chunk]
        )

    zi = turned.shape[3] // 2
    yo = nf // rows

    def convolve(chunk, carry):
        def arrive(index, carry):
            t, step = index // slabs, lax.rem(index, slabs)

            @pl.when(step != 0)
            def _():
                forward(chunk, t, step).wait_recv()

            return carry

        lax.fori_loop(0, steps * slabs, arrive, 0)

        def couple(kp, carry):
            parts = []
            for b in range(2):
                k = chunk * width + 2 * kp + b
                top, bottom = got[k, : nf // 2], got[k, nf // 2 :]
                values = jnp.concatenate(
                    [
                        product_with(pair_of(cas, 0), halves(top + bottom), ((1,), (0,))),
                        product_with(pair_of(cas, 1), halves(top - bottom), ((1,), (0,))),
                    ]
                )
                sq_x = squared_wave(2 * ((local * cols + col) * kb + k) + parity, nf, 1.0)
                squares = (sq_x + sq_y[...]) + sq_z[...]
                nonzero = jnp.where(squares > 0, squares, 1.0)
                weights = jnp.where(
                    squares > 0, DIPOLE_STRENGTH * (3.0 * sq_z[...] - squares) / nonzero, 0.0
                )
                values = halves(values * (weights / volume))
                along_z = product_with(pair_of(spread, b), values, ((1,), (1,)))
                parts.append(along_z.reshape(rows, cols, -1, nf))
            turned[:, :, kp] = jnp.concatenate(
                [parts[0][:, :, :-8], parts[0][:, :, -8:] + parts[1][:, :, :8], parts[1][:, :, 8:]],
                axis=2,
            )
            return carry

        lax.fori_loop(0, width // 2, couple, 0)

        def roll(j, carry):
            block = turned[j].reshape(-1, nf)
            stage[j] = product_with(halves(block), pair_of(rolled, j), ((1,), (0,)))
            return carry

        lax.fori_loop(0, rows, roll, 0)

        def pack(index, carry):
            step = far_first(index, rows)
            r = lax.rem(row + step, rows)
            for tile in range(nf // 128):
                lanes = lax.broadcasted_iota(jnp.int32, (1, 128), 1) + 128 * tile
                first, last = 128 * tile // yo, (128 * tile + 127) // yo
                value = None
                for p in range(last, first - 1, -1):
                    j = lax.rem(p - r + rows, rows)
                    block = stage[j, :, 128 * tile : 128 * tile + 128]
                    value = block if value is None else jnp.where(lanes < (p + 1) * yo, block, value)
                value = value.reshape(cols, width // 2, 2 * zi, 128)
                for c in range(cols):
                    packing[r, c, chunk, :, tile] = value[c]
            for b in range(cols - 1, -1, -1):
                c = lax.rem(col + b, cols)
                if b:
                    inverse(chunk, r, c).start()
                else:

                    @pl.when(step != 0)
                    def _():
                        inverse(chunk, r, c).start()

                    @pl.when(step == 0)
                    def _():
                        stay(chunk).start()

            return carry

        lax.fori_loop(0, rows, pack, 0)

        @pl.when(chunk == 0)
        def _():
            give_all()

        return carry

    lax.fori_loop(0, rounds, convolve, 0)

    def finish(chunk, carry):
        stay(chunk).wait()

        def one(source, carry):
            @pl.when(source != me)
            def _():
                r, c = source // cols, lax.rem(source, cols)
                pltpu.make_async_remote_copy(
                    src_ref=packing.at[r, c, chunk],
                    dst_ref=packed.at[source, chunk],
                    send_sem=out_sem.at[chunk, r, c],
                    recv_sem=in_sem.at[chunk, source],
                    device_id=(r, c),
                    device_id_type=MESH,
                ).wait()

            return carry

        lax.fori_loop(0, rows * cols, one, 0)

        def left(index, carry):
            t, step = index // slabs, lax.rem(index, slabs)

            @pl.when(step != 0)
            def _():
                forward(chunk, t, step).wait_send()

            return carry

        lax.fori_loop(0, steps * slabs, left, 0)
        return carry

    lax.fori_loop(0, rounds, finish, 0)

    for t in range(given.shape[1] // 8):

        @pl.when(t < own)
        def _():
            for step in range(1, cols):
                give(t, step).wait_send()
            keep(t).wait()

    for strip in range(taken.shape[0]):
        source = (2 * strip + lax.rem(row, 2)) // steps

        @pl.when(col != source)
        def _():
            pltpu.make_async_remote_copy(
                src_ref=given.at[pl.ds(col * share, share), 0:8],
                dst_ref=taken.at[strip],
                send_sem=give_sem.at[0, 0],
                recv_sem=take_sem.at[strip],
                device_id=(row, source),
                device_id_type=MESH,
            ).wait_recv()


def out_kernel(sizes, volume, *refs):
    packed, cas, lift, taken, trap, damped, scale, fields, folded, total, partial, partials = refs[:12]
    send_sem, recv_sem = refs[12:]
    i = pl.program_id(0)
    rows, cols = sizes["rows"], sizes["cols"]
    row, col = lax.axis_index("rows"), lax.axis_index("cols")
    devices, me = rows * cols, row * cols + col
    zi, nf = pl.num_programs(0), trap.shape[3]
    nc = nf // 2
    barrier = pltpu.get_barrier_semaphore()

    @pl.when(i == 0)
    def _():
        def greet(step, carry):
            peer = lax.rem(me + step, devices)
            pl.semaphore_signal(
                barrier, inc=1, device_id=(peer // cols, lax.rem(peer, cols)), device_id_type=MESH
            )
            return carry

        lax.fori_loop(1, devices, greet, 0)

    strips = taken.shape[0]
    block = taken[:, :, 0].reshape(strips * rows * 8, nf)
    block = halves(jnp.where(i < zi // 2, block[:, :nc], block[:, nc:]))
    block = product_with(block, pair_of(lift), ((1,), (0,)))
    block = block.reshape(strips, rows, 8, nf)
    for strip in range(strips):
        fields[:, 8 * strip : 8 * strip + 8, :] = block[strip]
    tiles = nf // 128
    run = tiles * 2 * zi
    columns = [[], []]
    for tile in range(tiles):
        pieces = [packed[pl.ds(tile * 2 * zi + b * zi + i, nc, stride=run), :] for b in range(2)]
        columns[0].append(jnp.concatenate([piece[: nc // 2] for piece in pieces], axis=0))
        columns[1].append(jnp.concatenate([piece[nc // 2 :] for piece in pieces], axis=0))
    even, odd = [
        product_with(
            halves(jnp.concatenate(columns[p], axis=1)), pair_of(cas, p), ((0,), (0,))
        )
        for p in range(2)
    ]
    folded[:, :nc] = even + odd
    folded[:, nc:] = even - odd
    yo = nf // rows
    squares = jnp.zeros((8, nf), jnp.float32)
    for p in range(rows):
        j = lax.rem(p - row + rows, rows)
        evolved = fields[j]
        exponent = trap[j, 0] + CONTACT * (evolved * evolved) + folded[p * yo : (p + 1) * yo]
        result = jnp.exp(-TIME_STEP * exponent) * evolved
        damped[j, 0] = result
        squares += jnp.sum((result * result).reshape(yo // 8, 8, nf), axis=0)

    @pl.when(i == 0)
    def _():
        total[...] = squares

    @pl.when(i > 0)
    def _():
        total[...] += squares

    def copy(step):
        peer = lax.rem(me + step, devices)
        return pltpu.make_async_remote_copy(
            src_ref=partial,
            dst_ref=partials.at[me],
            send_sem=send_sem.at[step],
            recv_sem=recv_sem.at[step],
            device_id=(peer // cols, lax.rem(peer, cols)),
            device_id_type=MESH,
        )

    @pl.when(i == zi - 1)
    def _():
        partial[...] = jnp.full(partial.shape, jnp.sum(total[...]), jnp.float32)
        pl.semaphore_wait(barrier, devices - 1)

        def start(step, carry):
            copy(step).start()
            return carry

        def wait(step, carry):
            copy(step).wait()
            return carry

        lax.fori_loop(1, devices, start, 0)
        partials[me] = partial[...]
        lax.fori_loop(1, devices, wait, 0)
        scale[...] = lax.rsqrt(jnp.sum(partials[...], axis=0) / volume + EPSILON)


def fine_step(exchange, slab, scale, lift, potential):
    sizes = exchange.sizes
    rows, cols = sizes["rows"], sizes["cols"]
    devices = rows * cols
    nc, nf = lift.shape
    depth, yf = slab.shape[:2]
    kb = nf // devices
    yo, zo = nf // rows, nf // cols
    zi = zo // rows
    steps, rounds = yf // 8, kb // 2
    width, tiles = kb // rounds, nf // 128
    natural = np.arange(nf)
    waves = np.concatenate([natural[0::2], natural[1::2]])
    fine_matrix = cas_table(natural, nf)
    order = fine_matrix.reshape(cols, rows, zi, nf).transpose(1, 0, 2, 3)
    spread = [
        split(np.pad(order, ((0, 0), (0, 0), pads, (0, 0))).reshape(-1, nf))
        for pads in ((0, -zi % 8), (-zi % 8, 0))
    ]
    rolled = np.stack([split(np.roll(fine_matrix[waves], yo * j, axis=1)) for j in range(rows)])
    slabs = nf // yf
    shape = (cols, rows, 2, zi // 2)
    rise = lift.reshape((nc // 2, 2) + shape).transpose(4, 2, 3, 5, 1, 0).reshape(nf, nc)
    last = fine_matrix.reshape(shape + (nf,)).transpose(2, 0, 1, 3, 4).reshape(nf, nf)
    every = squared_waves(nf, 1.0).astype(np.float32)
    folded = np.stack([split(fine_matrix[parity::2, : nf // 2]) for parity in range(2)])
    operands = [
        slab,
        scale,
        split(rise),
        split(lift.T),
        folded,
        split(last),
        folded,
        np.stack(spread),
        rolled,
        every[waves][:, None],
        every[None, :],
    ]
    exchange.calls += 1
    vmem, hbm = pl.BlockSpec(memory_space=pltpu.VMEM), pl.BlockSpec(memory_space=pl.ANY)
    f32 = jnp.float32
    packed, taken = pl.pallas_call(
        functools.partial(fine_kernel, sizes, float(nf) ** 3),
        out_shape=[
            jax.ShapeDtypeStruct((devices, rounds, width // 2, tiles, 2 * zi, 128), f32),
            jax.ShapeDtypeStruct((yo // 8, nc // cols, 8, nf), f32),
        ],
        in_specs=[hbm] + [vmem] * (len(operands) - 1),
        out_specs=[hbm, hbm],
        scratch_shapes=[
            pltpu.VMEM((steps, depth, yf // steps, nf), f32),
            pltpu.VMEM((yf // steps, depth, nf), f32),
            pltpu.VMEM((nc, nc), f32),
            pltpu.VMEM((yf // steps, nc, nf), f32),
            pltpu.VMEM((nc, (steps + 1) // 2 * 8, nf), f32),
            pltpu.VMEM((yf // steps, nf // 2, nf), f32),
            pltpu.VMEM((nf // 2, yf, nf), f32),
            pltpu.VMEM((kb, nf, nf), f32),
            pltpu.VMEM((rows, cols * width * zi, nf), f32),
            pltpu.VMEM((rows, cols, width // 2, 2 * zi, nf), f32),
            pltpu.VMEM((rows, cols, rounds, width // 2, tiles, 2 * zi, 128), f32),
            pltpu.SemaphoreType.DMA((steps,)),
            pltpu.SemaphoreType.DMA((rounds, steps, slabs)),
            pltpu.SemaphoreType.DMA((rounds, steps, slabs)),
            pltpu.SemaphoreType.DMA((rounds, rows, cols)),
            pltpu.SemaphoreType.DMA((rounds, devices)),
            pltpu.SemaphoreType.DMA((rounds,)),
            pltpu.SemaphoreType.DMA(((steps + 1) // 2, cols)),
            pltpu.SemaphoreType.DMA((yo // 8,)),
        ],
        compiler_params=pltpu.CompilerParams(
            collective_id=exchange.calls - 1,
            has_side_effects=True,
            vmem_limit_bytes=60 * 1024 * 1024,
        ),
        name=f"fine_{exchange.calls - 1}",
    )(*operands)

    cas = [fine_matrix[p::2, : nf // 2] for p in range(2)]
    cas = np.stack([split(np.concatenate([c[0::2], c[1::2]])) for c in cas])
    block = pl.BlockSpec((rows, 1, yo, nf), lambda i: (0, i, 0, 0))
    exchange.calls += 1
    damped, scale = pl.pallas_call(
        functools.partial(out_kernel, sizes, float(nf) ** 3),
        grid=(zi,),
        in_specs=[
            vmem,
            vmem,
            vmem,
            pl.BlockSpec(
                (yo // 8, rows, 1, 8, nf), lambda i: (0, 0, lax.rem(i, zi // 2), 0, 0)
            ),
            block,
        ],
        out_specs=[block, pl.BlockSpec((8, 128), lambda i: (0, 0))],
        out_shape=[
            jax.ShapeDtypeStruct((rows, zi, yo, nf), f32),
            jax.ShapeDtypeStruct((8, 128), f32),
        ],
        scratch_shapes=[
            pltpu.VMEM((rows, yo, nf), f32),
            pltpu.VMEM((nf, nf), f32),
            pltpu.VMEM((8, nf), f32),
            pltpu.VMEM((8, 128), f32),
            pltpu.VMEM((devices, 8, 128), f32),
            pltpu.SemaphoreType.DMA((devices,)),
            pltpu.SemaphoreType.DMA((devices,)),
        ],
        compiler_params=pltpu.CompilerParams(
            collective_id=exchange.calls - 1,
            has_side_effects=True,
            vmem_limit_bytes=60 * 1024 * 1024,
        ),
        name="damp",
    )(
        packed.reshape(-1, 128),
        cas,
        split(lift),
        taken.reshape(yo // 8, rows, zi // 2, 8, nf),
        potential.reshape(rows, zi, yo, nf),
    )
    return damped.reshape(zo, yo, nf) * scale[0, 0]


def coarse_kernel(sizes, volume, *refs):
    wave, trap, evolve, cas, deep, tall, twice, joint, lift, sq_y, sq_z = refs[:11]
    risen, scale = refs[11:13]
    column, given, taken, field, well, stack, sent, got, back, home = refs[13:23]
    folded, lifted, square, partial, partials, mate_sent, mate_got = refs[23:30]
    send_sem, recv_sem, own_sem, mate_send, mate_recv = refs[30:35]
    rows, cols = sizes["rows"], sizes["cols"]
    row, col = lax.axis_index("rows"), lax.axis_index("cols")
    devices, me = rows * cols, row * cols + col
    xb, yb, nc = wave.shape
    zb, nf = nc // devices, lift.shape[1]
    strips = risen.shape[1] // 8
    pairs = zb // 2

    barrier = pltpu.get_barrier_semaphore()

    def greet(step, carry):
        peer = lax.rem(me + step, devices)
        pl.semaphore_signal(
            barrier, inc=1, device_id=(peer // cols, lax.rem(peer, cols)), device_id_type=MESH
        )
        return carry

    lax.fori_loop(1, devices, greet, 0)

    def ends(turn, device, slot):
        if turn < 2:
            return given.at[turn, device], taken.at[turn, slot]
        at, to = pl.ds(pairs * device, pairs), pl.ds(pairs * slot, pairs)
        if turn == 2:
            return sent.at[at], got.at[to]
        if turn == 3:
            return back.at[at], home.at[to]
        return partial, partials.at[slot]

    def copy(turn, step):
        peer = lax.rem(me + step, devices)
        source, target = ends(turn, peer, me)
        return pltpu.make_async_remote_copy(
            src_ref=source,
            dst_ref=target,
            send_sem=send_sem.at[turn, step],
            recv_sem=recv_sem.at[turn, step],
            device_id=(peer // cols, lax.rem(peer, cols)),
            device_id_type=MESH,
        )

    middle = rows // 2
    base, local = row // middle * middle, lax.rem(row, middle)
    mate_row = lax.rem(row + middle, rows)

    def to_mate(z):
        return pltpu.make_async_remote_copy(
            src_ref=mate_sent.at[z],
            dst_ref=mate_got.at[z],
            send_sem=mate_send.at[z],
            recv_sem=mate_recv.at[z],
            device_id=(mate_row, col),
            device_id_type=MESH,
        )

    def place_of(r, c, t):
        return pl.ds(pl.multiple_of(8 * strip_of(r, c, t, rows, cols, strips), 8), 8)

    def spread_ends(turn, r, c):
        index = turn - 5
        if index < strips:
            source = lifted.at[0, :, place_of(r, c, index)]
            return source, risen.at[pl.ds(pairs * me, pairs), 8 * index : 8 * index + 8]
        z, t = (index - strips) // strips, (index - strips) % strips
        at = pairs * (mate_row * cols + col) + z
        return lifted.at[1, z, place_of(r, c, t)], risen.at[at, 8 * t : 8 * t + 8]

    def spread(turn, step):
        r = base + lax.rem(local + step // cols, middle)
        c = lax.rem(col + lax.rem(step, cols), cols)
        source, target = spread_ends(turn, r, c)
        return pltpu.make_async_remote_copy(
            src_ref=source,
            dst_ref=target,
            send_sem=send_sem.at[turn, step],
            recv_sem=recv_sem.at[turn, step],
            device_id=(r, c),
            device_id_type=MESH,
        )

    def spread_own(turn):
        source, target = spread_ends(turn, row, col)
        return pltpu.make_async_copy(source, target, own_sem.at[turn])

    def spread_out(turns):
        def start(index, carry):
            for turn in turns:
                spread(turn, far_first(index, middle * cols)).start()
            return carry

        lax.fori_loop(0, middle * cols - 1, start, 0)
        for turn in turns:
            spread_own(turn).start()

    def own(turn):
        source, target = ends(turn, me, me)
        return pltpu.make_async_copy(source, target, own_sem.at[turn])

    def launch(turn):
        def start(index, carry):
            copy(turn, far_first(index, devices)).start()
            return carry

        lax.fori_loop(0, devices - 1, start, 0)
        own(turn).start()

    def arrive(turn):
        def wait(step, carry):
            copy(turn, step).wait_recv()
            return carry

        lax.fori_loop(1, devices, wait, 0)
        own(turn).wait()

    def scatter(turn, source):
        for high in range(xb // 8):
            for low in range(8):
                block = source[8 * high + low]
                if turn == 0:
                    column[low] = product_with(pair_of(evolve), halves(block), ((1,), (1,)))
                else:
                    column[low] = block.T
            turned = jnp.transpose(column[...], (1, 0, 2)).reshape(devices, zb, 8, yb)
            for z in range(zb):
                at = (high * zb + z) * yb
                given[turn, :, :, at : at + yb] = turned[:, z]

    def gather(turn, target):
        def one(r, carry):
            for c in range(cols):
                for high in range(xb // 8):
                    place = pl.ds(pl.multiple_of(r * xb + 8 * high, 8), 8)
                    for z in range(zb):
                        at = (high * zb + z) * yb
                        target[z, place, yb * c : yb * (c + 1)] = taken[
                            turn, r * cols + c, :, at : at + yb
                        ]
            return carry

        lax.fori_loop(0, rows, one, 0)

    scatter(0, wave)
    stack[zb:] = jnp.zeros((8 - zb, nc, nc), jnp.float32)
    pl.semaphore_wait(barrier, devices - 1)
    launch(0)
    scatter(1, trap)
    launch(1)
    arrive(0)
    gather(0, field)

    def left(matrix, values):
        return product_with(pair_of(matrix), halves(values), ((1,), (0,)))

    def right(values, matrix):
        return product_with(halves(values), pair_of(matrix), ((1,), (0,)))

    def forward(z, carry):
        evolved = right(left(evolve, field[z]), evolve)
        field[z] = evolved
        stack[z] = right(left(cas, evolved * evolved), cas)
        return carry

    lax.fori_loop(0, zb, forward, 0)
    turned = jnp.transpose(stack[...], (1, 0, 2)).reshape(nc // 2, 2, 8, nc)
    for e in range(2):
        sent[:, :, e * nc : (e + 1) * nc] = turned[:, e]
    launch(2)
    arrive(1)
    gather(1, well)
    arrive(2)
    for t in range(pairs):
        block = got[...].reshape(devices, pairs, 8, nf)[:, t].reshape(devices * 8, nf)
        values = left(deep, block)
        sq_x = [squared_wave(me * zb + 2 * t + e, nc, 2.0) for e in range(2)]
        lanes = lax.broadcasted_iota(jnp.int32, (1, 2 * nc), 1)
        squares = (jnp.where(lanes < nc, sq_x[0], sq_x[1]) + sq_y[...]) + sq_z[...]
        nonzero = jnp.where(squares > 0, squares, 1.0)
        weights = jnp.where(
            squares > 0, DIPOLE_STRENGTH * (3.0 * sq_z[...] - squares) / nonzero, 0.0
        )
        values = right(left(tall, values * (weights / volume)), twice)
        values = values.reshape(devices, 8, nf)
        for d in range(devices):
            back[pairs * d + t] = values[d]
    launch(3)
    arrive(3)
    folded[...] = jnp.transpose(home[...], (1, 0, 2))
    sums = jnp.zeros((8, nc), jnp.float32)
    for z in range(zb):
        square[...] = left(joint, folded[z])
        field_dd = square[:nc, :nc] + square[nc:, nc:]
        evolved = field[z]
        exponent = well[z] + CONTACT * (evolved * evolved) + field_dd
        damped = jnp.exp(-TIME_STEP * exponent) * evolved
        sums += jnp.sum((damped * damped).reshape(nc // 8, 8, nc), axis=0)
        mate_sent[z // 2, :, z % 2 * nc : (z % 2 + 1) * nc] = damped
        if z % 2:
            to_mate(z // 2).start()
    partial[...] = jnp.full(partial.shape, jnp.sum(sums), jnp.float32)
    launch(4)

    def raise_pair(slot, z, planes):
        for e in range(2):
            half = halves(planes[z, :, e * nc : (e + 1) * nc])
            high = product_with(pair_of(lift), half, ((1,), (1,)))
            lifted[slot, z, :, e * nc : (e + 1) * nc] = high

    for z in range(pairs):
        raise_pair(0, z, mate_sent)
    spread_out(range(5, 5 + strips))
    for z in range(pairs):
        to_mate(z).wait_recv()
        raise_pair(1, z, mate_got)
        first = 5 + strips + z * strips
        spread_out(range(first, first + strips))
    arrive(4)
    scale[...] = lax.rsqrt(jnp.sum(partials[...], axis=0) / volume + EPSILON)
    last = 5 + strips * (1 + pairs)

    def landed(step, carry):
        for turn in range(5, last):
            spread(turn, step).wait()
        return carry

    lax.fori_loop(1, middle * cols, landed, 0)
    for turn in range(5, last):
        spread_own(turn).wait()
    for z in range(pairs):
        to_mate(z).wait_send()

    def settle(step, carry):
        for turn in range(5):
            copy(turn, step).wait_send()
        return carry

    lax.fori_loop(1, devices, settle, 0)


def coarse_step(exchange, wave, potential, evolve, lift):
    sizes = exchange.sizes
    rows, cols = sizes["rows"], sizes["cols"]
    devices = rows * cols
    xb, yb, nc = wave.shape
    nf = lift.shape[1]
    zb, yf, pairs = nc // devices, 2 * nf // devices, nc // devices // 2
    cas = cas_table(np.arange(nc), nc)
    deep = np.pad(cas.reshape(nc, devices, zb), ((0, 0), (0, 0), (0, 8 - zb))).reshape(nc, -1)
    twice = np.kron(np.eye(2), cas)
    joint = np.concatenate([cas[:, 0::2], cas[:, 1::2]])
    every = squared_waves(nc, 2.0).astype(np.float32)
    operands = [wave, potential, split(evolve), split(cas), split(deep), split(deep.T)]
    operands += [split(twice), split(joint), split(lift.T)]
    operands += [np.tile(every, 2)[None, :], every[:, None]]
    exchange.calls += 1
    vmem, hbm = pl.BlockSpec(memory_space=pltpu.VMEM), pl.BlockSpec(memory_space=pl.ANY)
    f32 = jnp.float32
    lanes = zb * xb // 8 * yb
    half = (nc // 2, 8, 2 * nc)
    turns = 5 + yf // 8 * (1 + pairs)
    return pl.pallas_call(
        functools.partial(coarse_kernel, sizes, float(nc) ** 3),
        out_shape=[
            jax.ShapeDtypeStruct((nc // 2, yf, 2 * nc), f32),
            jax.ShapeDtypeStruct((8, 128), f32),
        ],
        in_specs=[vmem] * len(operands),
        out_specs=[hbm, vmem],
        scratch_shapes=[
            pltpu.VMEM((8, nc, yb), f32),
            pltpu.VMEM((2, devices, 8, lanes), f32),
            pltpu.VMEM((2, devices, 8, lanes), f32),
            pltpu.VMEM((zb, nc, nc), f32),
            pltpu.VMEM((zb, nc, nc), f32),
            pltpu.VMEM((8, nc, nc), f32),
            pltpu.VMEM(half, f32),
            pltpu.VMEM(half, f32),
            pltpu.VMEM(half, f32),
            pltpu.VMEM(half, f32),
            pltpu.VMEM((8, nc // 2, 2 * nc), f32),
            pltpu.VMEM((2, pairs, nf, 2 * nc), f32),
            pltpu.VMEM((2 * nc, 2 * nc), f32),
            pltpu.VMEM((8, 128), f32),
            pltpu.VMEM((devices, 8, 128), f32),
            pltpu.VMEM((pairs, nc, 2 * nc), f32),
            pltpu.VMEM((pairs, nc, 2 * nc), f32),
            pltpu.SemaphoreType.DMA((turns, devices)),
            pltpu.SemaphoreType.DMA((turns, devices)),
            pltpu.SemaphoreType.DMA((turns,)),
            pltpu.SemaphoreType.DMA((pairs,)),
            pltpu.SemaphoreType.DMA((pairs,)),
        ],
        compiler_params=pltpu.CompilerParams(
            collective_id=exchange.calls - 1,
            has_side_effects=True,
            vmem_limit_bytes=60 * 1024 * 1024,
        ),
        name=f"coarse_{exchange.calls - 1}",
    )(*operands)


def per_device(sizes, wave_coarse, potential_coarse, potential_fine):
    devices = sizes["rows"] * sizes["cols"]
    nc, nf = wave_coarse.shape[2], potential_fine.shape[2]
    exchange = Exchanger(sizes)

    positions = np.arange(nc)
    coarse_matrix = cas_table(positions, nc)
    decay = np.exp(-0.5 * TIME_STEP * squared_waves(nc, 2.0))[:, None] / nc
    evolve = coarse_matrix @ (decay * coarse_matrix)
    padded = np.where(positions < nc // 2, positions, positions + nc)
    lift = coarse_matrix @ (decay * cas_table(padded, 2 * nc))

    slab, scale = coarse_step(exchange, wave_coarse, potential_coarse, evolve, lift)
    return fine_step(exchange, slab, scale, lift, potential_fine)


def fits_slabs(sizes, nc, nf):
    rows, cols = sizes["rows"], sizes["cols"]
    devices = rows * cols
    if rows % 2 or cols % 2 or nc % devices or nf % (8 * devices // 2) or nf % (4 * devices):
        return False
    if nc // rows % 8 or nc // devices > 8 or nc // devices % 2:
        return False
    return nf % (8 * rows) == 0 and nf % 128 == 0 and nf // devices % 8 == 4 and 2 * nc == nf


def solution(mesh):
    sizes = {"rows": mesh.shape["rows"], "cols": mesh.shape["cols"]}
    placed = (P("rows", "cols", None), P("rows", "cols", None), P("cols", "rows", None))

    def run(wave_coarse, potential_coarse, potential_fine):
        nc, nf = wave_coarse.shape[0], potential_fine.shape[0]
        body = per_device if fits_slabs(sizes, nc, nf) else per_device_pencils
        return jax.shard_map(
            functools.partial(body, sizes),
            mesh=mesh,
            in_specs=placed,
            out_specs=P("cols", "rows", None),
            check_vma=False,
        )(wave_coarse, potential_coarse, potential_fine)

    return run
```
